256 devices in a mesh: slab: 8 (over z_lo, core), brick: 32 (over x, y, z_hi).
Axes of the slice: x: 4, y: 4, z: 8 (z_hi: 2, z_lo: 4; z = z_hi * 4 + z_lo), core: 2. Of those that a mesh axis runs over, the one named last changes fastest.
Arguments:
- features: float32 [64, 65536], P(None, ('slab', 'brick')), may hold values from -6 to 6
- cotangent: float32 [64, 65536], P(None, ('slab', 'brick')), may hold values from -6 to 6
- positions: float32 [3, 65536], P(None, ('slab', 'brick')), may hold values from 0 to 1, as said below
- edge_length: float32 [32, 65536], P(None, ('slab', 'brick')), may hold values from 1 to 6
- neighbors: int32 [32, 65536], P(None, ('slab', 'brick')), may hold values from 0 to 383
- send_map: int32 [4, 4096], P(None, ('slab', 'brick')), may hold values from 0 to 127
- atom_count: int32 [256], P(('slab', 'brick')), may hold values from 128 to 256, as said below
- short_weight: float32 [64, 64], replicated, may hold values from -0.75 to 0.75
- charge_weight: float32 [64, 64], replicated, may hold values from -0.75 to 0.75
- radial_weight: float32 [64, 8], replicated, may hold values from -2 to 2
Outputs:
- feature_grad: float32 [64, 65536], P(None, ('slab', 'brick'))
- short_grad: float32 [64, 64], replicated
- charge_grad: float32 [64, 64], replicated
- radial_grad: float32 [64, 8], replicated
The draws below stay inside these ranges and needn't reach their ends.
Inputs may be any that keep to these rules, and one draw needn't show every extreme that they name: `neighbors`: Entries may repeat. `send_map`: row 2p + q, columns d * 16 to (d + 1) * 16 - 1 list the atoms of brick d in its boundary group (p, q), as indices within the brick; they may repeat. `atom_count`: some brick has exactly 256 live atoms and some exactly 128. `positions`: an atom of brick d = s * 32 + b has its first coordinate in [b / 32, (b + 1) / 32] and its third in [s / 8, (s + 1) / 8].
All inputs are finite; a program needn't handle non-finite values.
Results may differ from the reference program's by a relative error of at most 0.0003.
Values sent between devices are 32-bit elements; how exact they have to be, the bound alone decides.
No kernel may reach another device: no remote copies, remote signals or barrier semaphores. Data moves between devices by JAX's collectives and lax.ppermute only.
A program may use at most 64 MiB of HBM per device.

```python
import math
import jax
import jax.numpy as jnp
from jax import lax

CH = 64
KX = 8
KY = 16
KZ = 8
NB = 8
NEIGH = 32
ATOM_DEV = 256
GQ = 16
SLABS = 8
BRICKS = 32
BRICKS_ALL = 256
ATOMS = 65536
N_SLAB = 8
N_BRICK = 32


def draw_positions(key, part):
    shares = jax.random.uniform(key, (3, ATOMS), dtype=jnp.float32)
    owner = jnp.arange(ATOMS, dtype=jnp.int32) // ATOM_DEV
    slab_of = (owner // BRICKS).astype(jnp.float32)
    brick_of = (owner % BRICKS).astype(jnp.float32)
    first_coord = (brick_of + shares[0]) / BRICKS
    third_coord = (slab_of + shares[2]) / SLABS
    return jnp.stack([first_coord, shares[1], third_coord]).astype(jnp.float32)


def draw_atom_count(key, part):
    counts = jax.random.randint(key, (BRICKS_ALL,), ATOM_DEV // 2, ATOM_DEV + 1)
    order = jax.random.permutation(jax.random.fold_in(key, 7), BRICKS_ALL)
    counts = counts.at[order[0]].set(ATOM_DEV)
    return counts.at[order[1]].set(ATOM_DEV // 2).astype(jnp.int32)


def place_ends(drawn, rng, least, high):
    extent = drawn.shape
    index_at = [jax.random.randint(jax.random.fold_in(rng, axis), (), 0, extent[axis]) for axis in range(len(extent))]
    drawn = drawn.at[tuple(index_at)].set(least)
    longest = extent.index(max(extent))
    index_at[longest] = (index_at[longest] + 1) % extent[longest]
    return drawn.at[tuple(index_at)].set(high)


def shard_levels(key, dims, pieces, smallest, high):
    loudness = 1.0
    for dim, shards_of in pieces:
        steps = jax.random.uniform(jax.random.fold_in(jax.random.fold_in(key, 6), dim), (shards_of,), jnp.float32, smallest / len(pieces), high / len(pieces))
        loudness = loudness * jnp.repeat(jnp.exp(steps), dims[dim] // shards_of).reshape((-1,) + (1,) * (len(dims) - 1 - dim))
    return loudness


def normal_values(own_key, shape, width, limit, pieces=(), kind=jnp.bfloat16):
    entries = jax.random.normal(own_key, shape, jnp.float32) * width
    if len(pieces) > 0:
        entries = shard_levels(own_key, shape, pieces, -0.22, 0.18) * entries
    return jnp.clip(entries, min=-limit, max=limit).astype(kind)


def setup_inputs(seed: int = 0) -> dict:
    arg_keys = jax.random.split(jax.random.key(seed), 11)
    return {
        "features": normal_values(arg_keys[0], (CH, ATOMS), 1.0, 6.0, ((1, 256),), jnp.float32),
        "cotangent": normal_values(arg_keys[1], (CH, ATOMS), 1.0, 6.0, ((1, 256),), jnp.float32),
        "positions": draw_positions(jax.random.fold_in(arg_keys[10], 71), 0),
        "edge_length": jnp.clip(1.0 + 5.0 * jax.random.uniform(arg_keys[3], (NEIGH, ATOMS), jnp.float32) ** shard_levels(arg_keys[3], (NEIGH, ATOMS), ((1, 256),), -0.2, 0.2), 1.0, 6.0),
        "neighbors": place_ends(jax.random.randint(arg_keys[4], (NEIGH, ATOMS), 0, ATOM_DEV + 8 * GQ), jax.random.fold_in(arg_keys[4], 1), 0, (ATOM_DEV + 8 * GQ) - 1).astype(jnp.int32),
        "send_map": place_ends(jax.random.randint(arg_keys[5], (4, GQ * BRICKS_ALL), 0, ATOM_DEV // 2), jax.random.fold_in(arg_keys[5], 1), 0, (ATOM_DEV // 2) - 1).astype(jnp.int32),
        "atom_count": draw_atom_count(jax.random.fold_in(arg_keys[10], 71), 0),
        "short_weight": normal_values(arg_keys[7], (CH, CH), CH ** -0.5, 0.75, (), jnp.float32),
        "charge_weight": normal_values(arg_keys[8], (CH, CH), CH ** -0.5, 0.75, (), jnp.float32),
        "radial_weight": normal_values(arg_keys[9], (CH, NB), NB ** -0.5, 2.0, (), jnp.float32),
    }


CUTOFF = 6.0
TWO_PI = 2.0 * math.pi
FULL_PRECISION = lax.Precision.HIGHEST

def radial_terms(lengths, count):
    orders = jnp.arange(1, count + 1, dtype=jnp.int32).astype(jnp.float32)
    scaled_r = lengths / CUTOFF
    envelope = (1.0 - scaled_r * scaled_r) ** 2
    wave_terms = jnp.sin(orders[:, None, None] * (jnp.pi * scaled_r)[None])
    return math.sqrt(2.0 / CUTOFF) * wave_terms * (envelope / lengths)[None]

def mode_tables():
    counter = jnp.arange(KX * KY * KZ, dtype=jnp.int32)
    mode_one = (counter // (KY * KZ) - KX // 2).astype(jnp.float32)
    mode_two = (counter // KZ % KY - KY // 2).astype(jnp.float32)
    mode_three = (counter % KZ - KZ // 2).astype(jnp.float32)
    squared = mode_one * mode_one + mode_two * mode_two + mode_three * mode_three
    filter_values = jnp.where(squared > 0.0, jnp.exp(-squared / 16.0) / jnp.maximum(squared, 1.0), 0.0)
    return (mode_one, mode_two, mode_three, filter_values)

def phase_parts(modes, fraction):
    angle_values = TWO_PI * (modes[0][:, None] * fraction[0][None, :] + modes[1][:, None] * fraction[1][None, :] + modes[2][:, None] * fraction[2][None, :])
    return (jnp.cos(angle_values), jnp.sin(angle_values))

def contract_last(left, right):
    return lax.dot_general(left, right, (((1,), (1,)), ((), ())), precision=FULL_PRECISION)

def contract_first(left, right):
    return lax.dot_general(left, right, (((0,), (0,)), ((), ())), precision=FULL_PRECISION)

def edge_terms(projected, lengths, targets, keep_mask, tangent, radial_weight, own_count, live_count):
    radial_values = radial_terms(lengths, radial_weight.shape[1])
    filter_edge = jnp.einsum('cm,meb->ceb', radial_weight, radial_values, precision=FULL_PRECISION)
    reach_mask = jnp.logical_or(targets >= own_count, targets < live_count).astype(jnp.float32) * keep_mask[None, :]
    weight = filter_edge * reach_mask[None]
    gathered = projected[:, targets]
    short_sum = lax.optimization_barrier(jnp.sum(weight * gathered, axis=1))
    sigmoid_v = jax.nn.sigmoid(short_sum)
    upstream = tangent * sigmoid_v * (1.0 + short_sum * (1.0 - sigmoid_v)) * keep_mask[None, :]
    spread = weight * upstream[:, None, :]
    radial_part = jnp.einsum('ceb,meb->cm', upstream[:, None, :] * gathered * reach_mask[None], radial_values, precision=FULL_PRECISION)
    return (spread, radial_part)

def reference(features, cotangent, positions, edge_length, neighbors, send_map, atom_count, short_weight, charge_weight, radial_weight):
    devices = N_SLAB * N_BRICK
    channels = features.shape[0]
    grad_scale = 1.0 / math.sqrt(ATOM_DEV * devices)

    def by_device(array):
        return array.reshape(array.shape[0], devices, ATOM_DEV).transpose(1, 0, 2)
    feat_dev = by_device(features)
    tangent_dev = by_device(cotangent)
    place_dev = by_device(positions)
    length_dev = by_device(edge_length)
    target_dev = by_device(neighbors)
    map_dev = send_map.reshape(4, devices, GQ).transpose(1, 0, 2)
    live_dev = (jnp.arange(ATOM_DEV, dtype=jnp.int32)[None, :] < atom_count[:, None]).astype(jnp.float32)
    device_ids = jnp.arange(devices, dtype=jnp.int32)
    slab_of = device_ids // N_BRICK
    brick_of = device_ids % N_BRICK
    slab_prev = (slab_of - 1) % N_SLAB * N_BRICK + brick_of
    slab_next = (slab_of + 1) % N_SLAB * N_BRICK + brick_of
    brick_prev = slab_of * N_BRICK + (brick_of - 1) % N_BRICK
    brick_next = slab_of * N_BRICK + (brick_of + 1) % N_BRICK
    sends = jax.vmap(lambda feature_block, pick_list: feature_block[:, pick_list])(feat_dev, map_dev)
    ghosts = jnp.concatenate([sends[slab_prev][:, :, 2:4], sends[slab_next][:, :, 0:2], sends[brick_prev][:, :, 1::2], sends[brick_next][:, :, 0::2]], axis=2)
    extended = jnp.concatenate([feat_dev, ghosts.reshape(devices, channels, 8 * GQ)], axis=2)

    def edge_device(device):
        projected = jnp.dot(short_weight, extended[device], precision=FULL_PRECISION)
        spread, radial_part = edge_terms(projected, length_dev[device], target_dev[device], live_dev[device], tangent_dev[device], radial_weight, ATOM_DEV, atom_count[device])
        grads_ext = jnp.zeros((channels, ATOM_DEV + 8 * GQ), jnp.float32).at[:, target_dev[device].reshape(-1)].add(spread.reshape(channels, -1))
        return (grads_ext, radial_part)
    grads_ext, radial_parts = lax.map(edge_device, device_ids)
    ghost_grads = grads_ext[:, :, ATOM_DEV:].reshape(devices, channels, 8, GQ)
    returned = jnp.stack([ghost_grads[slab_prev][:, :, 2] + ghost_grads[brick_prev][:, :, 6], ghost_grads[slab_prev][:, :, 3] + ghost_grads[brick_next][:, :, 4], ghost_grads[slab_next][:, :, 0] + ghost_grads[brick_prev][:, :, 7], ghost_grads[slab_next][:, :, 1] + ghost_grads[brick_next][:, :, 5]], axis=2)
    owned_grad = jax.vmap(lambda own_part, pick_list, back_part: own_part.at[:, pick_list].add(back_part))(grads_ext[:, :, :ATOM_DEV], map_dev.reshape(devices, 4 * GQ), returned.reshape(devices, channels, 4 * GQ))
    modes = mode_tables()

    def wave_device(running, device):
        cos_part, sin_part = phase_parts(modes, place_dev[device])
        gated = tangent_dev[device] * live_dev[device][None, :]
        return ((running[0] + contract_last(cos_part, gated), running[1] + contract_last(sin_part, gated)), None)
    zero_waves = jnp.zeros((KX * KY * KZ, channels), jnp.float32)
    (wave_real, wave_imag), _ = lax.scan(wave_device, (zero_waves, zero_waves), device_ids)
    weighted_real = wave_real * (modes[3] * grad_scale)[:, None]
    weighted_imag = wave_imag * (modes[3] * grad_scale)[:, None]

    def charge_device(device):
        cos_part, sin_part = phase_parts(modes, place_dev[device])
        return (contract_first(weighted_real, cos_part) + contract_first(weighted_imag, sin_part)) * live_dev[device][None, :]
    charge_field = lax.map(charge_device, device_ids)
    grad_dev = jnp.einsum('cb,dca->dba', short_weight, owned_grad, precision=FULL_PRECISION) + jnp.einsum('cb,dca->dba', charge_weight, charge_field, precision=FULL_PRECISION)
    feature_grad = grad_dev.transpose(1, 0, 2).reshape(channels, devices * ATOM_DEV)
    short_grad = grad_scale * jnp.einsum('dca,dba->cb', owned_grad, feat_dev, precision=FULL_PRECISION)
    charge_grad = grad_scale * jnp.einsum('dca,dba->cb', charge_field, feat_dev, precision=FULL_PRECISION)
    radial_grad = grad_scale * lax.optimization_barrier(jnp.sum(radial_parts, axis=0))
    return (feature_grad, short_grad, charge_grad, radial_grad)
```

```python
import math

import jax
import jax.numpy as jnp
import numpy as np
from jax import lax
from jax.experimental import pallas as pl
from jax.experimental.pallas import tpu as pltpu
from jax.sharding import PartitionSpec as P

KX = 8
KY = 16
KZ = 8
CUTOFF = 6.0
HALF_ROWS = 64
CHUNKS = 11
F32 = jnp.float32
BF16 = jnp.bfloat16
FULL_PRECISION = lax.Precision.HIGHEST
BOTH = ("slab", "brick")


def slot_modes(chunk, i, j):
    if chunk < 8:
        return (chunk - 4, j - 8, i - 4)
    if chunk == 8:
        return (4, j - 8, i - 3)
    if chunk == 9:
        return (i - 3, j - 8, 4)
    return (i - 4, 0, j - 4)


def weight_table(scale):
    where = {}
    for chunk in range(CHUNKS):
        for i in range(8):
            for j in range(8):
                where.setdefault(slot_modes(chunk, i, j), (chunk, i * 8 + j))
    table = np.zeros((CHUNKS, HALF_ROWS), np.float64)
    for k in range(KX * KY * KZ):
        n = (k // (KY * KZ) - KX // 2, k // KZ % KY - KY // 2, k % KZ - KZ // 2)
        squared = float(n[0] ** 2 + n[1] ** 2 + n[2] ** 2)
        if squared == 0.0:
            continue
        slot = where.get(n)
        if slot is None or n[1] > 0:
            slot = where[(-n[0], -n[1], -n[2])]
        table[slot] += math.exp(-squared / 16.0) / squared
    wide = np.ones((CHUNKS * HALF_ROWS, 128), np.float32)
    wide[:, :64] = (table.reshape(-1, 1) * scale).astype(np.float32)
    return wide


def split(value):
    high = value.astype(BF16)
    return high, (value - high.astype(F32)).astype(BF16)


def dot(left, right, contract=((1,), (0,))):
    return lax.dot_general(left, right, (contract, ((), ())), preferred_element_type=F32)


def dot_full(left, right, contract=((1,), (0,))):
    return lax.dot_general(
        left, right, (contract, ((), ())), precision=FULL_PRECISION, preferred_element_type=F32
    )


def sin_turns(turns):
    turns = turns - jnp.floor(turns + 0.5)
    folded = jnp.where(turns > 0.25, 0.5 - turns, jnp.where(turns < -0.25, -0.5 - turns, turns))
    angle = folded * (2.0 * math.pi)
    square = angle * angle
    poly = -1.0 / 39916800.0
    for divisor in (362880.0, -5040.0, 120.0, -6.0):
        poly = poly * square + 1.0 / divisor
    return angle + angle * square * poly


def wave_factors(turns, first):
    order = lax.broadcasted_iota(jnp.int32, (8, turns.shape[1]), 0) + first
    phase = order.astype(F32) * turns
    phase = phase - jnp.floor(phase + 0.5)
    return sin_turns(phase + 0.25), sin_turns(phase)


def complex_product(left, right):
    return (
        left[0] * right[0] - left[1] * right[1],
        left[0] * right[1] + left[1] * right[0],
    )


def chunk_waves(positions):
    one = wave_factors(positions[0:1], -4)
    one_up = wave_factors(positions[0:1], -3)
    two = wave_factors(positions[1:2], -8)
    three = wave_factors(positions[2:3], -4)
    three_up = wave_factors(positions[2:3], -3)

    def row(pair, index):
        return pair[0][index : index + 1], pair[1][index : index + 1]

    def chunk(number):
        if number < 8:
            outer, inner = complex_product(row(one, number), three), two
        elif number == 8:
            outer, inner = complex_product(row(one_up, 7), three_up), two
        elif number == 9:
            outer, inner = complex_product(row(three_up, 7), one_up), two
        else:
            outer, inner = one, three
        cos_part, sin_part = complex_product(
            (outer[0][:, None, :], outer[1][:, None, :]),
            (inner[0][None, :, :], inner[1][None, :, :]),
        )
        atoms = positions.shape[1]
        return jnp.concatenate(
            [cos_part.reshape(HALF_ROWS, atoms), sin_part.reshape(HALF_ROWS, atoms)], axis=0
        )

    return chunk


def live_row(count_ref, atoms):
    index = lax.broadcasted_iota(jnp.int32, (1, atoms), 1)
    return (index < count_ref[0]).astype(F32)


def send_selector(send_map, atoms, transposed=False):
    size = send_map.shape[1]
    spread = (
        lax.broadcasted_iota(jnp.int32, (size, 128), 1) % size
        == lax.broadcasted_iota(jnp.int32, (size, 128), 0)
    ).astype(F32)
    tiled = dot_full(send_map.astype(F32), spread)
    place = lax.broadcasted_iota(jnp.int32, (1, 128), 1) // size
    wanted = jnp.zeros((1, 128), F32)
    for slot, group in enumerate((2, 3, 0, 1, 1, 3, 0, 2)):
        wanted = jnp.where(place == slot, tiled[group : group + 1], wanted)
    atom = lax.broadcasted_iota(jnp.int32, (atoms, 128), 0).astype(F32)
    return (atom == jnp.round(wanted)).astype(F32).astype(BF16)


def pick_lanes(refs):
    place = lax.broadcasted_iota(jnp.int32, (64, 128), 1) // 32
    value = refs[3][...]
    for slot in range(3):
        value = jnp.where(place == slot, refs[slot][...], value)
    return value


def send_kernel(features_ref, map_ref, out_ref):
    features = features_ref[...]
    selector = send_selector(map_ref[...], features.shape[1])
    high, rest = split(features)
    middle, low = split(features - high.astype(F32))
    out_ref[...] = dot(high, selector) + (dot(middle, selector) + dot(low, selector))


def wave_kernel(count_ref, positions_ref, cotangent_ref, features_ref, table_ref, out_ref):
    chunk = chunk_waves(positions_ref[...])
    live = live_row(count_ref, positions_ref.shape[1])
    both = jnp.concatenate([cotangent_ref[...] * live, features_ref[...] * live], axis=0)
    high, low = split(both)
    stacked = jnp.concatenate([high, low], axis=0)
    for number in range(CHUNKS):
        wave_high, wave_low = split(chunk(number))
        part = dot(wave_high, stacked, ((1,), (1,)))
        part = part[:, :128] + part[:, 128:] + dot(wave_low, high, ((1,), (1,)))
        weight = table_ref[number * HALF_ROWS : (number + 1) * HALF_ROWS, :]
        base = number * 2 * HALF_ROWS
        out_ref[base : base + HALF_ROWS, :] = part[:HALF_ROWS] * weight
        out_ref[base + HALF_ROWS : base + 2 * HALF_ROWS, :] = part[HALF_ROWS:] * weight
    done = CHUNKS * 2 * HALF_ROWS
    out_ref[done:, :] = jnp.zeros((out_ref.shape[0] - done, 128), F32)


def edge_kernel(
    count_ref,
    features_ref,
    up_ref,
    down_ref,
    right_ref,
    left_ref,
    cotangent_ref,
    length_ref,
    neighbor_ref,
    short_ref,
    radial_ref,
    own_ref,
    ghost_ref,
    small_ref,
    basis_ref,
    selector_ref,
    gathered_ref,
    weight_ref,
):
    channels, atoms = features_ref.shape
    slots = length_ref.shape[0]
    columns = atoms + 128
    scale = small_ref.shape[0]
    extended = jnp.concatenate(
        [features_ref[...], pick_lanes((up_ref, down_ref, right_ref, left_ref))], axis=1
    )
    projected = jnp.concatenate(split(dot_full(short_ref[...], extended)), axis=0)
    live = live_row(count_ref, atoms)

    lengths = length_ref[...]
    targets = neighbor_ref[...]
    reach = jnp.where(jnp.logical_or(targets >= atoms, targets < count_ref[0]), live, 0.0)
    ratio = lengths * (1.0 / CUTOFF)
    envelope = 1.0 - ratio * ratio
    envelope = math.sqrt(2.0 / CUTOFF) * envelope * envelope / lengths * reach
    order = lax.broadcasted_iota(jnp.int32, (slots, 8, atoms), 1).astype(F32) + 1.0
    basis = sin_turns(order * (0.5 * ratio)[:, None, :]) * envelope[:, None, :]
    basis_ref[...] = basis.reshape(slots * 8, atoms)

    radial_high, radial_low = split(radial_ref[...])
    radial_wide = jnp.concatenate([radial_high, radial_high, radial_low], axis=1)
    column = lax.broadcasted_iota(jnp.int32, (columns, atoms), 0)

    def basis_of(slot):
        return split(basis_ref[pl.ds(pl.multiple_of(slot * 8, 8), 8), :])

    def forward(slot, total):
        selector = (column == neighbor_ref[pl.ds(slot, 1), :]).astype(F32).astype(BF16)
        selector_ref[slot] = selector
        found = dot(projected, selector)
        gathered = found[:channels] + found[channels:]
        basis_high, basis_low = basis_of(slot)
        weight = dot(radial_wide, jnp.concatenate([basis_high, basis_low, basis_high], axis=0))
        gathered_ref[slot] = gathered
        weight_ref[slot] = weight
        return total + weight * gathered

    short_sum = lax.fori_loop(0, slots, forward, jnp.zeros((channels, atoms), F32), unroll=2)
    gate = jax.nn.sigmoid(short_sum)
    upstream = cotangent_ref[...] * gate * (1.0 + short_sum * (1.0 - gate)) * live

    def backward(slot, running):
        grads, radial = running
        spread = jnp.concatenate(split(weight_ref[slot] * upstream), axis=0)
        grads = grads + dot(spread, selector_ref[slot], ((1,), (1,)))
        pulled = jnp.concatenate(split(gathered_ref[slot] * upstream), axis=0)
        pair = jnp.concatenate(basis_of(slot), axis=0)
        return grads, radial + dot(pulled, pair, ((1,), (1,)))

    grads, radial = lax.fori_loop(
        0,
        slots,
        backward,
        (jnp.zeros((2 * channels, columns), F32), jnp.zeros((2 * channels, 16), F32)),
        unroll=2,
    )
    grads = grads[:channels] + grads[channels:]
    radial = radial[:channels] + radial[channels:]
    radial = radial[:, :8] + radial[:, 8:]
    own_ref[...] = grads[:, :atoms]
    ghost_ref[...] = grads[:, atoms:]
    factor = 1.0 / math.sqrt(atoms * scale)
    short_part = dot_full(grads, extended, ((1,), (1,))) * factor
    rows = small_ref.shape[0] // channels
    small_ref[...] = jnp.zeros(small_ref.shape, F32)
    packed = jnp.concatenate(
        [short_part, radial * factor, jnp.zeros((channels, 128 - channels - 8), F32)], axis=1
    )
    small_ref[pl.ds(0, channels, stride=rows), :] = packed


def return_kernel(up_ref, down_ref, right_ref, left_ref, own_ref, map_ref, short_ref, out_ref):
    back = pick_lanes((up_ref, down_ref, right_ref, left_ref))
    selector = send_selector(map_ref[...], own_ref.shape[1])
    high, low = split(back)
    owned = own_ref[...] + (
        dot(high, selector, ((1,), (1,))) + dot(low, selector, ((1,), (1,)))
    )
    out_ref[...] = dot_full(short_ref[...], owned, ((0,), (0,)))


def charge_kernel(
    count_ref, positions_ref, waves_ref, partial_ref, charge_ref, grad_ref, out_ref, *, factor
):
    chunk = chunk_waves(positions_ref[...])
    channels, atoms = partial_ref.shape
    field = jnp.zeros((2 * channels, atoms), F32)
    grad = jnp.zeros((2 * channels, 128), F32)
    for number in range(CHUNKS):
        base = number * 2 * HALF_ROWS
        block = waves_ref[base : base + 2 * HALF_ROWS, :]
        turned = block.T[:channels]
        turned_high, turned_low = split(turned)
        turned = jnp.concatenate([turned_high, turned_low], axis=0)
        block_high, block_low = split(block)
        wave_high, wave_low = split(chunk(number))
        field = field + dot(turned, wave_high)
        grad = grad + dot(turned, block_high)
        extra = dot(turned_high, jnp.concatenate([wave_low, block_low], axis=1))
        field = field + jnp.concatenate([extra[:, :atoms], jnp.zeros((channels, atoms), F32)], axis=0)
        grad = grad + jnp.concatenate([extra[:, atoms:], jnp.zeros((channels, 128), F32)], axis=0)
    field = (field[:channels] + field[channels:]) * live_row(count_ref, atoms)
    grad = grad[:channels] + grad[channels:]
    grad_ref[...] = grad[:, channels : 2 * channels] * factor
    out_ref[...] = partial_ref[...] + dot_full(charge_ref[...], field, ((0,), (0,)))


def vmem(count):
    return [pl.BlockSpec(memory_space=pltpu.VMEM)] * count


def scalar_first(count):
    return [pl.BlockSpec(memory_space=pltpu.SMEM)] + vmem(count)


def shape(*dims):
    return jax.ShapeDtypeStruct(dims, F32)


def shifted(value, axis, step):
    size = lax.axis_size(axis)
    return lax.ppermute(value, axis, [(i, (i + step) % size) for i in range(size)])


def exchange(value):
    return lax.all_to_all(value, BOTH, 0, 0, tiled=True)


def on_device(
    features,
    cotangent,
    positions,
    edge_length,
    neighbors,
    send_map,
    atom_count,
    short_weight,
    charge_weight,
    radial_weight,
):
    channels, atoms = features.shape
    slots = neighbors.shape[0]
    devices = lax.axis_size("slab") * lax.axis_size("brick")
    factor = 1.0 / math.sqrt(atoms * devices)
    wave_rows = -(-CHUNKS * 2 * HALF_ROWS // devices)
    total_rows = wave_rows * devices

    outgoing = pl.pallas_call(
        send_kernel, out_shape=shape(channels, 128), in_specs=vmem(2), out_specs=vmem(1)[0]
    )(features, send_map)
    arrived = (
        shifted(outgoing, "slab", 1),
        shifted(outgoing, "slab", -1),
        shifted(outgoing, "brick", 1),
        shifted(outgoing, "brick", -1),
    )
    waves = pl.pallas_call(
        wave_kernel,
        out_shape=shape(total_rows, 128),
        in_specs=scalar_first(4),
        out_specs=vmem(1)[0],
    )(atom_count, positions, cotangent, features, jnp.asarray(weight_table(factor)))
    pieces = exchange(waves.reshape(devices, wave_rows, 128))
    mine = jnp.sum(pieces, axis=0)
    everyone = exchange(jnp.broadcast_to(mine[None], (devices, wave_rows, 128)))

    own, ghost, small = pl.pallas_call(
        edge_kernel,
        out_shape=(shape(channels, atoms), shape(channels, 128), shape(devices, 128)),
        in_specs=scalar_first(10),
        out_specs=tuple(vmem(3)),
        scratch_shapes=[
            pltpu.VMEM((slots * 8, atoms), F32),
            pltpu.VMEM((slots, atoms + 128, atoms), BF16),
            pltpu.VMEM((slots, channels, atoms), F32),
            pltpu.VMEM((slots, channels, atoms), F32),
        ],
    )(
        atom_count,
        features,
        *arrived,
        cotangent,
        edge_length,
        neighbors,
        short_weight,
        radial_weight,
    )
    small_sum = jnp.sum(exchange(small[:, None, :]), axis=0)
    small_all = exchange(jnp.broadcast_to(small_sum[None], (devices, 1, 128)))
    back = (
        shifted(ghost, "slab", -1),
        shifted(ghost, "slab", 1),
        shifted(ghost, "brick", -1),
        shifted(ghost, "brick", 1),
    )
    partial = pl.pallas_call(
        return_kernel, out_shape=shape(channels, atoms), in_specs=vmem(7), out_specs=vmem(1)[0]
    )(*back, own, send_map, short_weight)
    charge_grad, feature_grad = pl.pallas_call(
        lambda *refs: charge_kernel(*refs, factor=factor),
        out_shape=(shape(channels, channels), shape(channels, atoms)),
        in_specs=scalar_first(4),
        out_specs=tuple(vmem(2)),
    )(atom_count, positions, everyone.reshape(total_rows, 128), partial, charge_weight)
    small_rows = small_all.reshape(channels, devices // channels, 128)[:, 0]
    return (
        feature_grad,
        small_rows[:, :channels],
        charge_grad,
        small_rows[:, channels : channels + radial_weight.shape[1]],
    )


def solution(mesh):
    split_all = P(None, BOTH)
    placed = (split_all,) * 6 + (P(BOTH), P(), P(), P())
    return jax.shard_map(
        on_device,
        mesh=mesh,
        in_specs=placed,
        out_specs=(split_all, P(), P(), P()),
        check_vma=False,
    )
```

```python
import math

import jax
import jax.numpy as jnp
import numpy as np
from jax import lax
from jax.experimental import pallas as pl
from jax.experimental.pallas import tpu as pltpu
from jax.sharding import Mesh
from jax.sharding import PartitionSpec as P

KX = 8
KY = 16
KZ = 8
CUTOFF = 6.0
HALF_ROWS = 64
CHUNKS = 11
F32 = jnp.float32
BF16 = jnp.bfloat16
FULL_PRECISION = lax.Precision.HIGHEST
SLAB = ("chip", "core")
CHIPS = ("chip", "brick")
ALL = ("chip", "core", "brick")


def slot_modes(chunk, i, j):
    if chunk < 8:
        return (chunk - 4, j - 8, i - 4)
    if chunk == 8:
        return (4, j - 8, i - 3)
    if chunk == 9:
        return (i - 3, j - 8, 4)
    return (i - 4, 0, j - 4)


def weight_table(scale):
    where = {}
    for chunk in range(CHUNKS):
        for i in range(8):
            for j in range(8):
                where.setdefault(slot_modes(chunk, i, j), (chunk, i * 8 + j))
    table = np.zeros((CHUNKS, HALF_ROWS), np.float64)
    for k in range(KX * KY * KZ):
        n = (k // (KY * KZ) - KX // 2, k // KZ % KY - KY // 2, k % KZ - KZ // 2)
        squared = float(n[0] ** 2 + n[1] ** 2 + n[2] ** 2)
        if squared == 0.0:
            continue
        slot = where.get(n)
        if slot is None or n[1] > 0:
            slot = where[(-n[0], -n[1], -n[2])]
        table[slot] += math.exp(-squared / 16.0) / squared
    wide = np.ones((CHUNKS * HALF_ROWS, 128), np.float32)
    wide[:, :64] = (table.reshape(-1, 1) * scale).astype(np.float32)
    return wide


def split(value):
    high = value.astype(BF16)
    return high, (value - high.astype(F32)).astype(BF16)


def dot(left, right, contract=((1,), (0,))):
    return lax.dot_general(left, right, (contract, ((), ())), preferred_element_type=F32)


def dot_full(left, right, contract=((1,), (0,))):
    return lax.dot_general(
        left, right, (contract, ((), ())), precision=FULL_PRECISION, preferred_element_type=F32
    )


def sin_turns(turns):
    turns = turns - jnp.floor(turns + 0.5)
    folded = jnp.where(turns > 0.25, 0.5 - turns, jnp.where(turns < -0.25, -0.5 - turns, turns))
    angle = folded * (2.0 * math.pi)
    square = angle * angle
    poly = -1.0 / 39916800.0
    for divisor in (362880.0, -5040.0, 120.0, -6.0):
        poly = poly * square + 1.0 / divisor
    return angle + angle * square * poly


def wave_factors(turns, first):
    order = lax.broadcasted_iota(jnp.int32, (8, turns.shape[1]), 0) + first
    phase = order.astype(F32) * turns
    phase = phase - jnp.floor(phase + 0.5)
    return sin_turns(phase + 0.25), sin_turns(phase)


def complex_product(left, right):
    return (
        left[0] * right[0] - left[1] * right[1],
        left[0] * right[1] + left[1] * right[0],
    )


def chunk_waves(positions):
    one = wave_factors(positions[0:1], -4)
    one_up = wave_factors(positions[0:1], -3)
    two = wave_factors(positions[1:2], -8)
    three = wave_factors(positions[2:3], -4)
    three_up = wave_factors(positions[2:3], -3)

    def row(pair, index):
        return pair[0][index : index + 1], pair[1][index : index + 1]

    def chunk(number):
        if number < 8:
            outer, inner = complex_product(row(one, number), three), two
        elif number == 8:
            outer, inner = complex_product(row(one_up, 7), three_up), two
        elif number == 9:
            outer, inner = complex_product(row(three_up, 7), one_up), two
        else:
            outer, inner = one, three
        cos_part, sin_part = complex_product(
            (outer[0][:, None, :], outer[1][:, None, :]),
            (inner[0][None, :, :], inner[1][None, :, :]),
        )
        atoms = positions.shape[1]
        return jnp.concatenate(
            [cos_part.reshape(HALF_ROWS, atoms), sin_part.reshape(HALF_ROWS, atoms)], axis=0
        )

    return chunk


def live_row(count_ref, atoms):
    index = lax.broadcasted_iota(jnp.int32, (1, atoms), 1)
    return (index < count_ref[0]).astype(F32)


def send_selector(send_map, atoms, transposed=False):
    size = send_map.shape[1]
    spread = (
        lax.broadcasted_iota(jnp.int32, (size, 128), 1) % size
        == lax.broadcasted_iota(jnp.int32, (size, 128), 0)
    ).astype(F32)
    tiled = dot_full(send_map.astype(F32), spread)
    place = lax.broadcasted_iota(jnp.int32, (1, 128), 1) // size
    wanted = jnp.zeros((1, 128), F32)
    for slot, group in enumerate((2, 3, 0, 1, 1, 3, 0, 2)):
        wanted = jnp.where(place == slot, tiled[group : group + 1], wanted)
    atom = lax.broadcasted_iota(jnp.int32, (atoms, 128), 0).astype(F32)
    return (atom == jnp.round(wanted)).astype(F32).astype(BF16)


def pick_lanes(refs):
    place = lax.broadcasted_iota(jnp.int32, (64, 128), 1) // 32
    value = refs[3][...]
    for slot in range(3):
        value = jnp.where(place == slot, refs[slot][...], value)
    return value


def front_kernel(
    scalar_ref,
    positions_ref,
    cotangent_ref,
    features_ref,
    table_ref,
    map_ref,
    keep_ref,
    give_ref,
    outgoing_ref,
):
    features = features_ref[...]
    selector = send_selector(map_ref[...], features.shape[1])
    top, rest = split(features)
    middle, bottom = split(features - top.astype(F32))
    outgoing_ref[...] = dot(top, selector) + (dot(middle, selector) + dot(bottom, selector))

    chunk = chunk_waves(positions_ref[...])
    live = live_row(scalar_ref, positions_ref.shape[1])
    both = jnp.concatenate([cotangent_ref[...] * live, features * live], axis=0)
    high, low = split(both)
    stacked = jnp.concatenate([high, low], axis=0)
    first = scalar_ref[1] == 0
    half = keep_ref.shape[0] // (2 * HALF_ROWS)

    def store(number, value):
        base = number % half * 2 * HALF_ROWS
        mine = first if number < half else jnp.logical_not(first)

        @pl.when(mine)
        def _():
            keep_ref[base : base + 2 * HALF_ROWS, :] = value

        @pl.when(jnp.logical_not(mine))
        def _():
            give_ref[base : base + 2 * HALF_ROWS, :] = value

    for number in range(CHUNKS):
        wave_high, wave_low = split(chunk(number))
        part = dot(wave_high, stacked, ((1,), (1,)))
        part = part[:, :128] + part[:, 128:] + dot(wave_low, high, ((1,), (1,)))
        weight = table_ref[number * HALF_ROWS : (number + 1) * HALF_ROWS, :]
        store(number, part * jnp.concatenate([weight, weight], axis=0))
    for number in range(CHUNKS, 2 * half):
        store(number, jnp.zeros((2 * HALF_ROWS, 128), F32))


def edge_kernel(
    count_ref,
    features_ref,
    up_ref,
    down_ref,
    right_ref,
    left_ref,
    cotangent_ref,
    length_ref,
    neighbor_ref,
    short_ref,
    radial_ref,
    own_ref,
    ghost_ref,
    small_ref,
    basis_ref,
    selector_ref,
    gathered_ref,
    weight_ref,
):
    channels, atoms = features_ref.shape
    slots = length_ref.shape[0]
    columns = atoms + 128
    scale = small_ref.shape[0]
    extended = jnp.concatenate(
        [features_ref[...], pick_lanes((up_ref, down_ref, right_ref, left_ref))], axis=1
    )
    projected = jnp.concatenate(split(dot_full(short_ref[...], extended)), axis=0)
    live = live_row(count_ref, atoms)

    lengths = length_ref[...]
    targets = neighbor_ref[...]
    reach = jnp.where(jnp.logical_or(targets >= atoms, targets < count_ref[0]), live, 0.0)
    ratio = lengths * (1.0 / CUTOFF)
    envelope = 1.0 - ratio * ratio
    envelope = math.sqrt(2.0 / CUTOFF) * envelope * envelope / lengths * reach
    order = lax.broadcasted_iota(jnp.int32, (slots, 8, atoms), 1).astype(F32) + 1.0
    basis = sin_turns(order * (0.5 * ratio)[:, None, :]) * envelope[:, None, :]
    basis_ref[...] = basis.reshape(slots * 8, atoms)

    radial_high, radial_low = split(radial_ref[...])
    radial_wide = jnp.concatenate([radial_high, radial_high, radial_low], axis=1)
    column = lax.broadcasted_iota(jnp.int32, (columns, atoms), 0)

    def basis_of(slot):
        return split(basis_ref[pl.ds(pl.multiple_of(slot * 8, 8), 8), :])

    def forward(slot, total):
        selector = (column == neighbor_ref[pl.ds(slot, 1), :]).astype(F32).astype(BF16)
        selector_ref[slot] = selector
        found = dot(projected, selector)
        gathered = found[:channels] + found[channels:]
        basis_high, basis_low = basis_of(slot)
        weight = dot(radial_wide, jnp.concatenate([basis_high, basis_low, basis_high], axis=0))
        gathered_ref[slot] = gathered
        weight_ref[slot] = weight
        return total + weight * gathered

    short_sum = lax.fori_loop(0, slots, forward, jnp.zeros((channels, atoms), F32), unroll=2)
    gate = jax.nn.sigmoid(short_sum)
    upstream = cotangent_ref[...] * gate * (1.0 + short_sum * (1.0 - gate)) * live

    def backward(slot, running):
        grads, radial = running
        spread = jnp.concatenate(split(weight_ref[slot] * upstream), axis=0)
        grads = grads + dot(spread, selector_ref[slot], ((1,), (1,)))
        pulled = jnp.concatenate(split(gathered_ref[slot] * upstream), axis=0)
        pair = jnp.concatenate(basis_of(slot), axis=0)
        return grads, radial + dot(pulled, pair, ((1,), (1,)))

    grads, radial = lax.fori_loop(
        0,
        slots,
        backward,
        (jnp.zeros((2 * channels, columns), F32), jnp.zeros((2 * channels, 16), F32)),
        unroll=2,
    )
    grads = grads[:channels] + grads[channels:]
    radial = radial[:channels] + radial[channels:]
    radial = radial[:, :8] + radial[:, 8:]
    own_ref[...] = grads[:, :atoms]
    ghost_ref[...] = grads[:, atoms:]
    factor = 1.0 / math.sqrt(atoms * scale)
    short_part = dot_full(grads, extended, ((1,), (1,))) * factor
    rows = small_ref.shape[0] // channels
    small_ref[...] = jnp.zeros(small_ref.shape, F32)
    packed = jnp.concatenate(
        [short_part, radial * factor, jnp.zeros((channels, 128 - channels - 8), F32)], axis=1
    )
    small_ref[pl.ds(0, channels, stride=rows), :] = packed


def return_kernel(up_ref, down_ref, right_ref, left_ref, own_ref, map_ref, short_ref, out_ref):
    back = pick_lanes((up_ref, down_ref, right_ref, left_ref))
    selector = send_selector(map_ref[...], own_ref.shape[1])
    high, low = split(back)
    owned = own_ref[...] + (
        dot(high, selector, ((1,), (1,))) + dot(low, selector, ((1,), (1,)))
    )
    out_ref[...] = dot_full(short_ref[...], owned, ((0,), (0,)))


def charge_kernel(
    scalar_ref,
    positions_ref,
    mine_ref,
    other_ref,
    partial_ref,
    charge_ref,
    grad_ref,
    out_ref,
    *,
    factor,
):
    first = scalar_ref[1] == 0
    half = mine_ref.shape[0] // (2 * HALF_ROWS)
    chunk = chunk_waves(positions_ref[...])
    channels, atoms = partial_ref.shape
    field = jnp.zeros((2 * channels, atoms), F32)
    grad = jnp.zeros((2 * channels, 128), F32)
    for number in range(CHUNKS):
        base = number % half * 2 * HALF_ROWS
        mine = first if number < half else jnp.logical_not(first)
        rows = pl.ds(base, 2 * HALF_ROWS)
        block = jnp.where(mine, mine_ref[rows, :], other_ref[rows, :])
        turned = block.T[:channels]
        turned_high, turned_low = split(turned)
        turned = jnp.concatenate([turned_high, turned_low], axis=0)
        block_high, block_low = split(block)
        wave_high, wave_low = split(chunk(number))
        field = field + dot(turned, wave_high)
        grad = grad + dot(turned, block_high)
        extra = dot(turned_high, jnp.concatenate([wave_low, block_low], axis=1))
        field = field + jnp.concatenate([extra[:, :atoms], jnp.zeros((channels, atoms), F32)], axis=0)
        grad = grad + jnp.concatenate([extra[:, atoms:], jnp.zeros((channels, 128), F32)], axis=0)
    field = (field[:channels] + field[channels:]) * live_row(scalar_ref, atoms)
    grad = grad[:channels] + grad[channels:]
    grad_ref[...] = grad[:, channels : 2 * channels] * factor
    out_ref[...] = partial_ref[...] + dot_full(charge_ref[...], field, ((0,), (0,)))


def vmem(count):
    return [pl.BlockSpec(memory_space=pltpu.VMEM)] * count


def scalar_first(count):
    return [pl.BlockSpec(memory_space=pltpu.SMEM)] + vmem(count)


def work(micros):
    return pl.CostEstimate(
        flops=int(micros * 1e9), transcendentals=0, bytes_accessed=int(micros * 3e6)
    )


def shape(*dims):
    return jax.ShapeDtypeStruct(dims, F32)


def shifted(value, axis, step):
    size = lax.axis_size(axis)
    return lax.ppermute(value, axis, [(i, (i + step) % size) for i in range(size)])


def swapped(value):
    return lax.ppermute(value, "core", [(0, 1), (1, 0)])


def exchange(value, axes):
    return lax.all_to_all(value, axes, 0, 0, tiled=True)


def everywhere(value, axes):
    size = lax.axis_size(axes)
    return exchange(jnp.broadcast_to(value[None], (size,) + value.shape), axes)


def on_device(
    features,
    cotangent,
    positions,
    edge_length,
    neighbors,
    send_map,
    atom_count,
    short_weight,
    charge_weight,
    radial_weight,
):
    channels, atoms = features.shape
    slots = neighbors.shape[0]
    devices = lax.axis_size(ALL)
    chips = lax.axis_size(CHIPS)
    factor = 1.0 / math.sqrt(atoms * devices)
    wave_rows = -(-CHUNKS * 2 * HALF_ROWS // devices)
    half_rows = wave_rows * chips
    scalars = jnp.concatenate([atom_count, lax.axis_index("core").reshape(1)])

    keep, give, outgoing = pl.pallas_call(
        front_kernel,
        out_shape=(shape(half_rows, 128), shape(half_rows, 128), shape(channels, 128)),
        in_specs=scalar_first(5),
        out_specs=tuple(vmem(3)),
        cost_estimate=work(3.0),
    )(scalars, positions, cotangent, features, jnp.asarray(weight_table(factor)), send_map)
    pair = keep + swapped(give)
    pieces = exchange(pair.reshape(chips, 1, wave_rows * 128), CHIPS)
    arrived = (
        shifted(outgoing, SLAB, 1),
        shifted(outgoing, SLAB, -1),
        shifted(outgoing, "brick", 1),
        shifted(outgoing, "brick", -1),
    )
    mine = everywhere(jnp.sum(pieces, axis=0), CHIPS).reshape(half_rows, 128)
    other = swapped(mine)

    own, ghost, small = pl.pallas_call(
        edge_kernel,
        out_shape=(shape(channels, atoms), shape(channels, 128), shape(devices, 128)),
        in_specs=scalar_first(10),
        out_specs=tuple(vmem(3)),
        scratch_shapes=[
            pltpu.VMEM((slots * 8, atoms), F32),
            pltpu.VMEM((slots, atoms + 128, atoms), BF16),
            pltpu.VMEM((slots, channels, atoms), F32),
            pltpu.VMEM((slots, channels, atoms), F32),
        ],
        cost_estimate=work(10.0),
    )(
        scalars,
        features,
        *arrived,
        cotangent,
        edge_length,
        neighbors,
        short_weight,
        radial_weight,
    )
    small_all = everywhere(jnp.sum(exchange(small[:, None, :], ALL), axis=0), ALL)
    back = (
        shifted(ghost, SLAB, -1),
        shifted(ghost, SLAB, 1),
        shifted(ghost, "brick", -1),
        shifted(ghost, "brick", 1),
    )
    partial = pl.pallas_call(
        return_kernel,
        out_shape=shape(channels, atoms),
        in_specs=vmem(7),
        out_specs=vmem(1)[0],
        cost_estimate=work(2.0),
    )(*back, own, send_map, short_weight)
    charge_grad, feature_grad = pl.pallas_call(
        lambda *refs: charge_kernel(*refs, factor=factor),
        out_shape=(shape(channels, channels), shape(channels, atoms)),
        in_specs=scalar_first(5),
        out_specs=tuple(vmem(2)),
        cost_estimate=work(3.0),
    )(scalars, positions, mine, other, partial, charge_weight)
    small_rows = small_all.reshape(channels, devices // channels, 128)[:, 0]
    return (
        feature_grad,
        small_rows[:, :channels],
        charge_grad,
        small_rows[:, channels : channels + radial_weight.shape[1]],
    )


def solution(mesh):
    slabs, bricks = mesh.devices.shape
    fine = Mesh(mesh.devices.reshape(slabs // 2, 2, bricks), ALL)
    split_all = P(None, ALL)
    placed = (split_all,) * 6 + (P(ALL), P(), P(), P())
    return jax.shard_map(
        on_device,
        mesh=fine,
        in_specs=placed,
        out_specs=(split_all, P(), P(), P()),
        check_vma=False,
    )
```

```python
import functools
import math

import jax
import jax.numpy as jnp
import numpy as np
from jax import lax
from jax.experimental import pallas as pl
from jax.experimental.pallas import tpu as pltpu
from jax.sharding import Mesh
from jax.sharding import PartitionSpec as P

KX = 8
KY = 16
KZ = 8
CUTOFF = 6.0
HALF_ROWS = 64
CHUNKS = 11
F32 = jnp.float32
BF16 = jnp.bfloat16
FULL_PRECISION = lax.Precision.HIGHEST
SLAB = ("chip", "core")
CHIPS = ("chip", "brick")
ALL = ("chip", "core", "brick")


def slot_modes(chunk, i, j):
    if chunk < 8:
        return (chunk - 4, j - 8, i - 4)
    if chunk == 8:
        return (4, j - 8, i - 3)
    if chunk == 9:
        return (i - 3, j - 8, 4)
    return (i - 4, 0, j - 4)


def weight_table(scale):
    where = {}
    for chunk in range(CHUNKS):
        for i in range(8):
            for j in range(8):
                where.setdefault(slot_modes(chunk, i, j), (chunk, i * 8 + j))
    table = np.zeros((CHUNKS, HALF_ROWS), np.float64)
    for k in range(KX * KY * KZ):
        n = (k // (KY * KZ) - KX // 2, k // KZ % KY - KY // 2, k % KZ - KZ // 2)
        squared = float(n[0] ** 2 + n[1] ** 2 + n[2] ** 2)
        if squared == 0.0:
            continue
        slot = where.get(n)
        if slot is None or n[1] > 0:
            slot = where[(-n[0], -n[1], -n[2])]
        table[slot] += math.exp(-squared / 16.0) / squared
    wide = np.ones((CHUNKS * HALF_ROWS, 128), np.float32)
    wide[:, :64] = (table.reshape(-1, 1) * scale).astype(np.float32)
    return wide


def split(value):
    high = value.astype(BF16)
    return high, (value - high.astype(F32)).astype(BF16)


def dot(left, right, contract=((1,), (0,))):
    return lax.dot_general(left, right, (contract, ((), ())), preferred_element_type=F32)


def dot_full(left, right, contract=((1,), (0,))):
    return lax.dot_general(
        left, right, (contract, ((), ())), precision=FULL_PRECISION, preferred_element_type=F32
    )


def sin_turns(turns):
    turns = turns - jnp.floor(turns + 0.5)
    folded = jnp.where(turns > 0.25, 0.5 - turns, jnp.where(turns < -0.25, -0.5 - turns, turns))
    angle = folded * (2.0 * math.pi)
    square = angle * angle
    poly = -1.0 / 39916800.0
    for divisor in (362880.0, -5040.0, 120.0, -6.0):
        poly = poly * square + 1.0 / divisor
    return angle + angle * square * poly


def wave_factors(turns, first):
    order = lax.broadcasted_iota(jnp.int32, (8, turns.shape[1]), 0) + first
    phase = order.astype(F32) * turns
    phase = phase - jnp.floor(phase + 0.5)
    return sin_turns(phase + 0.25), sin_turns(phase)


def complex_product(left, right):
    return (
        left[0] * right[0] - left[1] * right[1],
        left[0] * right[1] + left[1] * right[0],
    )


def chunk_waves(positions):
    one = wave_factors(positions[0:1], -4)
    one_up = wave_factors(positions[0:1], -3)
    two = wave_factors(positions[1:2], -8)
    three = wave_factors(positions[2:3], -4)
    three_up = wave_factors(positions[2:3], -3)

    def row(pair, index):
        return pair[0][index : index + 1], pair[1][index : index + 1]

    def chunk(number):
        if number < 8:
            outer, inner = complex_product(row(one, number), three), two
        elif number == 8:
            outer, inner = complex_product(row(one_up, 7), three_up), two
        elif number == 9:
            outer, inner = complex_product(row(three_up, 7), one_up), two
        else:
            outer, inner = one, three
        cos_part, sin_part = complex_product(
            (outer[0][:, None, :], outer[1][:, None, :]),
            (inner[0][None, :, :], inner[1][None, :, :]),
        )
        atoms = positions.shape[1]
        return jnp.concatenate(
            [cos_part.reshape(HALF_ROWS, atoms), sin_part.reshape(HALF_ROWS, atoms)], axis=0
        )

    return chunk


def live_row(count_ref, atoms):
    index = lax.broadcasted_iota(jnp.int32, (1, atoms), 1)
    return (index < count_ref[0]).astype(F32)


def send_selector(send_map, atoms, transposed=False):
    size = send_map.shape[1]
    spread = (
        lax.broadcasted_iota(jnp.int32, (size, 128), 1) % size
        == lax.broadcasted_iota(jnp.int32, (size, 128), 0)
    ).astype(F32)
    tiled = dot_full(send_map.astype(F32), spread)
    place = lax.broadcasted_iota(jnp.int32, (1, 128), 1) // size
    wanted = jnp.zeros((1, 128), F32)
    for slot, group in enumerate((2, 3, 0, 1, 1, 3, 0, 2)):
        wanted = jnp.where(place == slot, tiled[group : group + 1], wanted)
    atom = lax.broadcasted_iota(jnp.int32, (atoms, 128), 0).astype(F32)
    return (atom == jnp.round(wanted)).astype(F32).astype(BF16)


def pick_lanes(refs):
    place = lax.broadcasted_iota(jnp.int32, (64, 128), 1) // 32
    value = refs[3][...]
    for slot in range(3):
        value = jnp.where(place == slot, refs[slot][...], value)
    return value


def wave_kernel(
    count_ref,
    positions_ref,
    cotangent_ref,
    features_ref,
    table_ref,
    map_ref,
    keep_ref,
    give_ref,
    outgoing_ref,
):
    features = features_ref[...]
    selector = send_selector(map_ref[...], features.shape[1])
    top, rest = split(features)
    middle, bottom = split(features - top.astype(F32))
    outgoing_ref[...] = dot(top, selector) + (dot(middle, selector) + dot(bottom, selector))
    chunk = chunk_waves(positions_ref[...])
    live = live_row(count_ref, positions_ref.shape[1])
    both = jnp.concatenate([cotangent_ref[...] * live, features * live], axis=0)
    high, low = split(both)
    stacked = jnp.concatenate([high, low], axis=0)
    first = lax.axis_index("core") == 0

    def store(unit, value):
        rows = pl.ds(unit % CHUNKS * HALF_ROWS, HALF_ROWS)
        mine = first if unit < CHUNKS else jnp.logical_not(first)

        @pl.when(mine)
        def _():
            keep_ref[rows, :] = value

        @pl.when(jnp.logical_not(mine))
        def _():
            give_ref[rows, :] = value

    for number in range(CHUNKS):
        wave_high, wave_low = split(chunk(number))
        part = dot(wave_high, stacked, ((1,), (1,)))
        part = part[:, :128] + part[:, 128:] + dot(wave_low, high, ((1,), (1,)))
        weight = table_ref[number * HALF_ROWS : (number + 1) * HALF_ROWS, :]
        store(2 * number, part[:HALF_ROWS] * weight)
        store(2 * number + 1, part[HALF_ROWS:] * weight)


def edge_kernel(
    count_ref,
    features_ref,
    right_ref,
    left_ref,
    up_ref,
    down_ref,
    cotangent_ref,
    length_ref,
    neighbor_ref,
    short_ref,
    radial_ref,
    keep_ref,
    taken_ref,
    own_ref,
    ghost_ref,
    payload_ref,
    basis_ref,
    selector_ref,
    gathered_ref,
    weight_ref,
    *,
    factor,
):
    channels, atoms = features_ref.shape
    slots = length_ref.shape[0]
    columns = atoms + 128
    group = 4
    wide = group * atoms
    waves = keep_ref.shape[0]
    payload_ref[:waves, :] = keep_ref[...] + taken_ref[...]
    extended = jnp.concatenate(
        [features_ref[...], pick_lanes((up_ref, down_ref, right_ref, left_ref))], axis=1
    )
    projected = jnp.concatenate(split(dot_full(short_ref[...], extended)), axis=0)
    live = live_row(count_ref, atoms)

    lengths = length_ref[...]
    targets = neighbor_ref[...]
    reach = jnp.where(jnp.logical_or(targets >= atoms, targets < count_ref[0]), live, 0.0)
    ratio = lengths * (1.0 / CUTOFF)
    envelope = 1.0 - ratio * ratio
    envelope = math.sqrt(2.0 / CUTOFF) * envelope * envelope / lengths * reach
    order = lax.broadcasted_iota(jnp.int32, (slots, 8, atoms), 1).astype(F32) + 1.0
    basis = sin_turns(order * (0.5 * ratio)[:, None, :]) * envelope[:, None, :]
    basis_ref[...] = basis.reshape(slots * 8, atoms)

    radial_high, radial_low = split(radial_ref[...])
    radial_wide = jnp.concatenate([radial_high, radial_high, radial_low], axis=0)
    column = lax.broadcasted_iota(jnp.int32, (columns, wide), 0)

    def side_by_side(pieces):
        return jnp.concatenate(pieces, axis=1)

    def basis_of(turn):
        base = turn * group * 8
        return split(
            side_by_side(
                [basis_ref[pl.ds(pl.multiple_of(base + 8 * i, 8), 8), :] for i in range(group)]
            )
        )

    def forward(turn, total):
        picks = side_by_side([neighbor_ref[pl.ds(turn * group + i, 1), :] for i in range(group)])
        selector = (column == picks).astype(F32).astype(BF16)
        selector_ref[turn] = selector
        found = dot(projected, selector)
        gathered = found[:channels] + found[channels:]
        basis_high, basis_low = basis_of(turn)
        weight = dot(
            radial_wide, jnp.concatenate([basis_high, basis_low, basis_high], axis=0), ((0,), (0,))
        )
        gathered_ref[turn] = gathered
        weight_ref[turn] = weight
        product = weight * gathered
        for i in range(group):
            total = total + product[:, i * atoms : (i + 1) * atoms]
        return total

    turns = slots // group
    short_sum = lax.fori_loop(0, turns, forward, jnp.zeros((channels, atoms), F32))
    gate = jax.nn.sigmoid(short_sum)
    upstream = cotangent_ref[...] * gate * (1.0 + short_sum * (1.0 - gate)) * live
    upstream = side_by_side([upstream] * group)

    def backward(turn, running):
        grads, radial = running
        spread = jnp.concatenate(split(weight_ref[turn] * upstream), axis=0)
        grads = grads + dot(spread, selector_ref[turn], ((1,), (1,)))
        pulled = jnp.concatenate(split(gathered_ref[turn] * upstream), axis=0)
        pair = jnp.concatenate(basis_of(turn), axis=0)
        return grads, radial + dot(pulled, pair, ((1,), (1,)))

    grads, radial = lax.fori_loop(
        0,
        turns,
        backward,
        (jnp.zeros((2 * channels, columns), F32), jnp.zeros((2 * channels, 16), F32)),
    )
    grads = grads[:channels] + grads[channels:]
    radial = radial[:channels] + radial[channels:]
    radial = radial[:, :8] + radial[:, 8:]
    own_ref[...] = grads[:, :atoms]
    ghost_ref[...] = grads[:, atoms:]
    short_part = dot_full(grads, extended, ((1,), (1,))) * factor
    payload_ref[waves:, :] = jnp.concatenate(
        [short_part, radial * factor, jnp.zeros((channels, 128 - channels - 8), F32)], axis=1
    )


def return_kernel(right_ref, left_ref, up_ref, down_ref, own_ref, map_ref, short_ref, out_ref):
    back = pick_lanes((up_ref, down_ref, right_ref, left_ref))
    selector = send_selector(map_ref[...], own_ref.shape[1])
    high, low = split(back)
    owned = own_ref[...] + (
        dot(high, selector, ((1,), (1,))) + dot(low, selector, ((1,), (1,)))
    )
    out_ref[...] = dot_full(short_ref[...], owned, ((0,), (0,)))


def charge_kernel(
    count_ref,
    positions_ref,
    mine_ref,
    other_ref,
    partial_ref,
    charge_ref,
    grad_ref,
    out_ref,
    short_ref,
    radial_ref,
    *,
    factor,
):
    first = lax.axis_index("core") == 0
    waves = CHUNKS * HALF_ROWS
    small = mine_ref[waves:, :] + other_ref[waves:, :]
    channels, atoms = partial_ref.shape
    short_ref[...] = small[:, :channels]
    radial_ref[...] = small.T[channels : channels + 8, :]

    def unit(number):
        rows = pl.ds(number % CHUNKS * HALF_ROWS, HALF_ROWS)
        mine = first if number < CHUNKS else jnp.logical_not(first)
        return jnp.where(mine, mine_ref[rows, :], other_ref[rows, :])

    chunk = chunk_waves(positions_ref[...])
    field = jnp.zeros((2 * channels, atoms), F32)
    grad = jnp.zeros((2 * channels, 128), F32)
    for number in range(CHUNKS):
        block = jnp.concatenate([unit(2 * number), unit(2 * number + 1)], axis=0)
        turned = block.T[:channels]
        turned_high, turned_low = split(turned)
        turned = jnp.concatenate([turned_high, turned_low], axis=0)
        block_high, block_low = split(block)
        wave_high, wave_low = split(chunk(number))
        field = field + dot(turned, wave_high)
        grad = grad + dot(turned, block_high)
        extra = dot(turned_high, jnp.concatenate([wave_low, block_low], axis=1))
        field = field + jnp.concatenate([extra[:, :atoms], jnp.zeros((channels, atoms), F32)], axis=0)
        grad = grad + jnp.concatenate([extra[:, atoms:], jnp.zeros((channels, 128), F32)], axis=0)
    field = (field[:channels] + field[channels:]) * live_row(count_ref, atoms)
    grad = grad[:channels] + grad[channels:]
    grad_ref[...] = grad[:, channels : 2 * channels] * factor
    out_ref[...] = partial_ref[...] + dot_full(charge_ref[...], field, ((0,), (0,)))


def vmem(count):
    return [pl.BlockSpec(memory_space=pltpu.VMEM)] * count


def scalar_first(count):
    return [pl.BlockSpec(memory_space=pltpu.SMEM)] + vmem(count)


def work(micros):
    return pl.CostEstimate(
        flops=int(micros * 1e9), transcendentals=0, bytes_accessed=int(micros * 3e6)
    )


def shape(*dims):
    return jax.ShapeDtypeStruct(dims, F32)


def shifted(value, axis, step):
    size = lax.axis_size(axis)
    return lax.ppermute(value, axis, [(i, (i + step) % size) for i in range(size)])


def swapped(value):
    return lax.ppermute(value, "core", [(0, 1), (1, 0)])


def exchange(value, axes):
    return lax.all_to_all(value, axes, 0, 0, tiled=True)


def everywhere(value, axes):
    size = lax.axis_size(axes)
    return exchange(jnp.broadcast_to(value[None], (size,) + value.shape), axes)


def on_device(
    features,
    cotangent,
    positions,
    edge_length,
    neighbors,
    send_map,
    atom_count,
    short_weight,
    charge_weight,
    radial_weight,
):
    channels, atoms = features.shape
    slots = neighbors.shape[0]
    devices = lax.axis_size(ALL)
    chips = lax.axis_size(CHIPS)
    factor = 1.0 / math.sqrt(atoms * devices)
    half = CHUNKS * HALF_ROWS
    rows = half + channels
    width = rows // chips * 128

    keep, give, outgoing = pl.pallas_call(
        wave_kernel,
        out_shape=(shape(half, 128), shape(half, 128), shape(channels, 128)),
        in_specs=scalar_first(5),
        out_specs=tuple(vmem(3)),
        cost_estimate=work(4.0),
    )(atom_count, positions, cotangent, features, jnp.asarray(weight_table(factor)), send_map)
    right = shifted(outgoing, "brick", 1)
    left = shifted(outgoing, "brick", -1)
    up = shifted(outgoing, SLAB, 1)
    down = shifted(outgoing, SLAB, -1)
    taken = swapped(give)

    own, ghost, payload = pl.pallas_call(
        functools.partial(edge_kernel, factor=factor),
        out_shape=(shape(channels, atoms), shape(channels, 128), shape(rows, 128)),
        in_specs=scalar_first(12),
        out_specs=tuple(vmem(3)),
        scratch_shapes=[
            pltpu.VMEM((slots * 8, atoms), F32),
            pltpu.VMEM((slots // 4, atoms + 128, 4 * atoms), BF16),
            pltpu.VMEM((slots // 4, channels, 4 * atoms), F32),
            pltpu.VMEM((slots // 4, channels, 4 * atoms), F32),
        ],
        cost_estimate=work(10.0),
    )(
        atom_count,
        features,
        right,
        left,
        up,
        down,
        cotangent,
        edge_length,
        neighbors,
        short_weight,
        radial_weight.T,
        keep,
        taken,
    )
    pieces = exchange(payload.reshape(chips, 1, width), CHIPS)
    back = (
        shifted(ghost, "brick", -1),
        shifted(ghost, "brick", 1),
        shifted(ghost, SLAB, -1),
        shifted(ghost, SLAB, 1),
    )
    partial = pl.pallas_call(
        return_kernel,
        out_shape=shape(channels, atoms),
        in_specs=vmem(7),
        out_specs=vmem(1)[0],
        cost_estimate=work(2.0),
    )(*back, own, send_map, short_weight)
    summed, partial = lax.optimization_barrier((jnp.sum(pieces, axis=0), partial))
    mine = everywhere(summed, CHIPS).reshape(rows, 128)
    other = swapped(mine)
    charge_grad, feature_grad, short_grad, radial_grad = pl.pallas_call(
        functools.partial(charge_kernel, factor=factor),
        out_shape=(
            shape(channels, channels),
            shape(channels, atoms),
            shape(channels, channels),
            shape(radial_weight.shape[1], channels),
        ),
        in_specs=scalar_first(5),
        out_specs=tuple(vmem(4)),
        cost_estimate=work(3.0),
    )(atom_count, positions, mine, other, partial, charge_weight)
    return feature_grad, short_grad, charge_grad, radial_grad.T


def solution(mesh):
    slabs, bricks = mesh.devices.shape
    fine = Mesh(mesh.devices.reshape(slabs // 2, 2, bricks), ALL)
    split_all = P(None, ALL)
    placed = (split_all,) * 6 + (P(ALL), P(), P(), P())
    return jax.shard_map(
        on_device,
        mesh=fine,
        in_specs=placed,
        out_specs=(split_all, P(), P(), P()),
        check_vma=False,
    )
```

```python
import functools
import math

import jax
import jax.numpy as jnp
import numpy as np
from jax import lax
from jax.experimental import pallas as pl
from jax.experimental.pallas import tpu as pltpu
from jax.sharding import Mesh
from jax.sharding import PartitionSpec as P

KX = 8
KY = 16
KZ = 8
CUTOFF = 6.0
HALF_ROWS = 64
CHUNKS = 11
F32 = jnp.float32
BF16 = jnp.bfloat16
FULL_PRECISION = lax.Precision.HIGHEST
SLAB = ("chip", "core")
CHIPS = ("chip", "brick")
ALL = ("chip", "core", "brick")


def slot_modes(chunk, i, j):
    if chunk < 8:
        return (chunk - 4, j - 8, i - 4)
    if chunk == 8:
        return (4, j - 8, i - 3)
    if chunk == 9:
        return (i - 3, j - 8, 4)
    return (i - 4, 0, j - 4)


def weight_table(scale):
    where = {}
    for chunk in range(CHUNKS):
        for i in range(8):
            for j in range(8):
                where.setdefault(slot_modes(chunk, i, j), (chunk, i * 8 + j))
    table = np.zeros((CHUNKS, HALF_ROWS), np.float64)
    for k in range(KX * KY * KZ):
        n = (k // (KY * KZ) - KX // 2, k // KZ % KY - KY // 2, k % KZ - KZ // 2)
        squared = float(n[0] ** 2 + n[1] ** 2 + n[2] ** 2)
        if squared == 0.0:
            continue
        slot = where.get(n)
        if slot is None or n[1] > 0:
            slot = where[(-n[0], -n[1], -n[2])]
        table[slot] += math.exp(-squared / 16.0) / squared
    wide = np.ones((CHUNKS * HALF_ROWS, 128), np.float32)
    wide[:, :64] = (table.reshape(-1, 1) * scale).astype(np.float32)
    return wide


def split(value):
    high = value.astype(BF16)
    return high, (value - high.astype(F32)).astype(BF16)


def dot(left, right, contract=((1,), (0,))):
    return lax.dot_general(left, right, (contract, ((), ())), preferred_element_type=F32)


def dot_full(left, right, contract=((1,), (0,))):
    return lax.dot_general(
        left, right, (contract, ((), ())), precision=FULL_PRECISION, preferred_element_type=F32
    )


def sin_turns(turns):
    turns = turns - jnp.floor(turns + 0.5)
    folded = jnp.where(turns > 0.25, 0.5 - turns, jnp.where(turns < -0.25, -0.5 - turns, turns))
    angle = folded * (2.0 * math.pi)
    square = angle * angle
    poly = -1.0 / 39916800.0
    for divisor in (362880.0, -5040.0, 120.0, -6.0):
        poly = poly * square + 1.0 / divisor
    return angle + angle * square * poly


def wave_factors(turns, first):
    order = lax.broadcasted_iota(jnp.int32, (8, turns.shape[1]), 0) + first
    phase = order.astype(F32) * turns
    phase = phase - jnp.floor(phase + 0.5)
    return sin_turns(phase + 0.25), sin_turns(phase)


def complex_product(left, right):
    return (
        left[0] * right[0] - left[1] * right[1],
        left[0] * right[1] + left[1] * right[0],
    )


def chunk_waves(positions):
    one = wave_factors(positions[0:1], -4)
    one_up = wave_factors(positions[0:1], -3)
    two = wave_factors(positions[1:2], -8)
    three = wave_factors(positions[2:3], -4)
    three_up = wave_factors(positions[2:3], -3)

    def row(pair, index):
        return pair[0][index : index + 1], pair[1][index : index + 1]

    def chunk(number):
        if number < 8:
            outer, inner = complex_product(row(one, number), three), two
        elif number == 8:
            outer, inner = complex_product(row(one_up, 7), three_up), two
        elif number == 9:
            outer, inner = complex_product(row(three_up, 7), one_up), two
        else:
            outer, inner = one, three
        cos_part, sin_part = complex_product(
            (outer[0][:, None, :], outer[1][:, None, :]),
            (inner[0][None, :, :], inner[1][None, :, :]),
        )
        atoms = positions.shape[1]
        return jnp.concatenate(
            [cos_part.reshape(HALF_ROWS, atoms), sin_part.reshape(HALF_ROWS, atoms)], axis=0
        )

    return chunk


def live_row(count_ref, atoms):
    index = lax.broadcasted_iota(jnp.int32, (1, atoms), 1)
    return (index < count_ref[0]).astype(F32)


def send_selector(send_map, atoms, transposed=False):
    size = send_map.shape[1]
    spread = (
        lax.broadcasted_iota(jnp.int32, (size, 128), 1) % size
        == lax.broadcasted_iota(jnp.int32, (size, 128), 0)
    ).astype(F32)
    tiled = dot_full(send_map.astype(F32), spread)
    place = lax.broadcasted_iota(jnp.int32, (1, 128), 1) // size
    wanted = jnp.zeros((1, 128), F32)
    for slot, group in enumerate((2, 3, 0, 1, 1, 3, 0, 2)):
        wanted = jnp.where(place == slot, tiled[group : group + 1], wanted)
    atom = lax.broadcasted_iota(jnp.int32, (atoms, 128), 0).astype(F32)
    return (atom == jnp.round(wanted)).astype(F32).astype(BF16)


def pick_lanes(refs):
    place = lax.broadcasted_iota(jnp.int32, (64, 128), 1) // 32
    value = refs[3][...]
    for slot in range(3):
        value = jnp.where(place == slot, refs[slot][...], value)
    return value


def wave_kernel(
    count_ref,
    positions_ref,
    cotangent_ref,
    features_ref,
    table_ref,
    map_ref,
    keep_ref,
    give_ref,
    outgoing_ref,
):
    features = features_ref[...]
    selector = send_selector(map_ref[...], features.shape[1])
    top, rest = split(features)
    middle, bottom = split(features - top.astype(F32))
    outgoing_ref[...] = dot(top, selector) + (dot(middle, selector) + dot(bottom, selector))
    chunk = chunk_waves(positions_ref[...])
    live = live_row(count_ref, positions_ref.shape[1])
    both = jnp.concatenate([cotangent_ref[...] * live, features * live], axis=0)
    high, low = split(both)
    stacked = jnp.concatenate([high, low], axis=0)
    first = lax.axis_index("core") == 0

    def store(unit, value):
        rows = pl.ds(unit % CHUNKS * HALF_ROWS, HALF_ROWS)
        mine = first if unit < CHUNKS else jnp.logical_not(first)

        @pl.when(mine)
        def _():
            keep_ref[rows, :] = value

        @pl.when(jnp.logical_not(mine))
        def _():
            give_ref[rows, :] = value

    for number in range(CHUNKS):
        wave_high, wave_low = split(chunk(number))
        part = dot(wave_high, stacked, ((1,), (1,)))
        part = part[:, :128] + part[:, 128:] + dot(wave_low, high, ((1,), (1,)))
        weight = table_ref[number * HALF_ROWS : (number + 1) * HALF_ROWS, :]
        store(2 * number, part[:HALF_ROWS] * weight)
        store(2 * number + 1, part[HALF_ROWS:] * weight)


def edge_kernel(
    count_ref,
    features_ref,
    left_ref,
    right_ref,
    down_ref,
    up_ref,
    cotangent_ref,
    length_ref,
    neighbor_ref,
    short_ref,
    radial_ref,
    keep_ref,
    taken_ref,
    own_ref,
    ghost_ref,
    payload_ref,
    basis_ref,
    selector_ref,
    gathered_ref,
    weight_ref,
    *,
    factor,
):
    channels, atoms = features_ref.shape
    slots = length_ref.shape[0]
    columns = atoms + 128
    group = 4
    wide = group * atoms
    waves = keep_ref.shape[0]
    payload_ref[:waves, :] = keep_ref[...] + taken_ref[...]
    extended = jnp.concatenate(
        [features_ref[...], pick_lanes((up_ref, down_ref, right_ref, left_ref))], axis=1
    )
    projected = jnp.concatenate(split(dot_full(short_ref[...], extended)), axis=0)
    live = live_row(count_ref, atoms)

    lengths = length_ref[...]
    targets = neighbor_ref[...]
    reach = jnp.where(jnp.logical_or(targets >= atoms, targets < count_ref[0]), live, 0.0)
    ratio = lengths * (1.0 / CUTOFF)
    envelope = 1.0 - ratio * ratio
    envelope = math.sqrt(2.0 / CUTOFF) * envelope * envelope / lengths * reach
    order = lax.broadcasted_iota(jnp.int32, (slots, 8, atoms), 1).astype(F32) + 1.0
    basis = sin_turns(order * (0.5 * ratio)[:, None, :]) * envelope[:, None, :]
    basis_ref[...] = basis.reshape(slots * 8, atoms)

    radial_high, radial_low = split(radial_ref[...])
    radial_wide = jnp.concatenate([radial_high, radial_high, radial_low], axis=0)
    column = lax.broadcasted_iota(jnp.int32, (columns, wide), 0)

    def side_by_side(pieces):
        return jnp.concatenate(pieces, axis=1)

    def basis_of(turn):
        base = turn * group * 8
        return split(
            side_by_side(
                [basis_ref[pl.ds(pl.multiple_of(base + 8 * i, 8), 8), :] for i in range(group)]
            )
        )

    def forward(turn, total):
        picks = side_by_side([neighbor_ref[pl.ds(turn * group + i, 1), :] for i in range(group)])
        selector = (column == picks).astype(F32).astype(BF16)
        selector_ref[turn] = selector
        found = dot(projected, selector)
        gathered = found[:channels] + found[channels:]
        basis_high, basis_low = basis_of(turn)
        weight = dot(
            radial_wide, jnp.concatenate([basis_high, basis_low, basis_high], axis=0), ((0,), (0,))
        )
        gathered_ref[turn] = gathered
        weight_ref[turn] = weight
        product = weight * gathered
        for i in range(group):
            total = total + product[:, i * atoms : (i + 1) * atoms]
        return total

    turns = slots // group
    short_sum = lax.fori_loop(0, turns, forward, jnp.zeros((channels, atoms), F32))
    gate = jax.nn.sigmoid(short_sum)
    upstream = cotangent_ref[...] * gate * (1.0 + short_sum * (1.0 - gate)) * live
    upstream = side_by_side([upstream] * group)

    def backward(turn, running):
        grads, radial = running
        spread = jnp.concatenate(split(weight_ref[turn] * upstream), axis=0)
        grads = grads + dot(spread, selector_ref[turn], ((1,), (1,)))
        pulled = jnp.concatenate(split(gathered_ref[turn] * upstream), axis=0)
        pair = jnp.concatenate(basis_of(turn), axis=0)
        return grads, radial + dot(pulled, pair, ((1,), (1,)))

    grads, radial = lax.fori_loop(
        0,
        turns,
        backward,
        (jnp.zeros((2 * channels, columns), F32), jnp.zeros((2 * channels, 16), F32)),
    )
    grads = grads[:channels] + grads[channels:]
    radial = radial[:channels] + radial[channels:]
    radial = radial[:, :8] + radial[:, 8:]
    own_ref[...] = grads[:, :atoms]
    ghost_ref[...] = grads[:, atoms:]
    short_part = dot_full(grads, extended, ((1,), (1,))) * factor
    payload_ref[waves:, :] = jnp.concatenate(
        [short_part, radial * factor, jnp.zeros((channels, 128 - channels - 8), F32)], axis=1
    )


def return_kernel(right_ref, left_ref, up_ref, down_ref, own_ref, map_ref, short_ref, out_ref):
    back = pick_lanes((up_ref, down_ref, right_ref, left_ref))
    selector = send_selector(map_ref[...], own_ref.shape[1])
    high, low = split(back)
    owned = own_ref[...] + (
        dot(high, selector, ((1,), (1,))) + dot(low, selector, ((1,), (1,)))
    )
    out_ref[...] = dot_full(short_ref[...], owned, ((0,), (0,)))


def charge_kernel(
    count_ref,
    positions_ref,
    mine_ref,
    other_ref,
    partial_ref,
    charge_ref,
    grad_ref,
    out_ref,
    short_ref,
    radial_ref,
    *,
    factor,
):
    first = lax.axis_index("core") == 0
    waves = CHUNKS * HALF_ROWS
    small = mine_ref[waves:, :] + other_ref[waves:, :]
    channels, atoms = partial_ref.shape
    short_ref[...] = small[:, :channels]
    radial_ref[...] = small.T[channels : channels + 8, :]

    def unit(number):
        rows = pl.ds(number % CHUNKS * HALF_ROWS, HALF_ROWS)
        mine = first if number < CHUNKS else jnp.logical_not(first)
        return jnp.where(mine, mine_ref[rows, :], other_ref[rows, :])

    chunk = chunk_waves(positions_ref[...])
    field = jnp.zeros((2 * channels, atoms), F32)
    grad = jnp.zeros((2 * channels, 128), F32)
    for number in range(CHUNKS):
        block = jnp.concatenate([unit(2 * number), unit(2 * number + 1)], axis=0)
        turned = block.T[:channels]
        turned_high, turned_low = split(turned)
        turned = jnp.concatenate([turned_high, turned_low], axis=0)
        block_high, block_low = split(block)
        wave_high, wave_low = split(chunk(number))
        field = field + dot(turned, wave_high)
        grad = grad + dot(turned, block_high)
        extra = dot(turned_high, jnp.concatenate([wave_low, block_low], axis=1))
        field = field + jnp.concatenate([extra[:, :atoms], jnp.zeros((channels, atoms), F32)], axis=0)
        grad = grad + jnp.concatenate([extra[:, atoms:], jnp.zeros((channels, 128), F32)], axis=0)
    field = (field[:channels] + field[channels:]) * live_row(count_ref, atoms)
    grad = grad[:channels] + grad[channels:]
    grad_ref[...] = grad[:, channels : 2 * channels] * factor
    out_ref[...] = partial_ref[...] + dot_full(charge_ref[...], field, ((0,), (0,)))


def vmem(count):
    return [pl.BlockSpec(memory_space=pltpu.VMEM)] * count


def scalar_first(count):
    return [pl.BlockSpec(memory_space=pltpu.SMEM)] + vmem(count)


def work(micros):
    return pl.CostEstimate(
        flops=int(micros * 1e9), transcendentals=0, bytes_accessed=int(micros * 3e6)
    )


def shape(*dims):
    return jax.ShapeDtypeStruct(dims, F32)


def shifted(value, axis, step):
    size = lax.axis_size(axis)
    return lax.ppermute(value, axis, [(i, (i + step) % size) for i in range(size)])


def swapped(value):
    return lax.ppermute(value, "core", [(0, 1), (1, 0)])


def exchange(value, axes):
    return lax.all_to_all(value, axes, 0, 0, tiled=True)


def everywhere(value, axes):
    size = lax.axis_size(axes)
    return exchange(jnp.broadcast_to(value[None], (size,) + value.shape), axes)


def on_device(
    features,
    cotangent,
    positions,
    edge_length,
    neighbors,
    send_map,
    atom_count,
    short_weight,
    charge_weight,
    radial_weight,
):
    channels, atoms = features.shape
    slots = neighbors.shape[0]
    devices = lax.axis_size(ALL)
    chips = lax.axis_size(CHIPS)
    factor = 1.0 / math.sqrt(atoms * devices)
    half = CHUNKS * HALF_ROWS
    rows = half + channels
    width = rows // chips * 128

    keep, give, outgoing = pl.pallas_call(
        wave_kernel,
        out_shape=(shape(half, 128), shape(half, 128), shape(channels, 128)),
        in_specs=scalar_first(5),
        out_specs=tuple(vmem(3)),
        cost_estimate=work(4.0),
    )(atom_count, positions, cotangent, features, jnp.asarray(weight_table(factor)), send_map)
    right = shifted(outgoing, "brick", 1)
    left = shifted(outgoing, "brick", -1)
    up = shifted(outgoing, SLAB, 1)
    down = shifted(outgoing, SLAB, -1)
    taken = swapped(give)

    own, ghost, payload = pl.pallas_call(
        functools.partial(edge_kernel, factor=factor),
        out_shape=(shape(channels, atoms), shape(channels, 128), shape(rows, 128)),
        in_specs=scalar_first(12),
        out_specs=tuple(vmem(3)),
        scratch_shapes=[
            pltpu.VMEM((slots * 8, atoms), F32),
            pltpu.VMEM((slots // 4, atoms + 128, 4 * atoms), BF16),
            pltpu.VMEM((slots // 4, channels, 4 * atoms), F32),
            pltpu.VMEM((slots // 4, channels, 4 * atoms), F32),
        ],
        cost_estimate=work(10.0),
    )(
        atom_count,
        features,
        left,
        right,
        down,
        up,
        cotangent,
        edge_length,
        neighbors,
        short_weight,
        radial_weight.T,
        keep,
        taken,
    )
    pieces = exchange(payload.reshape(chips, 1, width), CHIPS)
    back_left = shifted(ghost, "brick", -1)
    back_right = shifted(ghost, "brick", 1)
    back_down = shifted(ghost, SLAB, -1)
    back_up = shifted(ghost, SLAB, 1)
    summed, back_left, back_right = lax.optimization_barrier(
        (jnp.sum(pieces, axis=0), back_left, back_right)
    )
    mine = everywhere(summed, CHIPS).reshape(rows, 128)
    partial = pl.pallas_call(
        return_kernel,
        out_shape=shape(channels, atoms),
        in_specs=vmem(7),
        out_specs=vmem(1)[0],
        cost_estimate=work(2.0),
    )(back_left, back_right, back_down, back_up, own, send_map, short_weight)
    mine, partial = lax.optimization_barrier((mine, partial))
    other = swapped(mine)
    charge_grad, feature_grad, short_grad, radial_grad = pl.pallas_call(
        functools.partial(charge_kernel, factor=factor),
        out_shape=(
            shape(channels, channels),
            shape(channels, atoms),
            shape(channels, channels),
            shape(radial_weight.shape[1], channels),
        ),
        in_specs=scalar_first(5),
        out_specs=tuple(vmem(4)),
        cost_estimate=work(3.0),
    )(atom_count, positions, mine, other, partial, charge_weight)
    return feature_grad, short_grad, charge_grad, radial_grad.T


def solution(mesh):
    slabs, bricks = mesh.devices.shape
    fine = Mesh(mesh.devices.reshape(slabs // 2, 2, bricks), ALL)
    split_all = P(None, ALL)
    placed = (split_all,) * 6 + (P(ALL), P(), P(), P())
    return jax.shard_map(
        on_device,
        mesh=fine,
        in_specs=placed,
        out_specs=(split_all, P(), P(), P()),
        check_vma=False,
    )
```

```python
import functools
import math

import jax
import jax.numpy as jnp
import numpy as np
from jax import lax
from jax.experimental import pallas as pl
from jax.experimental.pallas import tpu as pltpu
from jax.sharding import Mesh
from jax.sharding import PartitionSpec as P

KX = 8
KY = 16
KZ = 8
CUTOFF = 6.0
HALF_ROWS = 64
CHUNKS = 11
F32 = jnp.float32
BF16 = jnp.bfloat16
FULL_PRECISION = lax.Precision.HIGHEST
SLAB = ("chip", "core")
CHIPS = ("chip", "brick")
ALL = ("chip", "core", "brick")


def slot_modes(chunk, i, j):
    if chunk < 8:
        return (chunk - 4, j - 8, i - 4)
    if chunk == 8:
        return (4, j - 8, i - 3)
    if chunk == 9:
        return (i - 3, j - 8, 4)
    return (i - 4, 0, j - 4)


def weight_table(scale):
    where = {}
    for chunk in range(CHUNKS):
        for i in range(8):
            for j in range(8):
                where.setdefault(slot_modes(chunk, i, j), (chunk, i * 8 + j))
    table = np.zeros((CHUNKS, HALF_ROWS), np.float64)
    for k in range(KX * KY * KZ):
        n = (k // (KY * KZ) - KX // 2, k // KZ % KY - KY // 2, k % KZ - KZ // 2)
        squared = float(n[0] ** 2 + n[1] ** 2 + n[2] ** 2)
        if squared == 0.0:
            continue
        slot = where.get(n)
        if slot is None or n[1] > 0:
            slot = where[(-n[0], -n[1], -n[2])]
        table[slot] += math.exp(-squared / 16.0) / squared
    wide = np.ones((CHUNKS * HALF_ROWS, 128), np.float32)
    wide[:, :64] = (table.reshape(-1, 1) * scale).astype(np.float32)
    return wide


def split(value):
    high = value.astype(BF16)
    return high, (value - high.astype(F32)).astype(BF16)


def dot(left, right, contract=((1,), (0,))):
    return lax.dot_general(left, right, (contract, ((), ())), preferred_element_type=F32)


def dot_full(left, right, contract=((1,), (0,))):
    return lax.dot_general(
        left, right, (contract, ((), ())), precision=FULL_PRECISION, preferred_element_type=F32
    )


def sin_turns(turns):
    turns = turns - jnp.floor(turns + 0.5)
    folded = jnp.where(turns > 0.25, 0.5 - turns, jnp.where(turns < -0.25, -0.5 - turns, turns))
    angle = folded * (2.0 * math.pi)
    square = angle * angle
    poly = -1.0 / 39916800.0
    for divisor in (362880.0, -5040.0, 120.0, -6.0):
        poly = poly * square + 1.0 / divisor
    return angle + angle * square * poly


def wave_factors(turns, first):
    order = lax.broadcasted_iota(jnp.int32, (8, turns.shape[1]), 0) + first
    phase = order.astype(F32) * turns
    phase = phase - jnp.floor(phase + 0.5)
    return sin_turns(phase + 0.25), sin_turns(phase)


def complex_product(left, right):
    return (
        left[0] * right[0] - left[1] * right[1],
        left[0] * right[1] + left[1] * right[0],
    )


def chunk_waves(positions):
    one = wave_factors(positions[0:1], -4)
    one_up = wave_factors(positions[0:1], -3)
    two = wave_factors(positions[1:2], -8)
    three = wave_factors(positions[2:3], -4)
    three_up = wave_factors(positions[2:3], -3)

    def row(pair, index):
        return pair[0][index : index + 1], pair[1][index : index + 1]

    def chunk(number):
        if number < 8:
            outer, inner = complex_product(row(one, number), three), two
        elif number == 8:
            outer, inner = complex_product(row(one_up, 7), three_up), two
        elif number == 9:
            outer, inner = complex_product(row(three_up, 7), one_up), two
        else:
            outer, inner = one, three
        cos_part, sin_part = complex_product(
            (outer[0][:, None, :], outer[1][:, None, :]),
            (inner[0][None, :, :], inner[1][None, :, :]),
        )
        atoms = positions.shape[1]
        return jnp.concatenate(
            [cos_part.reshape(HALF_ROWS, atoms), sin_part.reshape(HALF_ROWS, atoms)], axis=0
        )

    return chunk


def live_row(count_ref, atoms):
    index = lax.broadcasted_iota(jnp.int32, (1, atoms), 1)
    return (index < count_ref[0]).astype(F32)


def send_selector(send_map, atoms, transposed=False):
    size = send_map.shape[1]
    spread = (
        lax.broadcasted_iota(jnp.int32, (size, 128), 1) % size
        == lax.broadcasted_iota(jnp.int32, (size, 128), 0)
    ).astype(F32)
    tiled = dot_full(send_map.astype(F32), spread)
    place = lax.broadcasted_iota(jnp.int32, (1, 128), 1) // size
    wanted = jnp.zeros((1, 128), F32)
    for slot, group in enumerate((2, 3, 0, 1, 1, 3, 0, 2)):
        wanted = jnp.where(place == slot, tiled[group : group + 1], wanted)
    atom = lax.broadcasted_iota(jnp.int32, (atoms, 128), 0).astype(F32)
    return (atom == jnp.round(wanted)).astype(F32).astype(BF16)


def pick_lanes(refs):
    place = lax.broadcasted_iota(jnp.int32, (64, 128), 1) // 32
    value = refs[3][...]
    for slot in range(3):
        value = jnp.where(place == slot, refs[slot][...], value)
    return value


def wave_kernel(
    count_ref,
    positions_ref,
    cotangent_ref,
    features_ref,
    table_ref,
    map_ref,
    keep_ref,
    give_ref,
    outgoing_ref,
):
    features = features_ref[...]
    selector = send_selector(map_ref[...], features.shape[1])
    top, rest = split(features)
    middle, bottom = split(features - top.astype(F32))
    outgoing_ref[...] = dot(top, selector) + (dot(middle, selector) + dot(bottom, selector))
    chunk = chunk_waves(positions_ref[...])
    live = live_row(count_ref, positions_ref.shape[1])
    both = jnp.concatenate([cotangent_ref[...] * live, features * live], axis=0)
    high, low = split(both)
    stacked = jnp.concatenate([high, low], axis=0)
    first = lax.axis_index("core") == 0

    def store(unit, value):
        rows = pl.ds(unit % CHUNKS * HALF_ROWS, HALF_ROWS)
        mine = first if unit < CHUNKS else jnp.logical_not(first)

        @pl.when(mine)
        def _():
            keep_ref[rows, :] = value

        @pl.when(jnp.logical_not(mine))
        def _():
            give_ref[rows, :] = value

    for number in range(CHUNKS):
        wave_high, wave_low = split(chunk(number))
        part = dot(wave_high, stacked, ((1,), (1,)))
        part = part[:, :128] + part[:, 128:] + dot(wave_low, high, ((1,), (1,)))
        weight = table_ref[number * HALF_ROWS : (number + 1) * HALF_ROWS, :]
        store(2 * number, part[:HALF_ROWS] * weight)
        store(2 * number + 1, part[HALF_ROWS:] * weight)


def edge_kernel(
    count_ref,
    features_ref,
    up_ref,
    down_ref,
    right_ref,
    left_ref,
    cotangent_ref,
    length_ref,
    neighbor_ref,
    short_ref,
    radial_ref,
    keep_ref,
    taken_ref,
    own_ref,
    ghost_ref,
    payload_ref,
    basis_ref,
    selector_ref,
    gathered_ref,
    weight_ref,
    grads_ref,
    upstream_ref,
    ratio_ref,
    envelope_ref,
    *,
    factor,
):
    channels, atoms = features_ref.shape
    slots = length_ref.shape[0]
    columns = atoms + 128
    group = 4
    wide = group * atoms
    waves = keep_ref.shape[0]
    payload_ref[:waves, :] = keep_ref[...] + taken_ref[...]
    extended = jnp.concatenate(
        [features_ref[...], pick_lanes((up_ref, down_ref, right_ref, left_ref))], axis=1
    )
    projected = jnp.concatenate(split(dot_full(short_ref[...], extended)), axis=0)
    live = live_row(count_ref, atoms)

    lengths = length_ref[...]
    targets = neighbor_ref[...]
    reach = jnp.where(jnp.logical_or(targets >= atoms, targets < count_ref[0]), live, 0.0)
    ratio = lengths * (1.0 / CUTOFF)
    envelope = 1.0 - ratio * ratio
    envelope_ref[...] = math.sqrt(2.0 / CUTOFF) * envelope * envelope / lengths * reach
    ratio_ref[...] = 0.5 * ratio
    order = lax.broadcasted_iota(jnp.int32, (8, atoms), 0).astype(F32) + 1.0

    radial_high, radial_low = split(radial_ref[...])
    radial_wide = jnp.concatenate([radial_high, radial_high, radial_low], axis=0)
    column = lax.broadcasted_iota(jnp.int32, (columns, 128), 0).astype(jnp.int16)
    one, zero = jnp.ones((), BF16), jnp.zeros((), BF16)

    def side_by_side(pieces):
        return jnp.concatenate(pieces, axis=1)

    def basis_of(turn):
        base = turn * group * 8
        return split(
            side_by_side(
                [basis_ref[pl.ds(pl.multiple_of(base + 8 * i, 8), 8), :] for i in range(group)]
            )
        )

    def forward(turn, total):
        tiles = []
        for i in range(group):
            picks = neighbor_ref[pl.ds(turn * group + i, 1), :]
            for lane in range(0, atoms, 128):
                pick = jnp.broadcast_to(picks[:, lane : lane + 128], (16, 128)).astype(jnp.int16)
                pick = jnp.concatenate([pick] * (columns // 16), axis=0)
                tiles.append(jnp.where(column == pick, one, zero))
        selector = side_by_side(tiles)
        selector_ref[turn] = selector
        found = dot(projected, selector)
        gathered = found[:channels] + found[channels:]
        for i in range(group):
            slot = turn * group + i
            basis_ref[pl.ds(pl.multiple_of(slot * 8, 8), 8), :] = (
                sin_turns(order * ratio_ref[pl.ds(slot, 1), :]) * envelope_ref[pl.ds(slot, 1), :]
            )
        basis_high, basis_low = basis_of(turn)
        weight = dot(
            radial_wide, jnp.concatenate([basis_high, basis_low, basis_high], axis=0), ((0,), (0,))
        )
        gathered_ref[turn] = gathered
        weight_ref[turn] = weight
        product = weight * gathered
        for i in range(group):
            total = total + product[:, i * atoms : (i + 1) * atoms]
        return total

    turns = slots // group
    short_sum = lax.fori_loop(0, turns, forward, jnp.zeros((channels, atoms), F32))
    gate = jax.nn.sigmoid(short_sum)
    upstream = cotangent_ref[...] * gate * (1.0 + short_sum * (1.0 - gate)) * live

    grads_ref[...] = jnp.zeros(grads_ref.shape, F32)
    upstream_ref[...] = upstream

    def backward(turn, radial):
        pieces = []
        pulls = []
        for i in range(group):
            lanes = pl.ds(i * atoms, atoms)
            pieces.append(jnp.concatenate(split(weight_ref[turn, :, lanes] * upstream_ref[...]), axis=0))
            pulls.append(jnp.concatenate(split(gathered_ref[turn, :, lanes] * upstream_ref[...]), axis=0))
        grads_ref[...] += dot(selector_ref[turn], side_by_side(pieces), ((1,), (1,)))
        pair = jnp.concatenate(basis_of(turn), axis=0)
        return radial + dot(pair, side_by_side(pulls), ((1,), (1,)))

    radial = lax.fori_loop(0, turns, backward, jnp.zeros((16, 2 * channels), F32)).T
    grads = grads_ref[...].T
    grads = grads[:channels] + grads[channels:]
    radial = radial[:channels] + radial[channels:]
    radial = radial[:, :8] + radial[:, 8:]
    own_ref[...] = grads[:, :atoms]
    ghost_ref[...] = grads[:, atoms:]
    short_part = dot_full(grads, extended, ((1,), (1,))) * factor
    payload_ref[waves:, :] = jnp.concatenate(
        [short_part, radial * factor, jnp.zeros((channels, 128 - channels - 8), F32)], axis=1
    )


def return_kernel(left_ref, right_ref, down_ref, up_ref, own_ref, map_ref, short_ref, out_ref):
    back = pick_lanes((up_ref, down_ref, right_ref, left_ref))
    selector = send_selector(map_ref[...], own_ref.shape[1])
    high, low = split(back)
    owned = own_ref[...] + (
        dot(high, selector, ((1,), (1,))) + dot(low, selector, ((1,), (1,)))
    )
    out_ref[...] = dot_full(short_ref[...], owned, ((0,), (0,)))


def sum_kernel(pieces_ref, out_ref, *, width):
    rows = pieces_ref.shape[0]
    block = 4 * width
    total = jnp.sum(pieces_ref[...].reshape(rows // block, block, 128), axis=0)
    mine = total[:width]
    for step in range(1, 4):
        mine = mine + total[step * width : (step + 1) * width]
    pattern = jnp.concatenate([mine] * 4, axis=0)
    out_ref[...] = jnp.broadcast_to(pattern[None], (rows // block, block, 128)).reshape(rows, 128)


def table_kernel(positions_ref, high_ref, low_ref):
    chunk = chunk_waves(positions_ref[...])
    for number in range(CHUNKS):
        rows = pl.ds(number * 2 * HALF_ROWS, 2 * HALF_ROWS)
        high_ref[rows, :], low_ref[rows, :] = split(chunk(number))


def half_charge(half_ref, high_ref, low_ref, first):
    waves = CHUNKS * HALF_ROWS
    rows = pl.ds(pl.multiple_of(jnp.where(first, 0, waves), HALF_ROWS), waves)
    block = half_ref[:waves, :]
    turned_high, turned_low = split(block.T[:64])
    block_high, block_low = split(block)
    wave_high = high_ref[rows, :]
    turned = jnp.concatenate([turned_high, turned_low], axis=0)
    field = dot(turned, wave_high)
    field = field[:64] + field[64:] + dot(turned_high, low_ref[rows, :])
    grad = dot(turned, block_high)
    grad = grad[:64] + grad[64:] + dot(turned_high, block_low)
    return field, grad


def mine_kernel(mine_ref, high_ref, low_ref, field_ref, grad_ref, small_ref):
    small_ref[...] = mine_ref[CHUNKS * HALF_ROWS :, :]
    first = lax.axis_index("core") == 0
    field_ref[...], grad_ref[...] = half_charge(mine_ref, high_ref, low_ref, first)


def charge_kernel(
    count_ref,
    other_ref,
    high_ref,
    low_ref,
    field_ref,
    sums_ref,
    mine_ref,
    partial_ref,
    charge_ref,
    grad_ref,
    out_ref,
    short_ref,
    radial_ref,
    *,
    factor,
):
    first = lax.axis_index("core") != 0
    waves = CHUNKS * HALF_ROWS
    small = mine_ref[...] + other_ref[waves:, :]
    channels, atoms = partial_ref.shape
    short_ref[...] = small[:, :channels]
    radial_ref[...] = small.T[channels : channels + 8, :]
    field, grad = half_charge(other_ref, high_ref, low_ref, first)
    field = (field + field_ref[...]) * live_row(count_ref, atoms)
    grad = grad + sums_ref[...]
    grad_ref[...] = grad[:, channels : 2 * channels] * factor
    out_ref[...] = partial_ref[...] + dot_full(charge_ref[...], field, ((0,), (0,)))


def vmem(count):
    return [pl.BlockSpec(memory_space=pltpu.VMEM)] * count


def scalar_first(count):
    return [pl.BlockSpec(memory_space=pltpu.SMEM)] + vmem(count)


def work(micros):
    return pl.CostEstimate(
        flops=int(micros * 1e9), transcendentals=0, bytes_accessed=int(micros * 3e6)
    )


def shape(*dims):
    return jax.ShapeDtypeStruct(dims, F32)


def near(*dims):
    return pltpu.VMEM(dims, F32)


def shifted(value, axis, step):
    size = lax.axis_size(axis)
    return lax.ppermute(value, axis, [(i, (i + step) % size) for i in range(size)])


def close(value):
    return pltpu.with_memory_space_constraint(value, pltpu.VMEM)


def swapped(value):
    return lax.ppermute(value, "core", [(0, 1), (1, 0)])


def exchange(value, axes):
    return lax.all_to_all(value, axes, 0, 0, tiled=True)


def on_device(
    features,
    cotangent,
    positions,
    edge_length,
    neighbors,
    send_map,
    atom_count,
    short_weight,
    charge_weight,
    radial_weight,
):
    channels, atoms = features.shape
    slots = neighbors.shape[0]
    devices = lax.axis_size(ALL)
    chips = lax.axis_size(CHIPS)
    factor = 1.0 / math.sqrt(atoms * devices)
    half = CHUNKS * HALF_ROWS
    rows = half + channels
    width = rows // chips * 128

    keep, give, outgoing = pl.pallas_call(
        wave_kernel,
        out_shape=(near(half, 128), near(half, 128), near(channels, 128)),
        in_specs=scalar_first(5),
        out_specs=tuple(vmem(3)),
        cost_estimate=work(4.0),
    )(atom_count, positions, cotangent, features, jnp.asarray(weight_table(factor)), send_map)
    up = shifted(outgoing, SLAB, 1)
    down = shifted(outgoing, SLAB, -1)
    right = shifted(outgoing, "brick", 1)
    left = shifted(outgoing, "brick", -1)
    taken = swapped(give)

    up, down, right, left = (close(x) for x in (up, down, right, left))
    keep, taken = close(keep), close(taken)
    own, ghost, payload = pl.pallas_call(
        functools.partial(edge_kernel, factor=factor),
        out_shape=(near(channels, atoms), near(channels, 128), near(rows, 128)),
        in_specs=scalar_first(12),
        out_specs=tuple(vmem(3)),
        scratch_shapes=[
            pltpu.VMEM((slots * 8, atoms), F32),
            pltpu.VMEM((slots // 4, atoms + 128, 4 * atoms), BF16),
            pltpu.VMEM((slots // 4, channels, 4 * atoms), F32),
            pltpu.VMEM((slots // 4, channels, 4 * atoms), F32),
            pltpu.VMEM((atoms + 128, 2 * channels), F32),
            pltpu.VMEM((channels, atoms), F32),
            pltpu.VMEM((slots, atoms), F32),
            pltpu.VMEM((slots, atoms), F32),
        ],
        cost_estimate=work(10.0),
    )(
        atom_count,
        features,
        up,
        down,
        right,
        left,
        cotangent,
        edge_length,
        neighbors,
        short_weight,
        radial_weight.T,
        keep,
        taken,
    )
    pieces = exchange(payload.reshape(chips, 1, width), CHIPS)
    back_right = shifted(ghost, "brick", 1)
    back_left = shifted(ghost, "brick", -1)
    back_up = shifted(ghost, SLAB, 1)
    back_down = shifted(ghost, SLAB, -1)
    pieces, back_right, back_left = lax.optimization_barrier((pieces, back_right, back_left))
    summed = pl.pallas_call(
        functools.partial(sum_kernel, width=rows // chips),
        out_shape=near(rows, 128),
        in_specs=vmem(1),
        out_specs=vmem(1)[0],
        cost_estimate=work(0.5),
    )(close(pieces.reshape(rows, 128)))
    mine = exchange(summed.reshape(chips, 1, width), CHIPS).reshape(rows, 128)
    back_right, back_left, back_up, back_down = (
        close(x) for x in (back_right, back_left, back_up, back_down)
    )
    partial = pl.pallas_call(
        return_kernel,
        out_shape=near(channels, atoms),
        in_specs=vmem(7),
        out_specs=vmem(1)[0],
        cost_estimate=work(2.0),
    )(back_right, back_left, back_up, back_down, close(own), send_map, short_weight)
    high, low = pl.pallas_call(
        table_kernel,
        out_shape=(pltpu.VMEM((2 * half, atoms), BF16), pltpu.VMEM((2 * half, atoms), BF16)),
        in_specs=vmem(1),
        out_specs=tuple(vmem(2)),
        cost_estimate=work(2.0),
    )(positions)
    mine, partial, high, low = lax.optimization_barrier((mine, partial, high, low))
    high, low = close(high), close(low)
    other = close(swapped(mine))
    field, sums, small = pl.pallas_call(
        mine_kernel,
        out_shape=(near(channels, atoms), near(channels, 128), near(channels, 128)),
        in_specs=vmem(3),
        out_specs=tuple(vmem(3)),
        cost_estimate=work(2.0),
    )(close(mine), high, low)
    charge_grad, feature_grad, short_grad, radial_grad = pl.pallas_call(
        functools.partial(charge_kernel, factor=factor),
        out_shape=(
            shape(channels, channels),
            shape(channels, atoms),
            shape(channels, channels),
            shape(radial_weight.shape[1], channels),
        ),
        in_specs=scalar_first(8),
        out_specs=tuple(vmem(4)),
        cost_estimate=work(3.0),
    )(
        atom_count,
        other,
        high,
        low,
        close(field),
        close(sums),
        close(small),
        close(partial),
        charge_weight,
    )
    return feature_grad, short_grad, charge_grad, radial_grad.T


def solution(mesh):
    slabs, bricks = mesh.devices.shape
    fine = Mesh(mesh.devices.reshape(slabs // 2, 2, bricks), ALL)
    split_all = P(None, ALL)
    placed = (split_all,) * 6 + (P(ALL), P(), P(), P())
    return jax.shard_map(
        on_device,
        mesh=fine,
        in_specs=placed,
        out_specs=(split_all, P(), P(), P()),
        check_vma=False,
    )
```

```python
import functools
import math

import jax
import jax.numpy as jnp
import numpy as np
from jax import lax
from jax.experimental import pallas as pl
from jax.experimental.pallas import tpu as pltpu
from jax.sharding import Mesh
from jax.sharding import PartitionSpec as P

KX = 8
KY = 16
KZ = 8
CUTOFF = 6.0
HALF_ROWS = 64
CHUNKS = 11
F32 = jnp.float32
BF16 = jnp.bfloat16
FULL_PRECISION = lax.Precision.HIGHEST
SLAB = ("chip", "core")
CHIPS = ("chip", "brick")
ALL = ("chip", "core", "brick")


def slot_modes(chunk, i, j):
    if chunk < 8:
        return (chunk - 4, j - 8, i - 4)
    if chunk == 8:
        return (4, j - 8, i - 3)
    if chunk == 9:
        return (i - 3, j - 8, 4)
    return (i - 4, 0, j - 4)


def weight_table(scale):
    where = {}
    for chunk in range(CHUNKS):
        for i in range(8):
            for j in range(8):
                where.setdefault(slot_modes(chunk, i, j), (chunk, i * 8 + j))
    table = np.zeros((CHUNKS, HALF_ROWS), np.float64)
    for k in range(KX * KY * KZ):
        n = (k // (KY * KZ) - KX // 2, k // KZ % KY - KY // 2, k % KZ - KZ // 2)
        squared = float(n[0] ** 2 + n[1] ** 2 + n[2] ** 2)
        if squared == 0.0:
            continue
        slot = where.get(n)
        if slot is None or n[1] > 0:
            slot = where[(-n[0], -n[1], -n[2])]
        table[slot] += math.exp(-squared / 16.0) / squared
    wide = np.ones((CHUNKS * HALF_ROWS, 128), np.float32)
    wide[:, :64] = (table.reshape(-1, 1) * scale).astype(np.float32)
    return wide


def split(value):
    high = value.astype(BF16)
    return high, (value - high.astype(F32)).astype(BF16)


def dot(left, right, contract=((1,), (0,))):
    return lax.dot_general(left, right, (contract, ((), ())), preferred_element_type=F32)


def dot_full(left, right, contract=((1,), (0,))):
    return lax.dot_general(
        left, right, (contract, ((), ())), precision=FULL_PRECISION, preferred_element_type=F32
    )


def sin_turns(turns):
    turns = turns - jnp.floor(turns + 0.5)
    folded = jnp.where(turns > 0.25, 0.5 - turns, jnp.where(turns < -0.25, -0.5 - turns, turns))
    angle = folded * (2.0 * math.pi)
    square = angle * angle
    poly = -1.0 / 39916800.0
    for divisor in (362880.0, -5040.0, 120.0, -6.0):
        poly = poly * square + 1.0 / divisor
    return angle + angle * square * poly


def wave_factors(turns, first):
    order = lax.broadcasted_iota(jnp.int32, (8, turns.shape[1]), 0) + first
    phase = order.astype(F32) * turns
    phase = phase - jnp.floor(phase + 0.5)
    return sin_turns(phase + 0.25), sin_turns(phase)


def complex_product(left, right):
    return (
        left[0] * right[0] - left[1] * right[1],
        left[0] * right[1] + left[1] * right[0],
    )


def chunk_waves(positions):
    one = wave_factors(positions[0:1], -4)
    one_up = wave_factors(positions[0:1], -3)
    two = wave_factors(positions[1:2], -8)
    three = wave_factors(positions[2:3], -4)
    three_up = wave_factors(positions[2:3], -3)

    def row(pair, index):
        return pair[0][index : index + 1], pair[1][index : index + 1]

    def chunk(number):
        if number < 8:
            outer, inner = complex_product(row(one, number), three), two
        elif number == 8:
            outer, inner = complex_product(row(one_up, 7), three_up), two
        elif number == 9:
            outer, inner = complex_product(row(three_up, 7), one_up), two
        else:
            outer, inner = one, three
        cos_part, sin_part = complex_product(
            (outer[0][:, None, :], outer[1][:, None, :]),
            (inner[0][None, :, :], inner[1][None, :, :]),
        )
        atoms = positions.shape[1]
        return jnp.concatenate(
            [cos_part.reshape(HALF_ROWS, atoms), sin_part.reshape(HALF_ROWS, atoms)], axis=0
        )

    return chunk


def live_row(count_ref, atoms):
    index = lax.broadcasted_iota(jnp.int32, (1, atoms), 1)
    return (index < count_ref[0]).astype(F32)


def send_selector(send_map, atoms, transposed=False):
    size = send_map.shape[1]
    spread = (
        lax.broadcasted_iota(jnp.int32, (size, 128), 1) % size
        == lax.broadcasted_iota(jnp.int32, (size, 128), 0)
    ).astype(F32)
    tiled = dot_full(send_map.astype(F32), spread)
    place = lax.broadcasted_iota(jnp.int32, (1, 128), 1) // size
    wanted = jnp.zeros((1, 128), F32)
    for slot, group in enumerate((2, 3, 0, 1, 1, 3, 0, 2)):
        wanted = jnp.where(place == slot, tiled[group : group + 1], wanted)
    atom = lax.broadcasted_iota(jnp.int32, (atoms, 128), 0).astype(F32)
    return (atom == jnp.round(wanted)).astype(F32).astype(BF16)


def pick_lanes(refs):
    place = lax.broadcasted_iota(jnp.int32, (64, 128), 1) // 32
    value = refs[3][...]
    for slot in range(3):
        value = jnp.where(place == slot, refs[slot][...], value)
    return value


def wave_kernel(
    count_ref,
    positions_ref,
    cotangent_ref,
    features_ref,
    table_ref,
    map_ref,
    keep_ref,
    give_ref,
    outgoing_ref,
    parts_ref,
):
    features = features_ref[...]
    selector = send_selector(map_ref[...], features.shape[1])
    top, rest = split(features)
    middle, bottom = split(features - top.astype(F32))
    outgoing_ref[...] = dot(top, selector) + (dot(middle, selector) + dot(bottom, selector))
    chunk = chunk_waves(positions_ref[...])
    live = live_row(count_ref, positions_ref.shape[1])
    both = jnp.concatenate([cotangent_ref[...] * live, features * live], axis=0)
    high, low = split(both)
    stacked = jnp.concatenate([high, low], axis=0)
    for number in range(CHUNKS):
        wave_high, wave_low = split(chunk(number))
        part = dot(wave_high, stacked, ((1,), (1,)))
        part = part[:, :128] + part[:, 128:] + dot(wave_low, high, ((1,), (1,)))
        weight = table_ref[number * HALF_ROWS : (number + 1) * HALF_ROWS, :]
        base = number * 2 * HALF_ROWS
        parts_ref[base : base + HALF_ROWS, :] = part[:HALF_ROWS] * weight
        parts_ref[base + HALF_ROWS : base + 2 * HALF_ROWS, :] = part[HALF_ROWS:] * weight
    half = keep_ref.shape[0]
    first = lax.axis_index("core") == 0
    lower, upper = parts_ref[:half, :], parts_ref[half:, :]
    keep_ref[...] = jnp.where(first, lower, upper)
    give_ref[...] = jnp.where(first, upper, lower)


def edge_kernel(
    count_ref,
    features_ref,
    up_ref,
    down_ref,
    right_ref,
    left_ref,
    cotangent_ref,
    length_ref,
    neighbor_ref,
    short_ref,
    radial_ref,
    keep_ref,
    taken_ref,
    own_ref,
    ghost_ref,
    payload_ref,
    basis_ref,
    selector_ref,
    gathered_ref,
    weight_ref,
    grads_ref,
    upstream_ref,
    ratio_ref,
    envelope_ref,
    *,
    factor,
):
    channels, atoms = features_ref.shape
    slots = length_ref.shape[0]
    columns = atoms + 128
    group = 4
    wide = group * atoms
    waves = keep_ref.shape[0]
    payload_ref[:waves, :] = keep_ref[...] + taken_ref[...]
    extended = jnp.concatenate(
        [features_ref[...], pick_lanes((up_ref, down_ref, right_ref, left_ref))], axis=1
    )
    projected = jnp.concatenate(split(dot_full(short_ref[...], extended)), axis=0)
    live = live_row(count_ref, atoms)

    lengths = length_ref[...]
    targets = neighbor_ref[...]
    reach = jnp.where(jnp.logical_or(targets >= atoms, targets < count_ref[0]), live, 0.0)
    ratio = lengths * (1.0 / CUTOFF)
    envelope = 1.0 - ratio * ratio
    envelope_ref[...] = math.sqrt(2.0 / CUTOFF) * envelope * envelope / lengths * reach
    ratio_ref[...] = 0.5 * ratio
    order = lax.broadcasted_iota(jnp.int32, (8, atoms), 0).astype(F32) + 1.0

    radial_high, radial_low = split(radial_ref[...])
    radial_wide = jnp.concatenate([radial_high, radial_high, radial_low], axis=0)
    column = lax.broadcasted_iota(jnp.int32, (columns, 128), 0).astype(jnp.int16)
    one, zero = jnp.ones((), BF16), jnp.zeros((), BF16)

    def side_by_side(pieces):
        return jnp.concatenate(pieces, axis=1)

    def basis_of(turn):
        base = turn * group * 8
        return split(
            side_by_side(
                [basis_ref[pl.ds(pl.multiple_of(base + 8 * i, 8), 8), :] for i in range(group)]
            )
        )

    def forward(turn, total):
        tiles = []
        for i in range(group):
            picks = neighbor_ref[pl.ds(turn * group + i, 1), :]
            for lane in range(0, atoms, 128):
                pick = jnp.broadcast_to(picks[:, lane : lane + 128], (16, 128)).astype(jnp.int16)
                pick = jnp.concatenate([pick] * (columns // 16), axis=0)
                tiles.append(jnp.where(column == pick, one, zero))
        selector = side_by_side(tiles)
        selector_ref[turn] = selector
        found = dot(projected, selector)
        gathered = found[:channels] + found[channels:]
        for i in range(group):
            slot = turn * group + i
            basis_ref[pl.ds(pl.multiple_of(slot * 8, 8), 8), :] = (
                sin_turns(order * ratio_ref[pl.ds(slot, 1), :]) * envelope_ref[pl.ds(slot, 1), :]
            )
        basis_high, basis_low = basis_of(turn)
        weight = dot(
            radial_wide, jnp.concatenate([basis_high, basis_low, basis_high], axis=0), ((0,), (0,))
        )
        gathered_ref[turn] = gathered
        weight_ref[turn] = weight
        product = weight * gathered
        for i in range(group):
            total = total + product[:, i * atoms : (i + 1) * atoms]
        return total

    turns = slots // group
    short_sum = lax.fori_loop(
        0, turns, forward, jnp.zeros((channels, atoms), F32), unroll=8
    )
    gate = jax.nn.sigmoid(short_sum)
    upstream = cotangent_ref[...] * gate * (1.0 + short_sum * (1.0 - gate)) * live

    grads_ref[...] = jnp.zeros(grads_ref.shape, F32)
    upstream_ref[...] = upstream

    def backward(turn, radial):
        pieces = []
        pulls = []
        for i in range(group):
            lanes = pl.ds(i * atoms, atoms)
            pieces.append(jnp.concatenate(split(weight_ref[turn, :, lanes] * upstream_ref[...]), axis=0))
            pulls.append(jnp.concatenate(split(gathered_ref[turn, :, lanes] * upstream_ref[...]), axis=0))
        grads_ref[...] += dot(selector_ref[turn], side_by_side(pieces), ((1,), (1,)))
        pair = jnp.concatenate(basis_of(turn), axis=0)
        return radial + dot(pair, side_by_side(pulls), ((1,), (1,)))

    radial = lax.fori_loop(
        0, turns, backward, jnp.zeros((16, 2 * channels), F32), unroll=8
    ).T
    grads = grads_ref[...].T
    grads = grads[:channels] + grads[channels:]
    radial = radial[:channels] + radial[channels:]
    radial = radial[:, :8] + radial[:, 8:]
    own_ref[...] = grads[:, :atoms]
    ghost_ref[...] = grads[:, atoms:]
    short_part = dot_full(grads, extended, ((1,), (1,))) * factor
    payload_ref[waves:, :] = jnp.concatenate(
        [short_part, radial * factor, jnp.zeros((channels, 128 - channels - 8), F32)], axis=1
    )


def return_kernel(left_ref, right_ref, down_ref, up_ref, own_ref, map_ref, short_ref, out_ref):
    back = pick_lanes((up_ref, down_ref, right_ref, left_ref))
    selector = send_selector(map_ref[...], own_ref.shape[1])
    high, low = split(back)
    owned = own_ref[...] + (
        dot(high, selector, ((1,), (1,))) + dot(low, selector, ((1,), (1,)))
    )
    out_ref[...] = dot_full(short_ref[...], owned, ((0,), (0,)))


def sum_kernel(pieces_ref, out_ref, *, width):
    rows = pieces_ref.shape[0]
    block = 4 * width
    total = jnp.sum(pieces_ref[...].reshape(rows // block, block, 128), axis=0)
    mine = total[:width]
    for step in range(1, 4):
        mine = mine + total[step * width : (step + 1) * width]
    pattern = jnp.concatenate([mine] * 4, axis=0)
    out_ref[...] = jnp.broadcast_to(pattern[None], (rows // block, block, 128)).reshape(rows, 128)


def table_kernel(positions_ref, high_ref, low_ref):
    chunk = chunk_waves(positions_ref[...])
    for number in range(CHUNKS):
        rows = pl.ds(number * 2 * HALF_ROWS, 2 * HALF_ROWS)
        high_ref[rows, :], low_ref[rows, :] = split(chunk(number))


def half_charge(half_ref, high_ref, low_ref, first):
    waves = CHUNKS * HALF_ROWS
    rows = pl.ds(pl.multiple_of(jnp.where(first, 0, waves), HALF_ROWS), waves)
    block = half_ref[:waves, :]
    turned_high, turned_low = split(block.T[:64])
    block_high, block_low = split(block)
    wave_high = high_ref[rows, :]
    turned = jnp.concatenate([turned_high, turned_low], axis=0)
    field = dot(turned, wave_high)
    field = field[:64] + field[64:] + dot(turned_high, low_ref[rows, :])
    grad = dot(turned, block_high)
    grad = grad[:64] + grad[64:] + dot(turned_high, block_low)
    return field, grad


def mine_kernel(mine_ref, high_ref, low_ref, field_ref, grad_ref, small_ref):
    small_ref[...] = mine_ref[CHUNKS * HALF_ROWS :, :]
    first = lax.axis_index("core") == 0
    field_ref[...], grad_ref[...] = half_charge(mine_ref, high_ref, low_ref, first)


def charge_kernel(
    count_ref,
    other_ref,
    high_ref,
    low_ref,
    field_ref,
    sums_ref,
    mine_ref,
    partial_ref,
    charge_ref,
    grad_ref,
    out_ref,
    short_ref,
    radial_ref,
    *,
    factor,
):
    first = lax.axis_index("core") != 0
    waves = CHUNKS * HALF_ROWS
    small = mine_ref[...] + other_ref[waves:, :]
    channels, atoms = partial_ref.shape
    short_ref[...] = small[:, :channels]
    radial_ref[...] = small.T[channels : channels + 8, :]
    field, grad = half_charge(other_ref, high_ref, low_ref, first)
    field = (field + field_ref[...]) * live_row(count_ref, atoms)
    grad = grad + sums_ref[...]
    grad_ref[...] = grad[:, channels : 2 * channels] * factor
    out_ref[...] = partial_ref[...] + dot_full(charge_ref[...], field, ((0,), (0,)))


def vmem(count):
    return [pl.BlockSpec(memory_space=pltpu.VMEM)] * count


def scalar_first(count):
    return [pl.BlockSpec(memory_space=pltpu.SMEM)] + vmem(count)


def work(micros):
    return pl.CostEstimate(
        flops=int(micros * 1e9), transcendentals=0, bytes_accessed=int(micros * 3e6)
    )


def shape(*dims):
    return jax.ShapeDtypeStruct(dims, F32)


def near(*dims):
    return pltpu.VMEM(dims, F32)


def shifted(value, axis, step):
    size = lax.axis_size(axis)
    return lax.ppermute(value, axis, [(i, (i + step) % size) for i in range(size)])


def close(value):
    return pltpu.with_memory_space_constraint(value, pltpu.VMEM)


def swapped(value):
    return lax.ppermute(value, "core", [(0, 1), (1, 0)])


def exchange(value, axes):
    return lax.all_to_all(value, axes, 0, 0, tiled=True)


def on_device(
    features,
    cotangent,
    positions,
    edge_length,
    neighbors,
    send_map,
    atom_count,
    short_weight,
    charge_weight,
    radial_weight,
):
    channels, atoms = features.shape
    slots = neighbors.shape[0]
    devices = lax.axis_size(ALL)
    chips = lax.axis_size(CHIPS)
    factor = 1.0 / math.sqrt(atoms * devices)
    half = CHUNKS * HALF_ROWS
    rows = half + channels
    width = rows // chips * 128

    keep, give, outgoing = pl.pallas_call(
        wave_kernel,
        out_shape=(near(half, 128), near(half, 128), near(channels, 128)),
        in_specs=scalar_first(5),
        out_specs=tuple(vmem(3)),
        scratch_shapes=[pltpu.VMEM((2 * half, 128), F32)],
        cost_estimate=work(4.0),
    )(atom_count, positions, cotangent, features, jnp.asarray(weight_table(factor)), send_map)
    up = shifted(outgoing, SLAB, 1)
    down = shifted(outgoing, SLAB, -1)
    right = shifted(outgoing, "brick", 1)
    left = shifted(outgoing, "brick", -1)
    taken = swapped(give)

    up, down, right, left = (close(x) for x in (up, down, right, left))
    keep, taken = close(keep), close(taken)
    own, ghost, payload = pl.pallas_call(
        functools.partial(edge_kernel, factor=factor),
        out_shape=(near(channels, atoms), near(channels, 128), near(rows, 128)),
        in_specs=scalar_first(12),
        out_specs=tuple(vmem(3)),
        scratch_shapes=[
            pltpu.VMEM((slots * 8, atoms), F32),
            pltpu.VMEM((slots // 4, atoms + 128, 4 * atoms), BF16),
            pltpu.VMEM((slots // 4, channels, 4 * atoms), F32),
            pltpu.VMEM((slots // 4, channels, 4 * atoms), F32),
            pltpu.VMEM((atoms + 128, 2 * channels), F32),
            pltpu.VMEM((channels, atoms), F32),
            pltpu.VMEM((slots, atoms), F32),
            pltpu.VMEM((slots, atoms), F32),
        ],
        cost_estimate=work(10.0),
    )(
        atom_count,
        features,
        up,
        down,
        right,
        left,
        cotangent,
        edge_length,
        neighbors,
        short_weight,
        radial_weight.T,
        keep,
        taken,
    )
    pieces = exchange(payload.reshape(chips, 1, width), CHIPS)
    back_right = shifted(ghost, "brick", 1)
    back_left = shifted(ghost, "brick", -1)
    back_up = shifted(ghost, SLAB, 1)
    back_down = shifted(ghost, SLAB, -1)
    pieces, back_right, back_left = lax.optimization_barrier((pieces, back_right, back_left))
    summed = pl.pallas_call(
        functools.partial(sum_kernel, width=rows // chips),
        out_shape=near(rows, 128),
        in_specs=vmem(1),
        out_specs=vmem(1)[0],
        cost_estimate=work(0.5),
    )(close(pieces.reshape(rows, 128)))
    mine = exchange(summed.reshape(chips, 1, width), CHIPS).reshape(rows, 128)
    back_right, back_left, back_up, back_down = (
        close(x) for x in (back_right, back_left, back_up, back_down)
    )
    partial = pl.pallas_call(
        return_kernel,
        out_shape=near(channels, atoms),
        in_specs=vmem(7),
        out_specs=vmem(1)[0],
        cost_estimate=work(2.0),
    )(back_right, back_left, back_up, back_down, close(own), send_map, short_weight)
    high, low = pl.pallas_call(
        table_kernel,
        out_shape=(pltpu.VMEM((2 * half, atoms), BF16), pltpu.VMEM((2 * half, atoms), BF16)),
        in_specs=vmem(1),
        out_specs=tuple(vmem(2)),
        cost_estimate=work(2.0),
    )(positions)
    mine, partial, high, low = lax.optimization_barrier((mine, partial, high, low))
    high, low = close(high), close(low)
    other = close(swapped(mine))
    field, sums, small = pl.pallas_call(
        mine_kernel,
        out_shape=(near(channels, atoms), near(channels, 128), near(channels, 128)),
        in_specs=vmem(3),
        out_specs=tuple(vmem(3)),
        cost_estimate=work(2.0),
    )(close(mine), high, low)
    charge_grad, feature_grad, short_grad, radial_grad = pl.pallas_call(
        functools.partial(charge_kernel, factor=factor),
        out_shape=(
            shape(channels, channels),
            shape(channels, atoms),
            shape(channels, channels),
            shape(radial_weight.shape[1], channels),
        ),
        in_specs=scalar_first(8),
        out_specs=tuple(vmem(4)),
        cost_estimate=work(3.0),
    )(
        atom_count,
        other,
        high,
        low,
        close(field),
        close(sums),
        close(small),
        close(partial),
        charge_weight,
    )
    return feature_grad, short_grad, charge_grad, radial_grad.T


def solution(mesh):
    slabs, bricks = mesh.devices.shape
    fine = Mesh(mesh.devices.reshape(slabs // 2, 2, bricks), ALL)
    split_all = P(None, ALL)
    placed = (split_all,) * 6 + (P(ALL), P(), P(), P())
    return jax.shard_map(
        on_device,
        mesh=fine,
        in_specs=placed,
        out_specs=(split_all, P(), P(), P()),
        check_vma=False,
    )
```

```python
import functools
import math

import jax
import jax.numpy as jnp
import numpy as np
from jax import lax
from jax.experimental import pallas as pl
from jax.experimental.pallas import tpu as pltpu
from jax.sharding import Mesh
from jax.sharding import PartitionSpec as P

KX = 8
KY = 16
KZ = 8
CUTOFF = 6.0
HALF_ROWS = 64
CHUNKS = 11
F32 = jnp.float32
BF16 = jnp.bfloat16
FULL_PRECISION = lax.Precision.HIGHEST
SLAB = ("chip", "core")
CHIPS = ("chip", "brick")
ALL = ("chip", "core", "brick")


def slot_modes(chunk, i, j):
    if chunk < 8:
        return (chunk - 4, j - 8, i - 4)
    if chunk == 8:
        return (4, j - 8, i - 3)
    if chunk == 9:
        return (i - 3, j - 8, 4)
    return (i - 4, 0, j - 4)


def weight_table(scale):
    where = {}
    for chunk in range(CHUNKS):
        for i in range(8):
            for j in range(8):
                where.setdefault(slot_modes(chunk, i, j), (chunk, i * 8 + j))
    table = np.zeros((CHUNKS, HALF_ROWS), np.float64)
    for k in range(KX * KY * KZ):
        n = (k // (KY * KZ) - KX // 2, k // KZ % KY - KY // 2, k % KZ - KZ // 2)
        squared = float(n[0] ** 2 + n[1] ** 2 + n[2] ** 2)
        if squared == 0.0:
            continue
        slot = where.get(n)
        if slot is None or n[1] > 0:
            slot = where[(-n[0], -n[1], -n[2])]
        table[slot] += math.exp(-squared / 16.0) / squared
    wide = np.ones((CHUNKS * HALF_ROWS, 128), np.float32)
    wide[:, :64] = (table.reshape(-1, 1) * scale).astype(np.float32)
    return wide


def split(value):
    high = value.astype(BF16)
    return high, (value - high.astype(F32)).astype(BF16)


def dot(left, right, contract=((1,), (0,))):
    return lax.dot_general(left, right, (contract, ((), ())), preferred_element_type=F32)


def dot_full(left, right, contract=((1,), (0,))):
    return lax.dot_general(
        left, right, (contract, ((), ())), precision=FULL_PRECISION, preferred_element_type=F32
    )


def sin_turns(turns):
    turns = turns - jnp.floor(turns + 0.5)
    folded = jnp.where(turns > 0.25, 0.5 - turns, jnp.where(turns < -0.25, -0.5 - turns, turns))
    angle = folded * (2.0 * math.pi)
    square = angle * angle
    poly = -1.0 / 39916800.0
    for divisor in (362880.0, -5040.0, 120.0, -6.0):
        poly = poly * square + 1.0 / divisor
    return angle + angle * square * poly


def wave_factors(turns, first):
    order = lax.broadcasted_iota(jnp.int32, (8, turns.shape[1]), 0) + first
    phase = order.astype(F32) * turns
    phase = phase - jnp.floor(phase + 0.5)
    return sin_turns(phase + 0.25), sin_turns(phase)


def complex_product(left, right):
    return (
        left[0] * right[0] - left[1] * right[1],
        left[0] * right[1] + left[1] * right[0],
    )


def chunk_waves(positions):
    one = wave_factors(positions[0:1], -4)
    one_up = wave_factors(positions[0:1], -3)
    two = wave_factors(positions[1:2], -8)
    three = wave_factors(positions[2:3], -4)
    three_up = wave_factors(positions[2:3], -3)

    def row(pair, index):
        return pair[0][index : index + 1], pair[1][index : index + 1]

    def chunk(number):
        if number < 8:
            outer, inner = complex_product(row(one, number), three), two
        elif number == 8:
            outer, inner = complex_product(row(one_up, 7), three_up), two
        elif number == 9:
            outer, inner = complex_product(row(three_up, 7), one_up), two
        else:
            outer, inner = one, three
        cos_part, sin_part = complex_product(
            (outer[0][:, None, :], outer[1][:, None, :]),
            (inner[0][None, :, :], inner[1][None, :, :]),
        )
        atoms = positions.shape[1]
        return jnp.concatenate(
            [cos_part.reshape(HALF_ROWS, atoms), sin_part.reshape(HALF_ROWS, atoms)], axis=0
        )

    return chunk


def live_row(count_ref, atoms):
    index = lax.broadcasted_iota(jnp.int32, (1, atoms), 1)
    return (index < count_ref[0]).astype(F32)


def send_selector(send_map, atoms, transposed=False):
    size = send_map.shape[1]
    spread = (
        lax.broadcasted_iota(jnp.int32, (size, 128), 1) % size
        == lax.broadcasted_iota(jnp.int32, (size, 128), 0)
    ).astype(F32)
    tiled = dot_full(send_map.astype(F32), spread)
    place = lax.broadcasted_iota(jnp.int32, (1, 128), 1) // size
    wanted = jnp.zeros((1, 128), F32)
    for slot, group in enumerate((2, 3, 0, 1, 1, 3, 0, 2)):
        wanted = jnp.where(place == slot, tiled[group : group + 1], wanted)
    atom = lax.broadcasted_iota(jnp.int32, (atoms, 128), 0).astype(F32)
    return (atom == jnp.round(wanted)).astype(F32).astype(BF16)


def pick_lanes(refs):
    place = lax.broadcasted_iota(jnp.int32, (64, 128), 1) // 32
    value = refs[3][...]
    for slot in range(3):
        value = jnp.where(place == slot, refs[slot][...], value)
    return value


def wave_kernel(
    count_ref,
    positions_ref,
    cotangent_ref,
    features_ref,
    table_ref,
    map_ref,
    keep_ref,
    give_ref,
    outgoing_ref,
    parts_ref,
):
    features = features_ref[...]
    selector = send_selector(map_ref[...], features.shape[1])
    top, rest = split(features)
    middle, bottom = split(features - top.astype(F32))
    outgoing_ref[...] = dot(top, selector) + (dot(middle, selector) + dot(bottom, selector))
    chunk = chunk_waves(positions_ref[...])
    live = live_row(count_ref, positions_ref.shape[1])
    both = jnp.concatenate([cotangent_ref[...] * live, features * live], axis=0)
    high, low = split(both)
    stacked = jnp.concatenate([high, low], axis=0)
    for number in range(CHUNKS):
        wave_high, wave_low = split(chunk(number))
        part = dot(wave_high, stacked, ((1,), (1,)))
        part = part[:, :128] + part[:, 128:] + dot(wave_low, high, ((1,), (1,)))
        weight = table_ref[number * HALF_ROWS : (number + 1) * HALF_ROWS, :]
        base = number * 2 * HALF_ROWS
        parts_ref[base : base + HALF_ROWS, :] = part[:HALF_ROWS] * weight
        parts_ref[base + HALF_ROWS : base + 2 * HALF_ROWS, :] = part[HALF_ROWS:] * weight
    half = keep_ref.shape[0]
    first = lax.axis_index("core") == 0
    lower, upper = parts_ref[:half, :], parts_ref[half:, :]
    keep_ref[...] = jnp.where(first, lower, upper)
    give_ref[...] = jnp.where(first, upper, lower)


def edge_kernel(
    count_ref,
    features_ref,
    up_ref,
    down_ref,
    right_ref,
    left_ref,
    cotangent_ref,
    length_ref,
    neighbor_ref,
    short_ref,
    radial_ref,
    keep_ref,
    taken_ref,
    own_ref,
    ghost_ref,
    payload_ref,
    basis_ref,
    selector_ref,
    gathered_ref,
    weight_ref,
    grads_ref,
    upstream_ref,
    ratio_ref,
    envelope_ref,
    *,
    factor,
):
    channels, atoms = features_ref.shape
    slots = length_ref.shape[0]
    columns = atoms + 128
    group = 4
    wide = group * atoms
    waves = keep_ref.shape[0]
    payload_ref[:waves, :] = keep_ref[...] + taken_ref[...]
    extended = jnp.concatenate(
        [features_ref[...], pick_lanes((up_ref, down_ref, right_ref, left_ref))], axis=1
    )
    projected = jnp.concatenate(split(dot_full(short_ref[...], extended)), axis=0)
    live = live_row(count_ref, atoms)

    lengths = length_ref[...]
    targets = neighbor_ref[...]
    reach = jnp.where(jnp.logical_or(targets >= atoms, targets < count_ref[0]), live, 0.0)
    ratio = lengths * (1.0 / CUTOFF)
    envelope = 1.0 - ratio * ratio
    envelope_ref[...] = math.sqrt(2.0 / CUTOFF) * envelope * envelope / lengths * reach
    ratio_ref[...] = 0.5 * ratio
    order = lax.broadcasted_iota(jnp.int32, (8, atoms), 0).astype(F32) + 1.0

    radial_high, radial_low = split(radial_ref[...])
    radial_wide = jnp.concatenate([radial_high, radial_high, radial_low], axis=0)
    column = lax.broadcasted_iota(jnp.int32, (columns, 128), 0).astype(jnp.int16)
    one, zero = jnp.ones((), BF16), jnp.zeros((), BF16)

    def side_by_side(pieces):
        return jnp.concatenate(pieces, axis=1)

    def basis_of(turn):
        base = turn * group * 8
        return split(
            side_by_side(
                [basis_ref[pl.ds(pl.multiple_of(base + 8 * i, 8), 8), :] for i in range(group)]
            )
        )

    def forward(turn, total):
        tiles = []
        for i in range(group):
            picks = neighbor_ref[pl.ds(turn * group + i, 1), :]
            for lane in range(0, atoms, 128):
                pick = jnp.broadcast_to(picks[:, lane : lane + 128], (16, 128)).astype(jnp.int16)
                pick = jnp.concatenate([pick] * (columns // 16), axis=0)
                tiles.append(jnp.where(column == pick, one, zero))
        selector = side_by_side(tiles)
        selector_ref[turn] = selector
        found = dot(projected, selector)
        gathered = found[:channels] + found[channels:]
        for i in range(group):
            slot = turn * group + i
            basis_ref[pl.ds(pl.multiple_of(slot * 8, 8), 8), :] = (
                sin_turns(order * ratio_ref[pl.ds(slot, 1), :]) * envelope_ref[pl.ds(slot, 1), :]
            )
        basis_high, basis_low = basis_of(turn)
        weight = dot(
            radial_wide, jnp.concatenate([basis_high, basis_low, basis_high], axis=0), ((0,), (0,))
        )
        gathered_ref[turn] = gathered
        weight_ref[turn] = weight
        product = weight * gathered
        for i in range(group):
            total = total + product[:, i * atoms : (i + 1) * atoms]
        return total

    turns = slots // group
    short_sum = lax.fori_loop(
        0, turns, forward, jnp.zeros((channels, atoms), F32), unroll=8
    )
    gate = jax.nn.sigmoid(short_sum)
    upstream = cotangent_ref[...] * gate * (1.0 + short_sum * (1.0 - gate)) * live

    grads_ref[...] = jnp.zeros(grads_ref.shape, F32)
    upstream_ref[...] = upstream

    def backward(turn, radial):
        pieces = []
        pulls = []
        for i in range(group):
            lanes = pl.ds(i * atoms, atoms)
            pieces.append(jnp.concatenate(split(weight_ref[turn, :, lanes] * upstream_ref[...]), axis=0))
            pulls.append(jnp.concatenate(split(gathered_ref[turn, :, lanes] * upstream_ref[...]), axis=0))
        grads_ref[...] += dot(selector_ref[turn], side_by_side(pieces), ((1,), (1,)))
        pair = jnp.concatenate(basis_of(turn), axis=0)
        return radial + dot(pair, side_by_side(pulls), ((1,), (1,)))

    radial = lax.fori_loop(
        0, turns, backward, jnp.zeros((16, 2 * channels), F32), unroll=8
    ).T
    grads = grads_ref[...].T
    grads = grads[:channels] + grads[channels:]
    radial = radial[:channels] + radial[channels:]
    radial = radial[:, :8] + radial[:, 8:]
    own_ref[...] = grads[:, :atoms]
    ghost_ref[...] = grads[:, atoms:]
    short_part = dot_full(grads, extended, ((1,), (1,))) * factor
    payload_ref[waves:, :] = jnp.concatenate(
        [short_part, radial * factor, jnp.zeros((channels, 128 - channels - 8), F32)], axis=1
    )


def return_kernel(left_ref, right_ref, down_ref, up_ref, own_ref, map_ref, short_ref, out_ref):
    back = pick_lanes((up_ref, down_ref, right_ref, left_ref))
    selector = send_selector(map_ref[...], own_ref.shape[1])
    high, low = split(back)
    owned = own_ref[...] + (
        dot(high, selector, ((1,), (1,))) + dot(low, selector, ((1,), (1,)))
    )
    out_ref[...] = dot_full(short_ref[...], owned, ((0,), (0,)))


def sum_kernel(pieces_ref, out_ref, *, width):
    rows = pieces_ref.shape[0]
    block = 4 * width
    total = jnp.sum(pieces_ref[...].reshape(rows // block, block, 128), axis=0)
    mine = total[:width]
    for step in range(1, 4):
        mine = mine + total[step * width : (step + 1) * width]
    pattern = jnp.concatenate([mine] * 4, axis=0)
    out_ref[...] = jnp.broadcast_to(pattern[None], (rows // block, block, 128)).reshape(rows, 128)


def table_kernel(positions_ref, high_ref, low_ref):
    chunk = chunk_waves(positions_ref[...])
    for number in range(CHUNKS):
        rows = pl.ds(number * 2 * HALF_ROWS, 2 * HALF_ROWS)
        high_ref[rows, :], low_ref[rows, :] = split(chunk(number))


def half_charge(half_ref, high_ref, low_ref, first):
    waves = CHUNKS * HALF_ROWS
    rows = pl.ds(pl.multiple_of(jnp.where(first, 0, waves), HALF_ROWS), waves)
    block = half_ref[:waves, :]
    turned_high, turned_low = split(block.T[:64])
    block_high, block_low = split(block)
    wave_high = high_ref[rows, :]
    turned = jnp.concatenate([turned_high, turned_low], axis=0)
    field = dot(turned, wave_high)
    field = field[:64] + field[64:] + dot(turned_high, low_ref[rows, :])
    grad = dot(turned, block_high)
    grad = grad[:64] + grad[64:] + dot(turned_high, block_low)
    return field, grad


def mine_kernel(mine_ref, high_ref, low_ref, field_ref, grad_ref, small_ref):
    small_ref[...] = mine_ref[CHUNKS * HALF_ROWS :, :]
    first = lax.axis_index("core") == 0
    field_ref[...], grad_ref[...] = half_charge(mine_ref, high_ref, low_ref, first)


def charge_kernel(
    count_ref,
    other_ref,
    high_ref,
    low_ref,
    field_ref,
    sums_ref,
    mine_ref,
    partial_ref,
    charge_ref,
    grad_ref,
    out_ref,
    short_ref,
    radial_ref,
    *,
    factor,
):
    first = lax.axis_index("core") != 0
    waves = CHUNKS * HALF_ROWS
    small = mine_ref[...] + other_ref[waves:, :]
    channels, atoms = partial_ref.shape
    short_ref[...] = small[:, :channels]
    radial_ref[...] = small.T[channels : channels + 8, :]
    field, grad = half_charge(other_ref, high_ref, low_ref, first)
    field = (field + field_ref[...]) * live_row(count_ref, atoms)
    grad = grad + sums_ref[...]
    grad_ref[...] = grad[:, channels : 2 * channels] * factor
    out_ref[...] = partial_ref[...] + dot_full(charge_ref[...], field, ((0,), (0,)))


def vmem(count):
    return [pl.BlockSpec(memory_space=pltpu.VMEM)] * count


def scalar_first(count):
    return [pl.BlockSpec(memory_space=pltpu.SMEM)] + vmem(count)


def work(micros):
    return pl.CostEstimate(
        flops=int(micros * 1e9), transcendentals=0, bytes_accessed=int(micros * 3e6)
    )


def shape(*dims):
    return jax.ShapeDtypeStruct(dims, F32)


def near(*dims):
    return pltpu.VMEM(dims, F32)


def shifted(value, axis, step):
    size = lax.axis_size(axis)
    return lax.ppermute(value, axis, [(i, (i + step) % size) for i in range(size)])


def close(value):
    return pltpu.with_memory_space_constraint(value, pltpu.VMEM)


def swapped(value):
    return lax.ppermute(value, "core", [(0, 1), (1, 0)])


def exchange(value, axes):
    return lax.all_to_all(value, axes, 0, 0, tiled=True)


def on_device(
    features,
    cotangent,
    positions,
    edge_length,
    neighbors,
    send_map,
    atom_count,
    short_weight,
    charge_weight,
    radial_weight,
):
    channels, atoms = features.shape
    slots = neighbors.shape[0]
    devices = lax.axis_size(ALL)
    chips = lax.axis_size(CHIPS)
    factor = 1.0 / math.sqrt(atoms * devices)
    half = CHUNKS * HALF_ROWS
    rows = half + channels
    width = rows // chips * 128

    keep, give, outgoing = pl.pallas_call(
        wave_kernel,
        out_shape=(near(half, 128), near(half, 128), near(channels, 128)),
        in_specs=scalar_first(5),
        out_specs=tuple(vmem(3)),
        scratch_shapes=[pltpu.VMEM((2 * half, 128), F32)],
        cost_estimate=work(4.0),
    )(atom_count, positions, cotangent, features, jnp.asarray(weight_table(factor)), send_map)
    up = shifted(outgoing, SLAB, 1)
    down = shifted(outgoing, SLAB, -1)
    right = shifted(outgoing, "brick", 1)
    left = shifted(outgoing, "brick", -1)
    taken = swapped(give)

    up, down, right, left = (close(x) for x in (up, down, right, left))
    keep, taken = close(keep), close(taken)
    own, ghost, payload = pl.pallas_call(
        functools.partial(edge_kernel, factor=factor),
        out_shape=(near(channels, atoms), near(channels, 128), near(rows, 128)),
        in_specs=scalar_first(12),
        out_specs=tuple(vmem(3)),
        scratch_shapes=[
            pltpu.VMEM((slots * 8, atoms), F32),
            pltpu.VMEM((slots // 4, atoms + 128, 4 * atoms), BF16),
            pltpu.VMEM((slots // 4, channels, 4 * atoms), F32),
            pltpu.VMEM((slots // 4, channels, 4 * atoms), F32),
            pltpu.VMEM((atoms + 128, 2 * channels), F32),
            pltpu.VMEM((channels, atoms), F32),
            pltpu.VMEM((slots, atoms), F32),
            pltpu.VMEM((slots, atoms), F32),
        ],
        cost_estimate=work(10.0),
    )(
        atom_count,
        features,
        up,
        down,
        right,
        left,
        cotangent,
        edge_length,
        neighbors,
        short_weight,
        radial_weight.T,
        keep,
        taken,
    )
    pieces = exchange(payload.reshape(chips, 1, width), CHIPS)
    back_right = shifted(ghost, "brick", 1)
    back_left = shifted(ghost, "brick", -1)
    back_up = shifted(ghost, SLAB, 1)
    back_down = shifted(ghost, SLAB, -1)
    summed = pl.pallas_call(
        functools.partial(sum_kernel, width=rows // chips),
        out_shape=near(rows, 128),
        in_specs=vmem(1),
        out_specs=vmem(1)[0],
        cost_estimate=work(0.5),
    )(close(pieces.reshape(rows, 128)))
    mine = exchange(summed.reshape(chips, 1, width), CHIPS).reshape(rows, 128)
    back_right, back_left, back_up, back_down = (
        close(x) for x in (back_right, back_left, back_up, back_down)
    )
    partial = pl.pallas_call(
        return_kernel,
        out_shape=near(channels, atoms),
        in_specs=vmem(7),
        out_specs=vmem(1)[0],
        cost_estimate=work(2.0),
    )(back_right, back_left, back_up, back_down, close(own), send_map, short_weight)
    high, low = pl.pallas_call(
        table_kernel,
        out_shape=(pltpu.VMEM((2 * half, atoms), BF16), pltpu.VMEM((2 * half, atoms), BF16)),
        in_specs=vmem(1),
        out_specs=tuple(vmem(2)),
        cost_estimate=work(2.0),
    )(positions)
    mine, partial, high, low = lax.optimization_barrier((mine, partial, high, low))
    high, low = close(high), close(low)
    other = close(swapped(mine))
    field, sums, small = pl.pallas_call(
        mine_kernel,
        out_shape=(near(channels, atoms), near(channels, 128), near(channels, 128)),
        in_specs=vmem(3),
        out_specs=tuple(vmem(3)),
        cost_estimate=work(2.0),
    )(close(mine), high, low)
    charge_grad, feature_grad, short_grad, radial_grad = pl.pallas_call(
        functools.partial(charge_kernel, factor=factor),
        out_shape=(
            shape(channels, channels),
            shape(channels, atoms),
            shape(channels, channels),
            shape(radial_weight.shape[1], channels),
        ),
        in_specs=scalar_first(8),
        out_specs=tuple(vmem(4)),
        cost_estimate=work(3.0),
    )(
        atom_count,
        other,
        high,
        low,
        close(field),
        close(sums),
        close(small),
        close(partial),
        charge_weight,
    )
    return feature_grad, short_grad, charge_grad, radial_grad.T


def solution(mesh):
    slabs, bricks = mesh.devices.shape
    fine = Mesh(mesh.devices.reshape(slabs // 2, 2, bricks), ALL)
    split_all = P(None, ALL)
    placed = (split_all,) * 6 + (P(ALL), P(), P(), P())
    return jax.shard_map(
        on_device,
        mesh=fine,
        in_specs=placed,
        out_specs=(split_all, P(), P(), P()),
        check_vma=False,
    )
```

```python
import functools
import math

import jax
import jax.numpy as jnp
import numpy as np
from jax import lax
from jax.experimental import pallas as pl
from jax.experimental.pallas import tpu as pltpu
from jax.sharding import Mesh
from jax.sharding import PartitionSpec as P

KX = 8
KY = 16
KZ = 8
CUTOFF = 6.0
HALF_ROWS = 64
CHUNKS = 11
F32 = jnp.float32
BF16 = jnp.bfloat16
FULL_PRECISION = lax.Precision.HIGHEST
SLAB = ("chip", "core")
CHIPS = ("chip", "brick")
ALL = ("chip", "core", "brick")


def slot_modes(chunk, i, j):
    if chunk < 8:
        return (chunk - 4, j - 8, i - 4)
    if chunk == 8:
        return (4, j - 8, i - 3)
    if chunk == 9:
        return (i - 3, j - 8, 4)
    return (i - 4, 0, j - 4)


def weight_table(scale):
    where = {}
    for chunk in range(CHUNKS):
        for i in range(8):
            for j in range(8):
                where.setdefault(slot_modes(chunk, i, j), (chunk, i * 8 + j))
    table = np.zeros((CHUNKS, HALF_ROWS), np.float64)
    for k in range(KX * KY * KZ):
        n = (k // (KY * KZ) - KX // 2, k // KZ % KY - KY // 2, k % KZ - KZ // 2)
        squared = float(n[0] ** 2 + n[1] ** 2 + n[2] ** 2)
        if squared == 0.0:
            continue
        slot = where.get(n)
        if slot is None or n[1] > 0:
            slot = where[(-n[0], -n[1], -n[2])]
        table[slot] += math.exp(-squared / 16.0) / squared
    wide = np.ones((CHUNKS * HALF_ROWS, 128), np.float32)
    wide[:, :64] = (table.reshape(-1, 1) * scale).astype(np.float32)
    return wide


def split(value):
    high = value.astype(BF16)
    return high, (value - high.astype(F32)).astype(BF16)


def dot(left, right, contract=((1,), (0,))):
    return lax.dot_general(left, right, (contract, ((), ())), preferred_element_type=F32)


def dot_full(left, right, contract=((1,), (0,))):
    return lax.dot_general(
        left, right, (contract, ((), ())), precision=FULL_PRECISION, preferred_element_type=F32
    )


def sin_turns(turns):
    turns = turns - jnp.floor(turns + 0.5)
    folded = jnp.where(turns > 0.25, 0.5 - turns, jnp.where(turns < -0.25, -0.5 - turns, turns))
    angle = folded * (2.0 * math.pi)
    square = angle * angle
    poly = -1.0 / 39916800.0
    for divisor in (362880.0, -5040.0, 120.0, -6.0):
        poly = poly * square + 1.0 / divisor
    return angle + angle * square * poly


def wave_factors(turns, first):
    order = lax.broadcasted_iota(jnp.int32, (8, turns.shape[1]), 0) + first
    phase = order.astype(F32) * turns
    phase = phase - jnp.floor(phase + 0.5)
    return sin_turns(phase + 0.25), sin_turns(phase)


def complex_product(left, right):
    return (
        left[0] * right[0] - left[1] * right[1],
        left[0] * right[1] + left[1] * right[0],
    )


def chunk_waves(positions):
    one = wave_factors(positions[0:1], -4)
    one_up = wave_factors(positions[0:1], -3)
    two = wave_factors(positions[1:2], -8)
    three = wave_factors(positions[2:3], -4)
    three_up = wave_factors(positions[2:3], -3)

    def row(pair, index):
        return pair[0][index : index + 1], pair[1][index : index + 1]

    def chunk(number):
        if number < 8:
            outer, inner = complex_product(row(one, number), three), two
        elif number == 8:
            outer, inner = complex_product(row(one_up, 7), three_up), two
        elif number == 9:
            outer, inner = complex_product(row(three_up, 7), one_up), two
        else:
            outer, inner = one, three
        cos_part, sin_part = complex_product(
            (outer[0][:, None, :], outer[1][:, None, :]),
            (inner[0][None, :, :], inner[1][None, :, :]),
        )
        atoms = positions.shape[1]
        return jnp.concatenate(
            [cos_part.reshape(HALF_ROWS, atoms), sin_part.reshape(HALF_ROWS, atoms)], axis=0
        )

    return chunk


def live_row(count_ref, atoms):
    index = lax.broadcasted_iota(jnp.int32, (1, atoms), 1)
    return (index < count_ref[0]).astype(F32)


def send_selector(send_map, atoms, transposed=False):
    size = send_map.shape[1]
    spread = (
        lax.broadcasted_iota(jnp.int32, (size, 128), 1) % size
        == lax.broadcasted_iota(jnp.int32, (size, 128), 0)
    ).astype(F32)
    tiled = dot_full(send_map.astype(F32), spread)
    place = lax.broadcasted_iota(jnp.int32, (1, 128), 1) // size
    wanted = jnp.zeros((1, 128), F32)
    for slot, group in enumerate((2, 3, 0, 1, 1, 3, 0, 2)):
        wanted = jnp.where(place == slot, tiled[group : group + 1], wanted)
    atom = lax.broadcasted_iota(jnp.int32, (atoms, 128), 0).astype(F32)
    return (atom == jnp.round(wanted)).astype(F32).astype(BF16)


def packed(value, place):
    lanes = slice(32 * place, 32 * place + 32)
    return jnp.concatenate([value[16 * q : 16 * q + 16, lanes] for q in range(4)], axis=1)


def unpacked(refs):
    values = [ref[...] for ref in refs]
    return jnp.concatenate(
        [
            jnp.concatenate([value[:, 32 * q : 32 * q + 32] for value in values], axis=1)
            for q in range(4)
        ],
        axis=0,
    )


def wave_kernel(
    count_ref,
    positions_ref,
    cotangent_ref,
    features_ref,
    table_ref,
    map_ref,
    keep_ref,
    give_ref,
    up_ref,
    down_ref,
    right_ref,
    left_ref,
    parts_ref,
):
    features = features_ref[...]
    selector = send_selector(map_ref[...], features.shape[1])
    top, rest = split(features)
    middle, bottom = split(features - top.astype(F32))
    outgoing = dot(top, selector) + (dot(middle, selector) + dot(bottom, selector))
    for place, ref in enumerate((up_ref, down_ref, right_ref, left_ref)):
        ref[...] = packed(outgoing, place)
    chunk = chunk_waves(positions_ref[...])
    live = live_row(count_ref, positions_ref.shape[1])
    both = jnp.concatenate([cotangent_ref[...] * live, features * live], axis=0)
    high, low = split(both)
    stacked = jnp.concatenate([high, low], axis=0)
    for number in range(CHUNKS):
        wave_high, wave_low = split(chunk(number))
        part = dot(wave_high, stacked, ((1,), (1,)))
        part = part[:, :128] + part[:, 128:] + dot(wave_low, high, ((1,), (1,)))
        weight = table_ref[number * HALF_ROWS : (number + 1) * HALF_ROWS, :]
        base = number * 2 * HALF_ROWS
        parts_ref[base : base + HALF_ROWS, :] = part[:HALF_ROWS] * weight
        parts_ref[base + HALF_ROWS : base + 2 * HALF_ROWS, :] = part[HALF_ROWS:] * weight
    half = keep_ref.shape[0]
    first = lax.axis_index("core") == 0
    lower, upper = parts_ref[:half, :], parts_ref[half:, :]
    keep_ref[...] = jnp.where(first, lower, upper)
    give_ref[...] = jnp.where(first, upper, lower)


def edge_kernel(
    count_ref,
    features_ref,
    up_ref,
    down_ref,
    right_ref,
    left_ref,
    cotangent_ref,
    length_ref,
    neighbor_ref,
    short_ref,
    radial_ref,
    keep_ref,
    taken_ref,
    own_ref,
    ghost_up_ref,
    ghost_down_ref,
    ghost_right_ref,
    ghost_left_ref,
    payload_ref,
    basis_ref,
    selector_ref,
    gathered_ref,
    weight_ref,
    grads_ref,
    upstream_ref,
    ratio_ref,
    envelope_ref,
    *,
    factor,
):
    channels, atoms = features_ref.shape
    slots = length_ref.shape[0]
    columns = atoms + 128
    group = 4
    wide = group * atoms
    waves = keep_ref.shape[0]
    payload_ref[:waves, :] = keep_ref[...] + taken_ref[...]
    extended = jnp.concatenate(
        [features_ref[...], unpacked((up_ref, down_ref, right_ref, left_ref))], axis=1
    )
    projected = jnp.concatenate(split(dot_full(short_ref[...], extended)), axis=0)
    live = live_row(count_ref, atoms)

    lengths = length_ref[...]
    targets = neighbor_ref[...]
    reach = jnp.where(jnp.logical_or(targets >= atoms, targets < count_ref[0]), live, 0.0)
    ratio = lengths * (1.0 / CUTOFF)
    envelope = 1.0 - ratio * ratio
    envelope_ref[...] = math.sqrt(2.0 / CUTOFF) * envelope * envelope / lengths * reach
    ratio_ref[...] = 0.5 * ratio
    order = lax.broadcasted_iota(jnp.int32, (8, atoms), 0).astype(F32) + 1.0

    radial_high, radial_low = split(radial_ref[...])
    radial_wide = jnp.concatenate([radial_high, radial_high, radial_low], axis=0)
    column = lax.broadcasted_iota(jnp.int32, (columns, 128), 0).astype(jnp.int16)
    one, zero = jnp.ones((), BF16), jnp.zeros((), BF16)

    def side_by_side(pieces):
        return jnp.concatenate(pieces, axis=1)

    def basis_of(turn):
        base = turn * group * 8
        return split(
            side_by_side(
                [basis_ref[pl.ds(pl.multiple_of(base + 8 * i, 8), 8), :] for i in range(group)]
            )
        )

    def forward(turn, total):
        tiles = []
        for i in range(group):
            picks = neighbor_ref[pl.ds(turn * group + i, 1), :]
            for lane in range(0, atoms, 128):
                pick = jnp.broadcast_to(picks[:, lane : lane + 128], (16, 128)).astype(jnp.int16)
                pick = jnp.concatenate([pick] * (columns // 16), axis=0)
                tiles.append(jnp.where(column == pick, one, zero))
        selector = side_by_side(tiles)
        selector_ref[turn] = selector
        found = dot(projected, selector)
        gathered = found[:channels] + found[channels:]
        for i in range(group):
            slot = turn * group + i
            basis_ref[pl.ds(pl.multiple_of(slot * 8, 8), 8), :] = (
                sin_turns(order * ratio_ref[pl.ds(slot, 1), :]) * envelope_ref[pl.ds(slot, 1), :]
            )
        basis_high, basis_low = basis_of(turn)
        weight = dot(
            radial_wide, jnp.concatenate([basis_high, basis_low, basis_high], axis=0), ((0,), (0,))
        )
        gathered_ref[turn] = gathered
        weight_ref[turn] = weight
        product = weight * gathered
        for i in range(group):
            total = total + product[:, i * atoms : (i + 1) * atoms]
        return total

    turns = slots // group
    short_sum = lax.fori_loop(
        0, turns, forward, jnp.zeros((channels, atoms), F32), unroll=8
    )
    gate = jax.nn.sigmoid(short_sum)
    upstream = cotangent_ref[...] * gate * (1.0 + short_sum * (1.0 - gate)) * live

    grads_ref[...] = jnp.zeros(grads_ref.shape, F32)
    upstream_ref[...] = upstream

    def backward(turn, radial):
        pieces = []
        pulls = []
        for i in range(group):
            lanes = pl.ds(i * atoms, atoms)
            pieces.append(jnp.concatenate(split(weight_ref[turn, :, lanes] * upstream_ref[...]), axis=0))
            pulls.append(jnp.concatenate(split(gathered_ref[turn, :, lanes] * upstream_ref[...]), axis=0))
        grads_ref[...] += dot(selector_ref[turn], side_by_side(pieces), ((1,), (1,)))
        pair = jnp.concatenate(basis_of(turn), axis=0)
        return radial + dot(pair, side_by_side(pulls), ((1,), (1,)))

    radial = lax.fori_loop(
        0, turns, backward, jnp.zeros((16, 2 * channels), F32), unroll=8
    ).T
    grads = grads_ref[...].T
    grads = grads[:channels] + grads[channels:]
    radial = radial[:channels] + radial[channels:]
    radial = radial[:, :8] + radial[:, 8:]
    own_ref[...] = grads[:, :atoms]
    for place, ref in enumerate((ghost_up_ref, ghost_down_ref, ghost_right_ref, ghost_left_ref)):
        ref[...] = packed(grads[:, atoms:], place)
    short_part = dot_full(grads, extended, ((1,), (1,))) * factor
    payload_ref[waves:, :] = jnp.concatenate(
        [short_part, radial * factor, jnp.zeros((channels, 128 - channels - 8), F32)], axis=1
    )


def return_kernel(left_ref, right_ref, down_ref, up_ref, own_ref, map_ref, short_ref, out_ref):
    back = unpacked((up_ref, down_ref, right_ref, left_ref))
    selector = send_selector(map_ref[...], own_ref.shape[1])
    high, low = split(back)
    owned = own_ref[...] + (
        dot(high, selector, ((1,), (1,))) + dot(low, selector, ((1,), (1,)))
    )
    out_ref[...] = dot_full(short_ref[...], owned, ((0,), (0,)))


def sum_kernel(pieces_ref, out_ref, *, width):
    rows = pieces_ref.shape[0]
    block = 4 * width
    total = jnp.sum(pieces_ref[...].reshape(rows // block, block, 128), axis=0)
    mine = total[:width]
    for step in range(1, 4):
        mine = mine + total[step * width : (step + 1) * width]
    pattern = jnp.concatenate([mine] * 4, axis=0)
    out_ref[...] = jnp.broadcast_to(pattern[None], (rows // block, block, 128)).reshape(rows, 128)


def table_kernel(positions_ref, high_ref, low_ref):
    chunk = chunk_waves(positions_ref[...])
    for number in range(CHUNKS):
        rows = pl.ds(number * 2 * HALF_ROWS, 2 * HALF_ROWS)
        high_ref[rows, :], low_ref[rows, :] = split(chunk(number))


def half_charge(half_ref, high_ref, low_ref, first):
    waves = CHUNKS * HALF_ROWS
    rows = pl.ds(pl.multiple_of(jnp.where(first, 0, waves), HALF_ROWS), waves)
    block = half_ref[:waves, :]
    turned_high, turned_low = split(block.T[:64])
    block_high, block_low = split(block)
    wave_high = high_ref[rows, :]
    turned = jnp.concatenate([turned_high, turned_low], axis=0)
    field = dot(turned, wave_high)
    field = field[:64] + field[64:] + dot(turned_high, low_ref[rows, :])
    grad = dot(turned, block_high)
    grad = grad[:64] + grad[64:] + dot(turned_high, block_low)
    return field, grad


def mine_kernel(mine_ref, high_ref, low_ref, field_ref, grad_ref, small_ref):
    small_ref[...] = mine_ref[CHUNKS * HALF_ROWS :, :]
    first = lax.axis_index("core") == 0
    field_ref[...], grad_ref[...] = half_charge(mine_ref, high_ref, low_ref, first)


def charge_kernel(
    count_ref,
    other_ref,
    high_ref,
    low_ref,
    field_ref,
    sums_ref,
    mine_ref,
    partial_ref,
    charge_ref,
    grad_ref,
    out_ref,
    short_ref,
    radial_ref,
    *,
    factor,
):
    first = lax.axis_index("core") != 0
    waves = CHUNKS * HALF_ROWS
    small = mine_ref[...] + other_ref[waves:, :]
    channels, atoms = partial_ref.shape
    short_ref[...] = small[:, :channels]
    radial_ref[...] = small.T[channels : channels + 8, :]
    field, grad = half_charge(other_ref, high_ref, low_ref, first)
    field = (field + field_ref[...]) * live_row(count_ref, atoms)
    grad = grad + sums_ref[...]
    grad_ref[...] = grad[:, channels : 2 * channels] * factor
    out_ref[...] = partial_ref[...] + dot_full(charge_ref[...], field, ((0,), (0,)))


def vmem(count):
    return [pl.BlockSpec(memory_space=pltpu.VMEM)] * count


def scalar_first(count):
    return [pl.BlockSpec(memory_space=pltpu.SMEM)] + vmem(count)


def work(micros):
    return pl.CostEstimate(
        flops=int(micros * 1e9), transcendentals=0, bytes_accessed=int(micros * 3e6)
    )


def shape(*dims):
    return jax.ShapeDtypeStruct(dims, F32)


def near(*dims):
    return pltpu.VMEM(dims, F32)


def shifted(value, axis, step):
    size = lax.axis_size(axis)
    return lax.ppermute(value, axis, [(i, (i + step) % size) for i in range(size)])


def close(value):
    return pltpu.with_memory_space_constraint(value, pltpu.VMEM)


def swapped(value):
    return lax.ppermute(value, "core", [(0, 1), (1, 0)])


def exchange(value, axes):
    return lax.all_to_all(value, axes, 0, 0, tiled=True)


def on_device(
    features,
    cotangent,
    positions,
    edge_length,
    neighbors,
    send_map,
    atom_count,
    short_weight,
    charge_weight,
    radial_weight,
):
    channels, atoms = features.shape
    slots = neighbors.shape[0]
    devices = lax.axis_size(ALL)
    chips = lax.axis_size(CHIPS)
    factor = 1.0 / math.sqrt(atoms * devices)
    half = CHUNKS * HALF_ROWS
    rows = half + channels
    width = rows // chips * 128

    message = near(channels // 4, 128)
    keep, give, *outgoing = pl.pallas_call(
        wave_kernel,
        out_shape=(near(half, 128), near(half, 128)) + (message,) * 4,
        in_specs=scalar_first(5),
        out_specs=tuple(vmem(6)),
        scratch_shapes=[pltpu.VMEM((2 * half, 128), F32)],
        cost_estimate=work(4.0),
    )(atom_count, positions, cotangent, features, jnp.asarray(weight_table(factor)), send_map)
    up = shifted(outgoing[0], SLAB, 1)
    down = shifted(outgoing[1], SLAB, -1)
    right = shifted(outgoing[2], "brick", 1)
    left = shifted(outgoing[3], "brick", -1)
    taken = swapped(give)

    up, down, right, left = (close(x) for x in (up, down, right, left))
    keep, taken = close(keep), close(taken)
    own, *ghost, payload = pl.pallas_call(
        functools.partial(edge_kernel, factor=factor),
        out_shape=(near(channels, atoms),) + (message,) * 4 + (near(rows, 128),),
        in_specs=scalar_first(12),
        out_specs=tuple(vmem(6)),
        scratch_shapes=[
            pltpu.VMEM((slots * 8, atoms), F32),
            pltpu.VMEM((slots // 4, atoms + 128, 4 * atoms), BF16),
            pltpu.VMEM((slots // 4, channels, 4 * atoms), F32),
            pltpu.VMEM((slots // 4, channels, 4 * atoms), F32),
            pltpu.VMEM((atoms + 128, 2 * channels), F32),
            pltpu.VMEM((channels, atoms), F32),
            pltpu.VMEM((slots, atoms), F32),
            pltpu.VMEM((slots, atoms), F32),
        ],
        cost_estimate=work(10.0),
    )(
        atom_count,
        features,
        up,
        down,
        right,
        left,
        cotangent,
        edge_length,
        neighbors,
        short_weight,
        radial_weight.T,
        keep,
        taken,
    )
    pieces = exchange(payload.reshape(chips, 1, width), CHIPS)
    back_right = shifted(ghost[3], "brick", 1)
    back_left = shifted(ghost[2], "brick", -1)
    back_up = shifted(ghost[1], SLAB, 1)
    back_down = shifted(ghost[0], SLAB, -1)
    summed = pl.pallas_call(
        functools.partial(sum_kernel, width=rows // chips),
        out_shape=near(rows, 128),
        in_specs=vmem(1),
        out_specs=vmem(1)[0],
        cost_estimate=work(0.5),
    )(close(pieces.reshape(rows, 128)))
    mine = exchange(summed.reshape(chips, 1, width), CHIPS).reshape(rows, 128)
    back_right, back_left, back_up, back_down = (
        close(x) for x in (back_right, back_left, back_up, back_down)
    )
    partial = pl.pallas_call(
        return_kernel,
        out_shape=near(channels, atoms),
        in_specs=vmem(7),
        out_specs=vmem(1)[0],
        cost_estimate=work(2.0),
    )(back_right, back_left, back_up, back_down, close(own), send_map, short_weight)
    high, low = pl.pallas_call(
        table_kernel,
        out_shape=(pltpu.VMEM((2 * half, atoms), BF16), pltpu.VMEM((2 * half, atoms), BF16)),
        in_specs=vmem(1),
        out_specs=tuple(vmem(2)),
        cost_estimate=work(2.0),
    )(positions)
    mine, partial, high, low = lax.optimization_barrier((mine, partial, high, low))
    high, low = close(high), close(low)
    other = close(swapped(mine))
    field, sums, small = pl.pallas_call(
        mine_kernel,
        out_shape=(near(channels, atoms), near(channels, 128), near(channels, 128)),
        in_specs=vmem(3),
        out_specs=tuple(vmem(3)),
        cost_estimate=work(2.0),
    )(close(mine), high, low)
    charge_grad, feature_grad, short_grad, radial_grad = pl.pallas_call(
        functools.partial(charge_kernel, factor=factor),
        out_shape=(
            shape(channels, channels),
            shape(channels, atoms),
            shape(channels, channels),
            shape(radial_weight.shape[1], channels),
        ),
        in_specs=scalar_first(8),
        out_specs=tuple(vmem(4)),
        cost_estimate=work(3.0),
    )(
        atom_count,
        other,
        high,
        low,
        close(field),
        close(sums),
        close(small),
        close(partial),
        charge_weight,
    )
    return feature_grad, short_grad, charge_grad, radial_grad.T


def solution(mesh):
    slabs, bricks = mesh.devices.shape
    fine = Mesh(mesh.devices.reshape(slabs // 2, 2, bricks), ALL)
    split_all = P(None, ALL)
    placed = (split_all,) * 6 + (P(ALL), P(), P(), P())
    return jax.shard_map(
        on_device,
        mesh=fine,
        in_specs=placed,
        out_specs=(split_all, P(), P(), P()),
        check_vma=False,
    )
```

```python
import functools
import math

import jax
import jax.numpy as jnp
import numpy as np
from jax import lax
from jax.experimental import pallas as pl
from jax.experimental.pallas import tpu as pltpu
from jax.sharding import Mesh
from jax.sharding import PartitionSpec as P

KX = 8
KY = 16
KZ = 8
CUTOFF = 6.0
HALF_ROWS = 64
CHUNKS = 11
F32 = jnp.float32
BF16 = jnp.bfloat16
SLAB = ("chip", "core")
CHIPS = ("chip", "brick")
ALL = ("chip", "core", "brick")


def slot_modes(chunk, i, j):
    if chunk < 8:
        return (chunk - 4, j - 8, i - 4)
    if chunk == 8:
        return (4, j - 8, i - 3)
    if chunk == 9:
        return (i - 3, j - 8, 4)
    return (i - 4, 0, j - 4)


def weight_table(scale):
    where = {}
    for chunk in range(CHUNKS):
        for i in range(8):
            for j in range(8):
                where.setdefault(slot_modes(chunk, i, j), (chunk, i * 8 + j))
    table = np.zeros((CHUNKS, HALF_ROWS), np.float64)
    for k in range(KX * KY * KZ):
        n = (k // (KY * KZ) - KX // 2, k // KZ % KY - KY // 2, k % KZ - KZ // 2)
        squared = float(n[0] ** 2 + n[1] ** 2 + n[2] ** 2)
        if squared == 0.0:
            continue
        slot = where.get(n)
        if slot is None or n[1] > 0:
            slot = where[(-n[0], -n[1], -n[2])]
        table[slot] += math.exp(-squared / 16.0) / squared
    wide = np.ones((CHUNKS * HALF_ROWS, 128), np.float32)
    wide[:, :64] = (table.reshape(-1, 1) * scale).astype(np.float32)
    return wide


def split(value):
    high = value.astype(BF16)
    return high, (value - high.astype(F32)).astype(BF16)


def dot(left, right, contract=((1,), (0,))):
    return lax.dot_general(left, right, (contract, ((), ())), preferred_element_type=F32)


def dot_full(left, right, contract=((1,), (0,))):
    left_high, left_low = split(left)
    right_high, right_low = split(right)
    return dot(left_high, right_high, contract) + (
        dot(left_high, right_low, contract) + dot(left_low, right_high, contract)
    )


def sin_turns(turns):
    turns = turns - jnp.floor(turns + 0.5)
    folded = jnp.where(turns > 0.25, 0.5 - turns, jnp.where(turns < -0.25, -0.5 - turns, turns))
    angle = folded * (2.0 * math.pi)
    square = angle * angle
    poly = -1.0 / 39916800.0
    for divisor in (362880.0, -5040.0, 120.0, -6.0):
        poly = poly * square + 1.0 / divisor
    return angle + angle * square * poly


def wave_factors(turns, first):
    order = lax.broadcasted_iota(jnp.int32, (8, turns.shape[1]), 0) + first
    phase = order.astype(F32) * turns
    phase = phase - jnp.floor(phase + 0.5)
    return sin_turns(phase + 0.25), sin_turns(phase)


def complex_product(left, right):
    return (
        left[0] * right[0] - left[1] * right[1],
        left[0] * right[1] + left[1] * right[0],
    )


def chunk_waves(positions):
    one = wave_factors(positions[0:1], -4)
    one_up = wave_factors(positions[0:1], -3)
    two = wave_factors(positions[1:2], -8)
    three = wave_factors(positions[2:3], -4)
    three_up = wave_factors(positions[2:3], -3)

    def row(pair, index):
        return pair[0][index : index + 1], pair[1][index : index + 1]

    def chunk(number):
        if number < 8:
            outer, inner = complex_product(row(one, number), three), two
        elif number == 8:
            outer, inner = complex_product(row(one_up, 7), three_up), two
        elif number == 9:
            outer, inner = complex_product(row(three_up, 7), one_up), two
        else:
            outer, inner = one, three
        cos_part, sin_part = complex_product(
            (outer[0][:, None, :], outer[1][:, None, :]),
            (inner[0][None, :, :], inner[1][None, :, :]),
        )
        atoms = positions.shape[1]
        return jnp.concatenate(
            [cos_part.reshape(HALF_ROWS, atoms), sin_part.reshape(HALF_ROWS, atoms)], axis=0
        )

    return chunk


def live_row(count_ref, atoms):
    index = lax.broadcasted_iota(jnp.int32, (1, atoms), 1)
    return (index < count_ref[0]).astype(F32)


def send_selector(send_map, atoms, transposed=False):
    size = send_map.shape[1]
    spread = (
        lax.broadcasted_iota(jnp.int32, (size, 128), 1) % size
        == lax.broadcasted_iota(jnp.int32, (size, 128), 0)
    ).astype(F32)
    tiled = dot_full(send_map.astype(F32), spread)
    place = lax.broadcasted_iota(jnp.int32, (1, 128), 1) // size
    wanted = jnp.zeros((1, 128), F32)
    for slot, group in enumerate((2, 3, 0, 1, 1, 3, 0, 2)):
        wanted = jnp.where(place == slot, tiled[group : group + 1], wanted)
    atom = lax.broadcasted_iota(jnp.int32, (atoms, 128), 0).astype(F32)
    return (atom == jnp.round(wanted)).astype(F32).astype(BF16)


def packed(value, place):
    lanes = slice(32 * place, 32 * place + 32)
    return jnp.concatenate([value[16 * q : 16 * q + 16, lanes] for q in range(4)], axis=1)


def unpacked(refs):
    values = [ref[...] for ref in refs]
    return jnp.concatenate(
        [
            jnp.concatenate([value[:, 32 * q : 32 * q + 32] for value in values], axis=1)
            for q in range(4)
        ],
        axis=0,
    )


def wave_kernel(
    count_ref,
    positions_ref,
    cotangent_ref,
    features_ref,
    table_ref,
    map_ref,
    keep_ref,
    give_ref,
    up_ref,
    down_ref,
    right_ref,
    left_ref,
    parts_ref,
):
    features = features_ref[...]
    selector = send_selector(map_ref[...], features.shape[1])
    top, rest = split(features)
    middle, bottom = split(features - top.astype(F32))
    outgoing = dot(top, selector) + (dot(middle, selector) + dot(bottom, selector))
    for place, ref in enumerate((up_ref, down_ref, right_ref, left_ref)):
        ref[...] = packed(outgoing, place)
    chunk = chunk_waves(positions_ref[...])
    live = live_row(count_ref, positions_ref.shape[1])
    both = jnp.concatenate([cotangent_ref[...] * live, features * live], axis=0)
    high, low = split(both)
    stacked = jnp.concatenate([high, low], axis=0)
    for number in range(CHUNKS):
        wave_high, wave_low = split(chunk(number))
        part = dot(wave_high, stacked, ((1,), (1,)))
        part = part[:, :128] + part[:, 128:] + dot(wave_low, high, ((1,), (1,)))
        weight = table_ref[number * HALF_ROWS : (number + 1) * HALF_ROWS, :]
        base = number * 2 * HALF_ROWS
        parts_ref[base : base + HALF_ROWS, :] = part[:HALF_ROWS] * weight
        parts_ref[base + HALF_ROWS : base + 2 * HALF_ROWS, :] = part[HALF_ROWS:] * weight
    half = keep_ref.shape[0]
    first = lax.axis_index("core") == 0
    lower, upper = parts_ref[:half, :], parts_ref[half:, :]
    keep_ref[...] = jnp.where(first, lower, upper)
    give_ref[...] = jnp.where(first, upper, lower)


def edge_kernel(
    count_ref,
    features_ref,
    up_ref,
    down_ref,
    right_ref,
    left_ref,
    cotangent_ref,
    length_ref,
    neighbor_ref,
    short_ref,
    radial_ref,
    keep_ref,
    taken_ref,
    own_ref,
    ghost_up_ref,
    ghost_down_ref,
    ghost_right_ref,
    ghost_left_ref,
    payload_ref,
    basis_ref,
    selector_ref,
    gathered_ref,
    weight_ref,
    grads_ref,
    upstream_ref,
    ratio_ref,
    envelope_ref,
    *,
    factor,
):
    channels, atoms = features_ref.shape
    slots = length_ref.shape[0]
    columns = atoms + 128
    group = 4
    wide = group * atoms
    waves = keep_ref.shape[0]
    payload_ref[:waves, :] = keep_ref[...] + taken_ref[...]
    extended = jnp.concatenate(
        [features_ref[...], unpacked((up_ref, down_ref, right_ref, left_ref))], axis=1
    )
    projected = jnp.concatenate(split(dot_full(short_ref[...], extended)), axis=0)
    live = live_row(count_ref, atoms)

    lengths = length_ref[...]
    targets = neighbor_ref[...]
    reach = jnp.where(jnp.logical_or(targets >= atoms, targets < count_ref[0]), live, 0.0)
    ratio = lengths * (1.0 / CUTOFF)
    envelope = 1.0 - ratio * ratio
    envelope_ref[...] = math.sqrt(2.0 / CUTOFF) * envelope * envelope / lengths * reach
    ratio_ref[...] = 0.5 * ratio
    order = lax.broadcasted_iota(jnp.int32, (8, atoms), 0).astype(F32) + 1.0

    radial_high, radial_low = split(radial_ref[...])
    radial_wide = jnp.concatenate([radial_high, radial_high, radial_low], axis=0)
    column = lax.broadcasted_iota(jnp.int32, (columns, 128), 0).astype(jnp.int16)
    one, zero = jnp.ones((), BF16), jnp.zeros((), BF16)

    def side_by_side(pieces):
        return jnp.concatenate(pieces, axis=1)

    def basis_of(turn):
        base = turn * group * 8
        return split(
            side_by_side(
                [basis_ref[pl.ds(pl.multiple_of(base + 8 * i, 8), 8), :] for i in range(group)]
            )
        )

    def forward(turn, total):
        tiles = []
        for i in range(group):
            picks = neighbor_ref[pl.ds(turn * group + i, 1), :]
            for lane in range(0, atoms, 128):
                pick = jnp.broadcast_to(picks[:, lane : lane + 128], (16, 128)).astype(jnp.int16)
                pick = jnp.concatenate([pick] * (columns // 16), axis=0)
                tiles.append(jnp.where(column == pick, one, zero))
        selector = side_by_side(tiles)
        selector_ref[turn] = selector
        found = dot(projected, selector)
        gathered = found[:channels] + found[channels:]
        for i in range(group):
            slot = turn * group + i
            basis_ref[pl.ds(pl.multiple_of(slot * 8, 8), 8), :] = (
                sin_turns(order * ratio_ref[pl.ds(slot, 1), :]) * envelope_ref[pl.ds(slot, 1), :]
            )
        basis_high, basis_low = basis_of(turn)
        weight = dot(
            radial_wide, jnp.concatenate([basis_high, basis_low, basis_high], axis=0), ((0,), (0,))
        )
        gathered_ref[turn] = gathered
        weight_ref[turn] = weight
        product = weight * gathered
        for i in range(group):
            total = total + product[:, i * atoms : (i + 1) * atoms]
        return total

    turns = slots // group
    short_sum = lax.fori_loop(
        0, turns, forward, jnp.zeros((channels, atoms), F32), unroll=8
    )
    gate = jax.nn.sigmoid(short_sum)
    upstream = cotangent_ref[...] * gate * (1.0 + short_sum * (1.0 - gate)) * live

    grads_ref[...] = jnp.zeros(grads_ref.shape, F32)
    upstream_ref[...] = upstream

    def backward(turn, radial):
        pieces = []
        pulls = []
        for i in range(group):
            lanes = pl.ds(i * atoms, atoms)
            pieces.append(jnp.concatenate(split(weight_ref[turn, :, lanes] * upstream_ref[...]), axis=0))
            pulls.append(jnp.concatenate(split(gathered_ref[turn, :, lanes] * upstream_ref[...]), axis=0))
        grads_ref[...] += dot(selector_ref[turn], side_by_side(pieces), ((1,), (1,)))
        pair = jnp.concatenate(basis_of(turn), axis=0)
        return radial + dot(pair, side_by_side(pulls), ((1,), (1,)))

    radial = lax.fori_loop(
        0, turns, backward, jnp.zeros((16, 2 * channels), F32), unroll=8
    ).T
    grads = grads_ref[...].T
    grads = grads[:channels] + grads[channels:]
    radial = radial[:channels] + radial[channels:]
    radial = radial[:, :8] + radial[:, 8:]
    own_ref[...] = grads[:, :atoms]
    for place, ref in enumerate((ghost_up_ref, ghost_down_ref, ghost_right_ref, ghost_left_ref)):
        ref[...] = packed(grads[:, atoms:], place)
    short_part = dot_full(grads, extended, ((1,), (1,))) * factor
    payload_ref[waves:, :] = jnp.concatenate(
        [short_part, radial * factor, jnp.zeros((channels, 128 - channels - 8), F32)], axis=1
    )


def return_kernel(left_ref, right_ref, down_ref, up_ref, own_ref, map_ref, short_ref, out_ref):
    back = unpacked((up_ref, down_ref, right_ref, left_ref))
    selector = send_selector(map_ref[...], own_ref.shape[1])
    high, low = split(back)
    owned = own_ref[...] + (
        dot(high, selector, ((1,), (1,))) + dot(low, selector, ((1,), (1,)))
    )
    out_ref[...] = dot_full(short_ref[...], owned, ((0,), (0,)))


def sum_kernel(pieces_ref, out_ref, *, width):
    rows = pieces_ref.shape[0]
    block = 4 * width
    total = jnp.sum(pieces_ref[...].reshape(rows // block, block, 128), axis=0)
    mine = total[:width]
    for step in range(1, 4):
        mine = mine + total[step * width : (step + 1) * width]
    pattern = jnp.concatenate([mine] * 4, axis=0)
    out_ref[...] = jnp.broadcast_to(pattern[None], (rows // block, block, 128)).reshape(rows, 128)


def table_kernel(positions_ref, high_ref, low_ref):
    chunk = chunk_waves(positions_ref[...])
    for number in range(CHUNKS):
        rows = pl.ds(number * 2 * HALF_ROWS, 2 * HALF_ROWS)
        high_ref[rows, :], low_ref[rows, :] = split(chunk(number))


def half_charge(half_ref, high_ref, low_ref, first):
    waves = CHUNKS * HALF_ROWS
    rows = pl.ds(pl.multiple_of(jnp.where(first, 0, waves), HALF_ROWS), waves)
    block = half_ref[:waves, :]
    turned_high, turned_low = split(block.T[:64])
    block_high, block_low = split(block)
    wave_high = high_ref[rows, :]
    turned = jnp.concatenate([turned_high, turned_low], axis=0)
    field = dot(turned, wave_high)
    field = field[:64] + field[64:] + dot(turned_high, low_ref[rows, :])
    grad = dot(turned, block_high)
    grad = grad[:64] + grad[64:] + dot(turned_high, block_low)
    return field, grad


def mine_kernel(mine_ref, high_ref, low_ref, field_ref, grad_ref, small_ref):
    small_ref[...] = mine_ref[CHUNKS * HALF_ROWS :, :]
    first = lax.axis_index("core") == 0
    field_ref[...], grad_ref[...] = half_charge(mine_ref, high_ref, low_ref, first)


def charge_kernel(
    count_ref,
    other_ref,
    high_ref,
    low_ref,
    field_ref,
    sums_ref,
    mine_ref,
    partial_ref,
    charge_ref,
    grad_ref,
    out_ref,
    short_ref,
    radial_ref,
    *,
    factor,
):
    first = lax.axis_index("core") != 0
    waves = CHUNKS * HALF_ROWS
    small = mine_ref[...] + other_ref[waves:, :]
    channels, atoms = partial_ref.shape
    short_ref[...] = small[:, :channels]
    radial_ref[...] = small.T[channels : channels + 8, :]
    field, grad = half_charge(other_ref, high_ref, low_ref, first)
    field = (field + field_ref[...]) * live_row(count_ref, atoms)
    grad = grad + sums_ref[...]
    grad_ref[...] = grad[:, channels : 2 * channels] * factor
    out_ref[...] = partial_ref[...] + dot_full(charge_ref[...], field, ((0,), (0,)))


def vmem(count):
    return [pl.BlockSpec(memory_space=pltpu.VMEM)] * count


def scalar_first(count):
    return [pl.BlockSpec(memory_space=pltpu.SMEM)] + vmem(count)


def work(micros):
    return pl.CostEstimate(
        flops=int(micros * 1e9), transcendentals=0, bytes_accessed=int(micros * 3e6)
    )


def shape(*dims):
    return jax.ShapeDtypeStruct(dims, F32)


def near(*dims):
    return pltpu.VMEM(dims, F32)


def shifted(value, axis, step):
    size = lax.axis_size(axis)
    return lax.ppermute(value, axis, [(i, (i + step) % size) for i in range(size)])


def close(value):
    return pltpu.with_memory_space_constraint(value, pltpu.VMEM)


def swapped(value):
    return lax.ppermute(value, "core", [(0, 1), (1, 0)])


def exchange(value, axes):
    return lax.all_to_all(value, axes, 0, 0, tiled=True)


def on_device(
    features,
    cotangent,
    positions,
    edge_length,
    neighbors,
    send_map,
    atom_count,
    short_weight,
    charge_weight,
    radial_weight,
):
    channels, atoms = features.shape
    slots = neighbors.shape[0]
    devices = lax.axis_size(ALL)
    chips = lax.axis_size(CHIPS)
    factor = 1.0 / math.sqrt(atoms * devices)
    half = CHUNKS * HALF_ROWS
    rows = half + channels
    width = rows // chips * 128

    message = near(channels // 4, 128)
    keep, give, *outgoing = pl.pallas_call(
        wave_kernel,
        out_shape=(near(half, 128), near(half, 128)) + (message,) * 4,
        in_specs=scalar_first(5),
        out_specs=tuple(vmem(6)),
        scratch_shapes=[pltpu.VMEM((2 * half, 128), F32)],
        cost_estimate=work(4.0),
    )(atom_count, positions, cotangent, features, jnp.asarray(weight_table(factor)), send_map)
    up = shifted(outgoing[0], SLAB, 1)
    down = shifted(outgoing[1], SLAB, -1)
    right = shifted(outgoing[2], "brick", 1)
    left = shifted(outgoing[3], "brick", -1)
    taken = swapped(give)

    up, down, right, left = (close(x) for x in (up, down, right, left))
    taken = close(taken)
    table = jax.ShapeDtypeStruct((2 * half, atoms), BF16)
    high, low = pl.pallas_call(
        table_kernel,
        out_shape=(table, table),
        in_specs=vmem(1),
        out_specs=tuple(vmem(2)),
        cost_estimate=work(2.0),
    )(positions)
    keep, high, low = lax.optimization_barrier((keep, high, low))
    keep = close(keep)
    own, *ghost, payload = pl.pallas_call(
        functools.partial(edge_kernel, factor=factor),
        out_shape=(near(channels, atoms),) + (message,) * 4 + (near(rows, 128),),
        in_specs=scalar_first(12),
        out_specs=tuple(vmem(6)),
        scratch_shapes=[
            pltpu.VMEM((slots * 8, atoms), F32),
            pltpu.VMEM((slots // 4, atoms + 128, 4 * atoms), BF16),
            pltpu.VMEM((slots // 4, channels, 4 * atoms), F32),
            pltpu.VMEM((slots // 4, channels, 4 * atoms), F32),
            pltpu.VMEM((atoms + 128, 2 * channels), F32),
            pltpu.VMEM((channels, atoms), F32),
            pltpu.VMEM((slots, atoms), F32),
            pltpu.VMEM((slots, atoms), F32),
        ],
        cost_estimate=work(10.0),
    )(
        atom_count,
        features,
        up,
        down,
        right,
        left,
        cotangent,
        edge_length,
        neighbors,
        short_weight,
        radial_weight.T,
        keep,
        taken,
    )
    pieces = exchange(payload.reshape(chips, 1, width), CHIPS)
    back_right = shifted(ghost[3], "brick", 1)
    back_left = shifted(ghost[2], "brick", -1)
    back_up = shifted(ghost[1], SLAB, 1)
    back_down = shifted(ghost[0], SLAB, -1)
    summed = pl.pallas_call(
        functools.partial(sum_kernel, width=rows // chips),
        out_shape=near(rows, 128),
        in_specs=vmem(1),
        out_specs=vmem(1)[0],
        cost_estimate=work(0.5),
    )(close(pieces.reshape(rows, 128)))
    mine = exchange(summed.reshape(chips, 1, width), CHIPS).reshape(rows, 128)
    back_right, back_left, back_up, back_down = (
        close(x) for x in (back_right, back_left, back_up, back_down)
    )
    partial = pl.pallas_call(
        return_kernel,
        out_shape=near(channels, atoms),
        in_specs=vmem(7),
        out_specs=vmem(1)[0],
        cost_estimate=work(2.0),
    )(back_right, back_left, back_up, back_down, close(own), send_map, short_weight)
    mine, partial = lax.optimization_barrier((mine, partial))
    high, low = close(high), close(low)
    other = close(swapped(mine))
    field, sums, small = pl.pallas_call(
        mine_kernel,
        out_shape=(near(channels, atoms), near(channels, 128), near(channels, 128)),
        in_specs=vmem(3),
        out_specs=tuple(vmem(3)),
        cost_estimate=work(2.0),
    )(close(mine), high, low)
    charge_grad, feature_grad, short_grad, radial_grad = pl.pallas_call(
        functools.partial(charge_kernel, factor=factor),
        out_shape=(
            shape(channels, channels),
            shape(channels, atoms),
            shape(channels, channels),
            shape(radial_weight.shape[1], channels),
        ),
        in_specs=scalar_first(8),
        out_specs=tuple(vmem(4)),
        cost_estimate=work(3.0),
    )(
        atom_count,
        other,
        high,
        low,
        close(field),
        close(sums),
        close(small),
        close(partial),
        charge_weight,
    )
    return feature_grad, short_grad, charge_grad, radial_grad.T


def solution(mesh):
    slabs, bricks = mesh.devices.shape
    fine = Mesh(mesh.devices.reshape(slabs // 2, 2, bricks), ALL)
    split_all = P(None, ALL)
    placed = (split_all,) * 6 + (P(ALL), P(), P(), P())
    return jax.shard_map(
        on_device,
        mesh=fine,
        in_specs=placed,
        out_specs=(split_all, P(), P(), P()),
        check_vma=False,
    )
```

```python
import functools
import math

import jax
import jax.numpy as jnp
import numpy as np
from jax import lax
from jax.experimental import pallas as pl
from jax.experimental.pallas import tpu as pltpu
from jax.sharding import Mesh
from jax.sharding import PartitionSpec as P

KX = 8
KY = 16
KZ = 8
CUTOFF = 6.0
HALF_ROWS = 64
CHUNKS = 11
F32 = jnp.float32
BF16 = jnp.bfloat16
SLAB = ("chip", "core")
CHIPS = ("chip", "brick")
ALL = ("chip", "core", "brick")


def slot_modes(chunk, i, j):
    if chunk < 8:
        return (chunk - 4, j - 8, i - 4)
    if chunk == 8:
        return (4, j - 8, i - 3)
    if chunk == 9:
        return (i - 3, j - 8, 4)
    return (i - 4, 0, j - 4)


def weight_table(scale):
    where = {}
    for chunk in range(CHUNKS):
        for i in range(8):
            for j in range(8):
                where.setdefault(slot_modes(chunk, i, j), (chunk, i * 8 + j))
    table = np.zeros((CHUNKS, HALF_ROWS), np.float64)
    for k in range(KX * KY * KZ):
        n = (k // (KY * KZ) - KX // 2, k // KZ % KY - KY // 2, k % KZ - KZ // 2)
        squared = float(n[0] ** 2 + n[1] ** 2 + n[2] ** 2)
        if squared == 0.0:
            continue
        slot = where.get(n)
        if slot is None or n[1] > 0:
            slot = where[(-n[0], -n[1], -n[2])]
        table[slot] += math.exp(-squared / 16.0) / squared
    wide = np.ones((CHUNKS * HALF_ROWS, 128), np.float32)
    wide[:, :64] = (table.reshape(-1, 1) * scale).astype(np.float32)
    return wide


def split(value):
    high = value.astype(BF16)
    return high, (value - high.astype(F32)).astype(BF16)


def dot(left, right, contract=((1,), (0,))):
    return lax.dot_general(left, right, (contract, ((), ())), preferred_element_type=F32)


def dot_full(left, right, contract=((1,), (0,))):
    left_high, left_low = split(left)
    right_high, right_low = split(right)
    return dot(left_high, right_high, contract) + (
        dot(left_high, right_low, contract) + dot(left_low, right_high, contract)
    )


def sin_turns(turns):
    turns = turns - jnp.floor(turns + 0.5)
    folded = jnp.where(turns > 0.25, 0.5 - turns, jnp.where(turns < -0.25, -0.5 - turns, turns))
    angle = folded * (2.0 * math.pi)
    square = angle * angle
    poly = -1.0 / 39916800.0
    for divisor in (362880.0, -5040.0, 120.0, -6.0):
        poly = poly * square + 1.0 / divisor
    return angle + angle * square * poly


def wave_factors(turns, first):
    order = lax.broadcasted_iota(jnp.int32, (8, turns.shape[1]), 0) + first
    phase = order.astype(F32) * turns
    phase = phase - jnp.floor(phase + 0.5)
    return sin_turns(phase + 0.25), sin_turns(phase)


def complex_product(left, right):
    return (
        left[0] * right[0] - left[1] * right[1],
        left[0] * right[1] + left[1] * right[0],
    )


def chunk_waves(positions):
    one = wave_factors(positions[0:1], -4)
    one_up = wave_factors(positions[0:1], -3)
    two = wave_factors(positions[1:2], -8)
    three = wave_factors(positions[2:3], -4)
    three_up = wave_factors(positions[2:3], -3)

    def row(pair, index):
        return pair[0][index : index + 1], pair[1][index : index + 1]

    def chunk(number):
        if number < 8:
            outer, inner = complex_product(row(one, number), three), two
        elif number == 8:
            outer, inner = complex_product(row(one_up, 7), three_up), two
        elif number == 9:
            outer, inner = complex_product(row(three_up, 7), one_up), two
        else:
            outer, inner = one, three
        cos_part, sin_part = complex_product(
            (outer[0][:, None, :], outer[1][:, None, :]),
            (inner[0][None, :, :], inner[1][None, :, :]),
        )
        atoms = positions.shape[1]
        return jnp.concatenate(
            [cos_part.reshape(HALF_ROWS, atoms), sin_part.reshape(HALF_ROWS, atoms)], axis=0
        )

    return chunk


def live_row(count_ref, atoms):
    index = lax.broadcasted_iota(jnp.int32, (1, atoms), 1)
    return (index < count_ref[0]).astype(F32)


def send_selector(send_map, atoms, transposed=False):
    size = send_map.shape[1]
    spread = (
        lax.broadcasted_iota(jnp.int32, (size, 128), 1) % size
        == lax.broadcasted_iota(jnp.int32, (size, 128), 0)
    ).astype(F32)
    tiled = dot_full(send_map.astype(F32), spread)
    place = lax.broadcasted_iota(jnp.int32, (1, 128), 1) // size
    wanted = jnp.zeros((1, 128), F32)
    for slot, group in enumerate((2, 3, 0, 1, 1, 3, 0, 2)):
        wanted = jnp.where(place == slot, tiled[group : group + 1], wanted)
    atom = lax.broadcasted_iota(jnp.int32, (atoms, 128), 0).astype(F32)
    return (atom == jnp.round(wanted)).astype(F32).astype(BF16)


def packed(value, place):
    lanes = slice(32 * place, 32 * place + 32)
    return jnp.concatenate([value[16 * q : 16 * q + 16, lanes] for q in range(4)], axis=1)


def unpacked(refs):
    values = [ref[...] for ref in refs]
    return jnp.concatenate(
        [
            jnp.concatenate([value[:, 32 * q : 32 * q + 32] for value in values], axis=1)
            for q in range(4)
        ],
        axis=0,
    )


def wave_kernel(
    count_ref,
    positions_ref,
    cotangent_ref,
    features_ref,
    table_ref,
    map_ref,
    keep_ref,
    give_ref,
    up_ref,
    down_ref,
    right_ref,
    left_ref,
    parts_ref,
):
    features = features_ref[...]
    selector = send_selector(map_ref[...], features.shape[1])
    top, rest = split(features)
    middle, bottom = split(features - top.astype(F32))
    outgoing = dot(top, selector) + (dot(middle, selector) + dot(bottom, selector))
    for place, ref in enumerate((up_ref, down_ref, right_ref, left_ref)):
        ref[...] = packed(outgoing, place)
    chunk = chunk_waves(positions_ref[...])
    live = live_row(count_ref, positions_ref.shape[1])
    both = jnp.concatenate([cotangent_ref[...] * live, features * live], axis=0)
    high, low = split(both)
    stacked = jnp.concatenate([high, low], axis=0)
    for number in range(CHUNKS):
        wave_high, wave_low = split(chunk(number))
        part = dot(wave_high, stacked, ((1,), (1,)))
        part = part[:, :128] + part[:, 128:] + dot(wave_low, high, ((1,), (1,)))
        weight = table_ref[number * HALF_ROWS : (number + 1) * HALF_ROWS, :]
        base = number * 2 * HALF_ROWS
        parts_ref[base : base + HALF_ROWS, :] = part[:HALF_ROWS] * weight
        parts_ref[base + HALF_ROWS : base + 2 * HALF_ROWS, :] = part[HALF_ROWS:] * weight
    half = keep_ref.shape[0]
    first = lax.axis_index("core") == 0
    lower, upper = parts_ref[:half, :], parts_ref[half:, :]
    keep_ref[...] = jnp.where(first, lower, upper)
    give_ref[...] = jnp.where(first, upper, lower)


def edge_kernel(
    count_ref,
    features_ref,
    up_ref,
    down_ref,
    right_ref,
    left_ref,
    cotangent_ref,
    length_ref,
    neighbor_ref,
    short_ref,
    radial_ref,
    keep_ref,
    taken_ref,
    own_ref,
    ghost_up_ref,
    ghost_down_ref,
    ghost_right_ref,
    ghost_left_ref,
    payload_ref,
    basis_ref,
    selector_ref,
    gathered_ref,
    weight_ref,
    grads_ref,
    upstream_ref,
    ratio_ref,
    envelope_ref,
    *,
    factor,
):
    channels, atoms = features_ref.shape
    slots = length_ref.shape[0]
    columns = atoms + 128
    group = 8
    wide = group * atoms
    waves = keep_ref.shape[0]
    payload_ref[:waves, :] = keep_ref[...] + taken_ref[...]
    extended = jnp.concatenate(
        [features_ref[...], unpacked((up_ref, down_ref, right_ref, left_ref))], axis=1
    )
    projected = jnp.concatenate(split(dot_full(short_ref[...], extended)), axis=0)
    live = live_row(count_ref, atoms)

    lengths = length_ref[...]
    targets = neighbor_ref[...]
    reach = jnp.where(jnp.logical_or(targets >= atoms, targets < count_ref[0]), live, 0.0)
    ratio = lengths * (1.0 / CUTOFF)
    envelope = 1.0 - ratio * ratio
    envelope_ref[...] = math.sqrt(2.0 / CUTOFF) * envelope * envelope / lengths * reach
    ratio_ref[...] = 0.5 * ratio
    order = lax.broadcasted_iota(jnp.int32, (8, atoms), 0).astype(F32) + 1.0

    radial_high, radial_low = split(radial_ref[...])
    radial_wide = jnp.concatenate([radial_high, radial_high, radial_low], axis=0)
    column = lax.broadcasted_iota(jnp.int32, (columns, 128), 0).astype(jnp.int16)
    one, zero = jnp.ones((), BF16), jnp.zeros((), BF16)

    def side_by_side(pieces):
        return jnp.concatenate(pieces, axis=1)

    def basis_of(turn):
        base = turn * group * 8
        return split(
            side_by_side(
                [basis_ref[pl.ds(pl.multiple_of(base + 8 * i, 8), 8), :] for i in range(group)]
            )
        )

    def forward(turn, total):
        tiles = []
        for i in range(group):
            picks = neighbor_ref[pl.ds(turn * group + i, 1), :]
            for lane in range(0, atoms, 128):
                pick = jnp.broadcast_to(picks[:, lane : lane + 128], (16, 128)).astype(jnp.int16)
                pick = jnp.concatenate([pick] * (columns // 16), axis=0)
                tiles.append(jnp.where(column == pick, one, zero))
        selector = side_by_side(tiles)
        selector_ref[turn] = selector
        found = dot(projected, selector)
        gathered = found[:channels] + found[channels:]
        for i in range(group):
            slot = turn * group + i
            basis_ref[pl.ds(pl.multiple_of(slot * 8, 8), 8), :] = (
                sin_turns(order * ratio_ref[pl.ds(slot, 1), :]) * envelope_ref[pl.ds(slot, 1), :]
            )
        basis_high, basis_low = basis_of(turn)
        weight = dot(
            radial_wide, jnp.concatenate([basis_high, basis_low, basis_high], axis=0), ((0,), (0,))
        )
        gathered_ref[turn] = gathered
        weight_ref[turn] = weight
        product = weight * gathered
        for i in range(group):
            total = total + product[:, i * atoms : (i + 1) * atoms]
        return total

    turns = slots // group
    short_sum = lax.fori_loop(
        0, turns, forward, jnp.zeros((channels, atoms), F32), unroll=4
    )
    gate = jax.nn.sigmoid(short_sum)
    upstream = cotangent_ref[...] * gate * (1.0 + short_sum * (1.0 - gate)) * live

    grads_ref[...] = jnp.zeros(grads_ref.shape, F32)
    upstream_ref[...] = upstream

    def backward(turn, radial):
        pieces = []
        pulls = []
        for i in range(group):
            lanes = pl.ds(i * atoms, atoms)
            pieces.append(jnp.concatenate(split(weight_ref[turn, :, lanes] * upstream_ref[...]), axis=0))
            pulls.append(jnp.concatenate(split(gathered_ref[turn, :, lanes] * upstream_ref[...]), axis=0))
        grads_ref[...] += dot(selector_ref[turn], side_by_side(pieces), ((1,), (1,)))
        pair = jnp.concatenate(basis_of(turn), axis=0)
        return radial + dot(pair, side_by_side(pulls), ((1,), (1,)))

    radial = lax.fori_loop(
        0, turns, backward, jnp.zeros((16, 2 * channels), F32), unroll=4
    ).T
    grads = grads_ref[...].T
    grads = grads[:channels] + grads[channels:]
    radial = radial[:channels] + radial[channels:]
    radial = radial[:, :8] + radial[:, 8:]
    own_ref[...] = grads[:, :atoms]
    for place, ref in enumerate((ghost_up_ref, ghost_down_ref, ghost_right_ref, ghost_left_ref)):
        ref[...] = packed(grads[:, atoms:], place)
    short_part = dot_full(grads, extended, ((1,), (1,))) * factor
    payload_ref[waves:, :] = jnp.concatenate(
        [short_part, radial * factor, jnp.zeros((channels, 128 - channels - 8), F32)], axis=1
    )


def return_kernel(left_ref, right_ref, down_ref, up_ref, own_ref, map_ref, short_ref, out_ref):
    back = unpacked((up_ref, down_ref, right_ref, left_ref))
    selector = send_selector(map_ref[...], own_ref.shape[1])
    high, low = split(back)
    owned = own_ref[...] + (
        dot(high, selector, ((1,), (1,))) + dot(low, selector, ((1,), (1,)))
    )
    out_ref[...] = dot_full(short_ref[...], owned, ((0,), (0,)))


def sum_kernel(pieces_ref, out_ref, *, width):
    rows = pieces_ref.shape[0]
    block = 4 * width
    total = jnp.sum(pieces_ref[...].reshape(rows // block, block, 128), axis=0)
    mine = total[:width]
    for step in range(1, 4):
        mine = mine + total[step * width : (step + 1) * width]
    pattern = jnp.concatenate([mine] * 4, axis=0)
    out_ref[...] = jnp.broadcast_to(pattern[None], (rows // block, block, 128)).reshape(rows, 128)


def table_kernel(positions_ref, high_ref, low_ref):
    chunk = chunk_waves(positions_ref[...])
    for number in range(CHUNKS):
        rows = pl.ds(number * 2 * HALF_ROWS, 2 * HALF_ROWS)
        high_ref[rows, :], low_ref[rows, :] = split(chunk(number))


def half_charge(half_ref, high_ref, low_ref, first):
    waves = CHUNKS * HALF_ROWS
    rows = pl.ds(pl.multiple_of(jnp.where(first, 0, waves), HALF_ROWS), waves)
    block = half_ref[:waves, :]
    turned_high, turned_low = split(block.T[:64])
    block_high, block_low = split(block)
    wave_high = high_ref[rows, :]
    turned = jnp.concatenate([turned_high, turned_low], axis=0)
    field = dot(turned, wave_high)
    field = field[:64] + field[64:] + dot(turned_high, low_ref[rows, :])
    grad = dot(turned, block_high)
    grad = grad[:64] + grad[64:] + dot(turned_high, block_low)
    return field, grad


def mine_kernel(mine_ref, high_ref, low_ref, field_ref, grad_ref, small_ref):
    small_ref[...] = mine_ref[CHUNKS * HALF_ROWS :, :]
    first = lax.axis_index("core") == 0
    field_ref[...], grad_ref[...] = half_charge(mine_ref, high_ref, low_ref, first)


def charge_kernel(
    count_ref,
    other_ref,
    high_ref,
    low_ref,
    field_ref,
    sums_ref,
    mine_ref,
    partial_ref,
    charge_ref,
    grad_ref,
    out_ref,
    short_ref,
    radial_ref,
    *,
    factor,
):
    first = lax.axis_index("core") != 0
    waves = CHUNKS * HALF_ROWS
    small = mine_ref[...] + other_ref[waves:, :]
    channels, atoms = partial_ref.shape
    short_ref[...] = small[:, :channels]
    radial_ref[...] = small.T[channels : channels + 8, :]
    field, grad = half_charge(other_ref, high_ref, low_ref, first)
    field = (field + field_ref[...]) * live_row(count_ref, atoms)
    grad = grad + sums_ref[...]
    grad_ref[...] = grad[:, channels : 2 * channels] * factor
    out_ref[...] = partial_ref[...] + dot_full(charge_ref[...], field, ((0,), (0,)))


def vmem(count):
    return [pl.BlockSpec(memory_space=pltpu.VMEM)] * count


def scalar_first(count):
    return [pl.BlockSpec(memory_space=pltpu.SMEM)] + vmem(count)


def work(micros):
    return pl.CostEstimate(
        flops=int(micros * 1e9), transcendentals=0, bytes_accessed=int(micros * 3e6)
    )


def shape(*dims):
    return jax.ShapeDtypeStruct(dims, F32)


def near(*dims):
    return pltpu.VMEM(dims, F32)


def shifted(value, axis, step):
    size = lax.axis_size(axis)
    return lax.ppermute(value, axis, [(i, (i + step) % size) for i in range(size)])


def close(value):
    return pltpu.with_memory_space_constraint(value, pltpu.VMEM)


def swapped(value):
    return lax.ppermute(value, "core", [(0, 1), (1, 0)])


def exchange(value, axes):
    return lax.all_to_all(value, axes, 0, 0, tiled=True)


def on_device(
    features,
    cotangent,
    positions,
    edge_length,
    neighbors,
    send_map,
    atom_count,
    short_weight,
    charge_weight,
    radial_weight,
):
    channels, atoms = features.shape
    slots = neighbors.shape[0]
    devices = lax.axis_size(ALL)
    chips = lax.axis_size(CHIPS)
    factor = 1.0 / math.sqrt(atoms * devices)
    half = CHUNKS * HALF_ROWS
    rows = half + channels
    width = rows // chips * 128

    message = near(channels // 4, 128)
    keep, give, *outgoing = pl.pallas_call(
        wave_kernel,
        out_shape=(near(half, 128), near(half, 128)) + (message,) * 4,
        in_specs=scalar_first(5),
        out_specs=tuple(vmem(6)),
        scratch_shapes=[pltpu.VMEM((2 * half, 128), F32)],
        cost_estimate=work(4.0),
    )(atom_count, positions, cotangent, features, jnp.asarray(weight_table(factor)), send_map)
    up = shifted(outgoing[0], SLAB, 1)
    down = shifted(outgoing[1], SLAB, -1)
    right = shifted(outgoing[2], "brick", 1)
    left = shifted(outgoing[3], "brick", -1)
    taken = swapped(give)

    up, down, right, left = (close(x) for x in (up, down, right, left))
    taken = close(taken)
    table = jax.ShapeDtypeStruct((2 * half, atoms), BF16)
    high, low = pl.pallas_call(
        table_kernel,
        out_shape=(table, table),
        in_specs=vmem(1),
        out_specs=tuple(vmem(2)),
        cost_estimate=work(2.0),
    )(positions)
    keep, high, low = lax.optimization_barrier((keep, high, low))
    keep = close(keep)
    own, *ghost, payload = pl.pallas_call(
        functools.partial(edge_kernel, factor=factor),
        out_shape=(near(channels, atoms),) + (message,) * 4 + (near(rows, 128),),
        in_specs=scalar_first(12),
        out_specs=tuple(vmem(6)),
        scratch_shapes=[
            pltpu.VMEM((slots * 8, atoms), F32),
            pltpu.VMEM((slots // 8, atoms + 128, 8 * atoms), BF16),
            pltpu.VMEM((slots // 8, channels, 8 * atoms), F32),
            pltpu.VMEM((slots // 8, channels, 8 * atoms), F32),
            pltpu.VMEM((atoms + 128, 2 * channels), F32),
            pltpu.VMEM((channels, atoms), F32),
            pltpu.VMEM((slots, atoms), F32),
            pltpu.VMEM((slots, atoms), F32),
        ],
        cost_estimate=work(10.0),
    )(
        atom_count,
        features,
        up,
        down,
        right,
        left,
        cotangent,
        edge_length,
        neighbors,
        short_weight,
        radial_weight.T,
        keep,
        taken,
    )
    pieces = exchange(payload.reshape(chips, 1, width), CHIPS)
    back_right = shifted(ghost[3], "brick", 1)
    back_left = shifted(ghost[2], "brick", -1)
    back_up = shifted(ghost[1], SLAB, 1)
    back_down = shifted(ghost[0], SLAB, -1)
    summed = pl.pallas_call(
        functools.partial(sum_kernel, width=rows // chips),
        out_shape=near(rows, 128),
        in_specs=vmem(1),
        out_specs=vmem(1)[0],
        cost_estimate=work(0.5),
    )(close(pieces.reshape(rows, 128)))
    mine = exchange(summed.reshape(chips, 1, width), CHIPS).reshape(rows, 128)
    back_right, back_left, back_up, back_down = (
        close(x) for x in (back_right, back_left, back_up, back_down)
    )
    partial = pl.pallas_call(
        return_kernel,
        out_shape=near(channels, atoms),
        in_specs=vmem(7),
        out_specs=vmem(1)[0],
        cost_estimate=work(2.0),
    )(back_right, back_left, back_up, back_down, close(own), send_map, short_weight)
    mine, partial = lax.optimization_barrier((mine, partial))
    high, low = close(high), close(low)
    other = close(swapped(mine))
    field, sums, small = pl.pallas_call(
        mine_kernel,
        out_shape=(near(channels, atoms), near(channels, 128), near(channels, 128)),
        in_specs=vmem(3),
        out_specs=tuple(vmem(3)),
        cost_estimate=work(2.0),
    )(close(mine), high, low)
    charge_grad, feature_grad, short_grad, radial_grad = pl.pallas_call(
        functools.partial(charge_kernel, factor=factor),
        out_shape=(
            shape(channels, channels),
            shape(channels, atoms),
            shape(channels, channels),
            shape(radial_weight.shape[1], channels),
        ),
        in_specs=scalar_first(8),
        out_specs=tuple(vmem(4)),
        cost_estimate=work(3.0),
    )(
        atom_count,
        other,
        high,
        low,
        close(field),
        close(sums),
        close(small),
        close(partial),
        charge_weight,
    )
    return feature_grad, short_grad, charge_grad, radial_grad.T


def solution(mesh):
    slabs, bricks = mesh.devices.shape
    fine = Mesh(mesh.devices.reshape(slabs // 2, 2, bricks), ALL)
    split_all = P(None, ALL)
    placed = (split_all,) * 6 + (P(ALL), P(), P(), P())
    return jax.shard_map(
        on_device,
        mesh=fine,
        in_specs=placed,
        out_specs=(split_all, P(), P(), P()),
        check_vma=False,
    )
```
